32 devices in a mesh: row: 4 (over y, core), col: 8 (over z, x).
Axes of the slice: x: 2, y: 2, z: 4, core: 2. Of those that a mesh axis runs over, the one named last changes fastest.
Arguments:
- contribution: float32 [8, 4, 4, 8, 128, 128], P(None, 'row', None, 'col'), may hold values from -6 to 6
- parent_tiles: float32 [16, 4, 8, 8, 128, 128], P(None, 'row', None, 'col'), may hold values from -6 to 6
- row_basis: float32 [8, 4, 64, 128], P(None, 'row'), may hold values from -2.4 to 2.4
- pivot_basis: float32 [8, 4, 64, 2048], P(None, 'row', None, 'col'), may hold values from -0.125 to 0.125
- tile_ranks: int32 [32], replicated, may hold values from 16 to 64, as said below
- block_map: int32 [32], replicated, may hold values from 0 to 63, as said below
- panel_start: int32 [1], replicated, may hold values from 0 to 31
- pivot_inverse: float32 [512, 512], replicated
Outputs:
- updated_parent: float32 [16, 4, 8, 8, 128, 128], P(None, 'row', None, 'col')
The draws below stay inside these ranges and needn't reach their ends.
Inputs may be any that keep to these rules, and one draw needn't show every extreme that they name: `tile_ranks`: multiples of 16; both 16 and 64 occur. `block_map`: child tile row u * 8 + l, for 0 <= l < 8, maps to parent tile row 2 * 8 * u + h_u + l with 0 <= h_u < 8; the 4 values h_u are distinct modulo 4.
All inputs are finite; a program needn't handle non-finite values.
Results may differ from the reference program's by a relative error of at most 0.0003.
Values sent between devices are 32-bit elements; how exact they have to be, the bound alone decides.
A program may use at most 128 MiB of HBM per device.

```python
import jax
import jax.numpy as jnp
from jax import lax

B = 128
P_SIZE = 2048
RMAX = 64
PANEL_T = 4
CT_COL = 4
GRID_R = 4
GRID_C = 8
NTC = 32
CT_ROW = 8
PT_ROW = 16
PT_COL = 8
PW = 512


def draw_block_map(key, part):
    key_perm, key_coin = jax.random.split(jax.random.fold_in(key, 11))
    residues = jax.random.permutation(key_perm, GRID_R)[:CT_COL]
    coins = jax.random.randint(key_coin, (CT_COL,), 0, GRID_C // GRID_R)
    shifts = residues + GRID_R * coins
    blocks = jnp.arange(CT_COL)[:, None]
    within = jnp.arange(GRID_C)[None, :]
    return (2 * GRID_C * blocks + shifts[:, None] + within).reshape(-1).astype(jnp.int32)


def draw_tile_ranks(key, part):
    key_rank, key_place = jax.random.split(jax.random.fold_in(key, 23))
    levels = 16 * jax.random.randint(key_rank, (NTC,), 1, RMAX // 16 + 1)
    order = jax.random.permutation(key_place, NTC)
    levels = levels.at[order[0]].set(RMAX).at[order[1]].set(16)
    return levels.astype(jnp.int32)


def draw_pivot_inverse(key, part):
    key_noise = jax.random.fold_in(key, 37)
    noise = jnp.clip(jax.random.normal(key_noise, (PW, PW), jnp.float32), -4.0, 4.0)
    matrix = jnp.eye(PW, dtype=jnp.float32) + 0.5 * noise / jnp.sqrt(jnp.float32(PW))
    return (matrix / (2.0 * jnp.sqrt(jnp.float32(PW)))).astype(jnp.float32)


def shard_levels(rng, dims, cuts, smallest, top_value):
    gain, own = 1.0, jax.random.fold_in(rng, 6)
    for axis_at, blocks in cuts:
        draws = jnp.exp(jax.random.uniform(jax.random.fold_in(own, axis_at), (blocks,), jnp.float32, smallest / len(cuts), top_value / len(cuts)))
        gain = gain * jnp.repeat(draws, dims[axis_at] // blocks).reshape([-1 if axis == axis_at else 1 for axis in range(len(dims))])
    return gain


def normal_values(stream_key, shape, width, bound, cuts=(), held_as=jnp.bfloat16):
    loudness = shard_levels(stream_key, shape, cuts, -0.22, 0.18) if cuts else 1.0
    array = jax.random.normal(stream_key, shape, jnp.float32) * width * loudness
    return jnp.minimum(jnp.maximum(array, -bound), bound).astype(held_as)


def setup_inputs(seed: int = 0) -> dict:
    splits = jax.random.split(jax.random.key(seed), 9)
    return {
        "contribution": normal_values(splits[0], (CT_ROW, GRID_R, CT_COL, GRID_C, B, B), 1.0, 6.0, ((1, 4), (3, 8)), jnp.float32),
        "parent_tiles": normal_values(splits[1], (PT_ROW, GRID_R, PT_COL, GRID_C, B, B), 1.0, 6.0, ((1, 4), (3, 8)), jnp.float32),
        "row_basis": normal_values(splits[2], (CT_ROW, GRID_R, RMAX, B), 0.4, 2.4, ((1, 4),), jnp.float32),
        "pivot_basis": normal_values(splits[3], (CT_ROW, GRID_R, RMAX, P_SIZE), P_SIZE ** -0.5, 0.125, ((1, 4), (3, 8)), jnp.float32),
        "tile_ranks": draw_tile_ranks(jax.random.fold_in(splits[8], 71), 0),
        "block_map": draw_block_map(jax.random.fold_in(splits[8], 71), 0),
        "panel_start": jax.random.randint(splits[6], (1,), 0, NTC).astype(jnp.int32),
        "pivot_inverse": draw_pivot_inverse(jax.random.fold_in(splits[8], 71), 0),
    }


highest = lax.Precision.HIGHEST


def reference(contribution, parent_tiles, row_basis, pivot_basis, tile_ranks, block_map, panel_start, pivot_inverse):
    child_total = contribution.shape[0] * contribution.shape[1]
    parent_total = parent_tiles.shape[0] * parent_tiles.shape[1]
    tile_size = contribution.shape[4]
    rank_max = row_basis.shape[2]
    kept_cols = (jnp.arange(rank_max, dtype=jnp.int32)[None, :] < tile_ranks[:, None]).astype(jnp.float32)
    bases = row_basis.reshape(child_total, rank_max, tile_size) * kept_cols[:, :, None]
    pivots = pivot_basis.reshape(child_total * rank_max, -1)
    gram = jnp.dot(pivots, pivots.T, precision=highest, preferred_element_type=jnp.float32)
    gram = gram.reshape(child_total, rank_max, child_total, rank_max)
    half_product = jnp.einsum("irx,irju->ixju", bases, gram, precision=highest, preferred_element_type=jnp.float32)
    update = jnp.einsum("ixju,juy->ijxy", half_product, bases, precision=highest, preferred_element_type=jnp.float32)
    tile_index = jnp.arange(child_total, dtype=jnp.int32)
    lower_mask = tile_index[:, None] >= tile_index[None, :]
    blocks = contribution.reshape(child_total, child_total, tile_size, tile_size)
    moved_tiles = jnp.where(lower_mask[:, :, None, None], blocks - update, jnp.float32(0.0))
    parent_grid = parent_tiles.reshape(parent_total, parent_total, tile_size, tile_size)
    assembled = parent_grid.at[block_map[:, None], block_map[None, :]].add(moved_tiles)
    start_col = panel_start[0].astype(jnp.int32)
    panel = lax.dynamic_slice_in_dim(assembled, start_col, PANEL_T, axis=1)
    row_panel = jnp.transpose(panel, (0, 2, 1, 3)).reshape(parent_total, tile_size, PANEL_T * tile_size)
    scaled = jnp.einsum("axp,pq->axq", row_panel, pivot_inverse, precision=highest, preferred_element_type=jnp.float32)
    col_index = jnp.arange(parent_total, dtype=jnp.int32)

    def trailing_row(inputs):
        row_id, current, scaled_row = inputs
        trailing = jnp.einsum("xq,byq->bxy", scaled_row, row_panel, precision=highest, preferred_element_type=jnp.float32)
        window = (row_id >= col_index) & (col_index >= start_col + PANEL_T)
        return jnp.where(window[:, None, None], current - trailing, current)

    result = lax.map(trailing_row, (col_index, assembled, scaled))
    return result.reshape(parent_tiles.shape)
```

```python
import jax
import jax.numpy as jnp
from jax import lax
from jax.experimental import pallas as pl
from jax.experimental.pallas import tpu as pltpu
from jax.sharding import PartitionSpec as P

PANEL_T = 4
f32 = jnp.float32
bf16 = jnp.bfloat16
i32 = jnp.int32
MESH = pl.DeviceIdType.MESH
DMA = pltpu.SemaphoreType.DMA
SMEM = pl.BlockSpec(memory_space=pltpu.SMEM)
VMEM = pl.BlockSpec(memory_space=pltpu.VMEM)
ANY = pl.BlockSpec(memory_space=pl.ANY)


def split(x):
    top = x.astype(bf16)
    return top, (x - top.astype(f32)).astype(bf16)


def dot3(a, b, dims):
    (ah, al), (bh, bl) = a, b
    one = lambda p, q: lax.dot_general(p, q, (dims, ((), ())), preferred_element_type=f32)
    return one(ah, bh) + (one(ah, bl) + one(al, bh))


def ring_place(p, n):
    return jnp.where(p < n // 2, 2 * p, 2 * (n - 1 - p) + 1)


def ring_spot(me, n):
    return jnp.where(me % 2 == 0, me // 2, n - 1 - me // 2)


def greet(targets):
    barrier = pltpu.get_barrier_semaphore()
    for target in targets:
        pl.semaphore_signal(barrier, inc=1, device_id=target, device_id_type=MESH)
    pl.semaphore_wait(barrier, len(targets))


def remote(src, dst, send, recv, to):
    return pltpu.make_async_remote_copy(src, dst, send, recv, device_id=to, device_id_type=MESH)


class Layout:
    def __init__(self, bmap, blocks):
        self.map = bmap
        self.S = blocks
        self.R, self.C = lax.axis_size("row"), lax.axis_size("col")
        self.row, self.col = lax.axis_index("row"), lax.axis_index("col")

    def shift(self, u):
        return self.map[u * self.C] - 2 * self.C * u

    def src_row(self, u, row=None):
        row = self.row if row is None else row
        return lax.rem(row + self.C * self.R - self.shift(u), self.R)

    def src_col(self, s, col=None):
        col = self.col if col is None else col
        return lax.rem(col + self.C - self.shift(s), self.C)

    def first_row(self, u, row=None):
        return lax.div(2 * self.C * u + self.shift(u) + self.src_row(u, row), self.R)

    def first_col(self, s):
        return lax.div(2 * self.C * s + self.shift(s) + self.src_col(s), self.C)


def own_column(start, col, C, bcols):
    k = lax.rem(col - start + C * bcols, C)
    return k, jnp.minimum(lax.div(start + k, C), bcols - 1)


def pick_kernel(bmap, start, parent, rest, sems):
    per, S = rest.shape[:2]
    bcols = parent.shape[2]
    at = Layout(bmap, S)
    _, b = own_column(start[0], at.col, at.C, bcols)
    copies = []
    for u in range(S):
        first = at.first_row(u)
        for q in range(per):
            a = 2 * per * u + q
            a = jnp.where((a >= first) & (a < first + per), a + per, a)
            copies.append(pltpu.make_async_copy(parent.at[a, 0, b, 0], rest.at[q, u], sems.at[q, u]))
            copies[-1].start()
    for copy in copies:
        copy.wait()


def pick_rest(bmap, start, parent, per, S):
    tile = parent.shape[-1]
    return pl.pallas_call(
        pick_kernel,
        in_specs=[SMEM, SMEM, ANY],
        out_specs=VMEM,
        out_shape=jax.ShapeDtypeStruct((per, S, tile, tile), f32),
        scratch_shapes=[DMA((per, S))],
        name="pick_rest",
    )(bmap, start, parent)


def shift_kernel(h, s, per, *refs):
    R, n = lax.axis_size("row"), lax.axis_size("col")
    me, my_col = lax.axis_index("row"), lax.axis_index("col")
    gather = s == 0
    if gather:
        child, piv, bas, moved, all_piv, all_bas, send, recv, own_sem, d_send, d_recv, r_send, r_recv = refs
    else:
        child, moved, send, recv = refs
    blocks = moved.shape[0] // per
    pairs = R // 2
    other = me + 1 - 2 * (me % 2)

    signals = []
    if h:
        signals.append({"col": (my_col + n - h) % n})
    if gather:
        signals += [{"row": (me + k) % R} for k in range(1, R)]
    if signals:
        greet(signals)

    def part(i):
        src = child.at[pl.ds(per * (s + i), per), 0, s, 0]
        dst = moved.at[pl.ds(per * i, per)]
        if h:
            return remote(src, dst, send.at[i], recv.at[i], {"col": (my_col + h) % n})
        return pltpu.make_async_copy(src, dst, recv.at[i])

    if gather:
        T = piv.shape[0]
        cuts = [(piv, all_piv, j * T // 4, T // 4) for j in range(4)]
        cuts += [(bas, all_bas, j * T // 2, T // 2) for j in range(2)]

        def direct(o, j):
            src, dst, a, size = cuts[j]
            to = other if o == 0 else (me // 2 + o) % pairs * 2 + me % 2
            return remote(src.at[pl.ds(a, size), 0], dst.at[me, pl.ds(a, size)], d_send.at[o, j], d_recv.at[o, j],
                          {"row": to})

        def relay(o, j):
            _, dst, a, size = cuts[j]
            d = (me // 2 - o + pairs) % pairs * 2 + me % 2
            return remote(dst.at[d, pl.ds(a, size)], dst.at[d, pl.ds(a, size)], r_send.at[o, j], r_recv.at[o, j],
                          {"row": other})

        away = [(o, j) for j in range(len(cuts)) for o in range(1, pairs)]
        near = [(0, j) for j in range(len(cuts))]
        for o, j in away:
            direct(o, j).start()
    for i in range(blocks):
        part(i).start()
    if gather:
        own = [pltpu.make_async_copy(src.at[:, 0], dst.at[me], own_sem.at[j])
               for j, (src, dst) in enumerate(((piv, all_piv), (bas, all_bas)))]
        for copy in own:
            copy.start()
        for o, j in near:
            direct(o, j).start()
        for o, j in away:
            direct(o, j).wait_recv()
            relay(o, j).start()
        for o, j in near:
            direct(o, j).wait_recv()
        for o, j in away:
            relay(o, j).wait_recv()
            relay(o, j).wait_send()
        for o, j in away + near:
            direct(o, j).wait_send()
        for copy in own:
            copy.wait()
    for i in range(blocks):
        if h:
            part(i).wait_recv()
            part(i).wait_send()
        else:
            part(i).wait()


def shift_columns(h, s, per, ident, child, *factors):
    R = lax.axis_size("row")
    T, tile = child.shape[0], child.shape[-1]
    blocks = T // per - s
    moved = jax.ShapeDtypeStruct((per * blocks, tile, tile), f32)
    remote_ids = bool(h) or bool(factors)
    params = pltpu.CompilerParams(collective_id=ident, has_side_effects=True) if remote_ids else None
    shapes, scratch = [moved], [DMA((blocks,)), DMA((blocks,))]
    if factors:
        shapes += [jax.ShapeDtypeStruct((R,) + (f.shape[0],) + f.shape[2:], f32) for f in factors]
        scratch += [DMA((2,))] + [DMA((R // 2, 6))] * 4
    out = pl.pallas_call(
        lambda *refs: shift_kernel(h, s, per, *refs),
        in_specs=[ANY] * (1 + len(factors)),
        out_specs=[VMEM] * len(shapes),
        out_shape=shapes,
        scratch_shapes=scratch,
        compiler_params=params,
        name=f"shift_{s}_{h}",
    )(child, *factors)
    return tuple(out)


def product_kernel(per, S, bmap, everyone, out, mine_top, mine_low, their_top, their_low):
    R, T, rank, width = everyone.shape
    C = out.shape[0]
    spot = Layout(bmap, S)
    for t in range(T):
        top, low = split(everyone[spot.src_row(t // per), t])
        mine_top[t * rank : (t + 1) * rank, :] = top
        mine_low[t * rank : (t + 1) * rank, :] = low
    at = 0
    for s in range(S):
        for c in range(C):
            src = spot.src_col(s, c)
            top, low = split(everyone[lax.rem(src, R), s * per + lax.div(src, R)])
            their_top[c * rank : (c + 1) * rank, :] = top
            their_low[c * rank : (c + 1) * rank, :] = low
        first = s * per * rank
        size = T * rank - first
        mine = (mine_top[first:, :], mine_low[first:, :])
        got = dot3((their_top[...], their_low[...]), mine, ((1,), (1,)))
        out[:, :, at : at + size] = got.reshape(C, rank, size)
        at += size


def products(bmap, everyone, C, per):
    R, T, rank, width = everyone.shape
    S = T // per
    total = sum((S - s) * per * rank for s in range(S))
    return pl.pallas_call(
        lambda *refs: product_kernel(per, S, *refs),
        in_specs=[SMEM, VMEM],
        out_specs=VMEM,
        out_shape=jax.ShapeDtypeStruct((C, rank, total), f32),
        scratch_shapes=[pltpu.VMEM((T * rank, width), bf16)] * 2 + [pltpu.VMEM((C * rank, width), bf16)] * 2,
        name="products",
    )(bmap, everyone)


PARTS = 4


def sum_kernel(per, bmap, partial, *refs):
    S = len(refs) - 9
    moved = refs[:S]
    out, landed, slots, outbox, send, recv, row_send, row_recv, own_sem = refs[S:]
    R, n = lax.axis_size("row"), lax.axis_size("col")
    my_row, me = lax.axis_index("row"), lax.axis_index("col")
    chunk = partial.shape[1] // (2 * PARTS)
    pos = ring_spot(me, n)
    right = ring_place((pos + 1) % n, n)
    left = ring_place((pos + n - 1) % n, n)
    greet([{"col": left}, {"col": right}] + [{"row": (my_row + k) % R} for k in range(1, R)])
    rows = lambda side, h: pl.ds((PARTS * side + h) * chunk, chunk)

    def part(side, k, h):
        q = (pos - 1 - k + n) % n if side == 0 else (pos + 1 + k) % n
        return partial.at[ring_place(q, n), rows(side, h)]

    def hop(side, k, h):
        src = part(side, 0, h) if k == 0 else slots.at[side, k - 1, h]
        return remote(src, slots.at[side, k, h], send.at[side, k, h], recv.at[side, k, h],
                      {"col": right if side == 0 else left})

    def cross(k):
        return remote(outbox.at[k - 1], landed.at[k], row_send.at[k - 1], row_recv.at[k - 1], {"row": (my_row + k) % R})

    for h in range(PARTS):
        for side in range(2):
            hop(side, 0, h).start()

    spot = Layout(bmap, S)
    for k in [R // 2] + [k for k in range(R) if k != R // 2]:
        block = sum(u * (lax.rem(spot.shift(u), R) == k).astype(i32) for u in range(S))
        for s in range(S):
            place = jnp.clip(block - s, 0, S - 1 - s)
            for p in range(per):
                tile = moved[s][place * per + p]
                if k == 0:
                    landed[0, s, p] = tile
                else:
                    outbox[k - 1, s, p] = tile
        if k:
            cross(k).start()

    every = [(k, h, side) for k in range(n - 1) for h in range(PARTS) for side in range(2)]
    for k, h, side in every:
        if k > 0:
            hop(side, k - 1, h).wait_recv()
            slots[side, k - 1, h] = slots[side, k - 1, h] + part(side, k, h)[...]
            hop(side, k, h).start()
    for h in range(PARTS):
        for side in range(2):
            hop(side, n - 2, h).wait_recv()
            out[rows(side, h), :] = slots[side, n - 2, h] + partial[me, rows(side, h), :]
    for k in range(1, R):
        cross(k).wait_recv()
        cross(k).wait_send()
    for k, h, side in every:
        hop(side, k, h).wait_send()


def sum_and_rows(bmap, partial, moved, per):
    R = lax.axis_size("row")
    n, rank, total = partial.shape
    S, tile = len(moved), moved[0].shape[-1]
    box = (S, per, tile, tile)
    return pl.pallas_call(
        lambda *refs: sum_kernel(per, *refs),
        in_specs=[SMEM] + [VMEM] * (1 + S),
        out_specs=[VMEM] * 2,
        out_shape=[jax.ShapeDtypeStruct((rank, total), f32), jax.ShapeDtypeStruct((R,) + box, f32)],
        scratch_shapes=[
            pltpu.VMEM((2, n - 1, PARTS, rank // (2 * PARTS), total), f32),
            pltpu.VMEM((R - 1,) + box, f32),
            DMA((2, n - 1, PARTS)), DMA((2, n - 1, PARTS)), DMA((R - 1,)), DMA((R - 1,)), DMA,
        ],
        compiler_params=pltpu.CompilerParams(collective_id=1, has_side_effects=True),
        name="sum_and_rows",
    )(bmap, partial, *moved)


def update_kernel(per, C, bmap, start, ranks, weights, bases, landed, parent, came, out, held, own, sems):
    S, T, tile = out.shape[:3]
    R, _, rank, _ = bases.shape
    bcols = parent.shape[2]
    spot = Layout(bmap, S)
    k, b = own_column(start[0], spot.col, C, bcols)
    is_owner = k < PANEL_T
    copies = []
    for u in range(S):
        first = spot.first_row(u)
        for q in range(per):
            p = lax.rem(q + per * S * 2 - first, per)
            copies.append(pltpu.make_async_copy(parent.at[first + p, 0, b, 0], own.at[q, u], sems.at[q, u]))
            copies[-1].start()

    depth = lax.broadcasted_iota(i32, (rank, tile), 0)

    def basis(row, t):
        return split(jnp.where(depth < ranks[t * R + row], bases[row, t], 0.0))

    at = 0
    for s in range(S):
        size = (S - s) * per * rank
        src = spot.src_col(s)
        j = s * C + src
        col_basis = basis(lax.rem(src, R), s * per + lax.div(src, R))
        half = dot3(split(weights[:, at : at + size]), col_basis, ((0,), (0,)))
        at += size
        for t in range(s * per, T):
            u, p = t // per, t % per
            i = t - s * per
            row = spot.src_row(u)
            update = dot3(basis(row, t), split(half[i * rank : (i + 1) * rank]), ((0,), (0,)))
            moved = landed[lax.rem(spot.shift(u), R), s, p]
            out[s, t] = jnp.where(t * R + row >= j, moved - update, 0.0)

    s_own = lax.div(b, bcols // S)
    reached = spot.first_col(s_own) == b
    for copy in copies:
        copy.wait()
    for u in range(S):
        first = spot.first_row(u)
        for q in range(per):
            p = lax.rem(q + per * S * 2 - first, per)
            child = jnp.where(reached & (s_own <= u), out[jnp.minimum(s_own, u), u * per + p], 0.0)
            held[q, u] = jnp.where(is_owner, own[q, u] + child, came[q, u])


def updates(bmap, start, ranks, weights, bases, landed, parent, came, C, per):
    R, T, rank, tile = bases.shape
    S = T // per
    piece = (per, S, tile, tile)
    return pl.pallas_call(
        lambda *refs: update_kernel(per, C, *refs),
        in_specs=[SMEM, SMEM, SMEM, VMEM, VMEM, VMEM, ANY, VMEM],
        out_specs=[VMEM, VMEM],
        out_shape=[jax.ShapeDtypeStruct((S, T, tile, tile), f32), jax.ShapeDtypeStruct(piece, f32)],
        scratch_shapes=[pltpu.VMEM(piece, f32), DMA((per, S))],
        name="updates",
    )(bmap, start, ranks, weights, bases, landed, parent, came)


def panel_kernel(u0, held, panel, cols, send, recv, own_sem, self_sem, cross_send, cross_recv, relay_send):
    R, n = lax.axis_size("row"), lax.axis_size("col")
    my_row, me = lax.axis_index("row"), lax.axis_index("col")
    us = pl.ds(u0, held.shape[1] - u0)
    pos = ring_spot(me, n)
    right = ring_place((pos + 1) % n, n)
    left = ring_place((pos + n - 1) % n, n)
    root, parity = me % R, me // R
    is_root = my_row == root
    partner = my_row + 1 - 2 * (my_row % 2)
    greet([{"col": left}, {"col": right}] + [{"row": (my_row + k) % R} for k in range(1, R)])

    own = pltpu.make_async_copy(held, panel.at[me], own_sem)
    own.start()

    def block(side, k):
        return ring_place((pos - k + n) % n if side == 0 else (pos + k) % n, n)

    def step(side, k, h):
        d = block(side, k)
        src = held.at[h, us] if k == 0 else panel.at[d, h, us]
        return remote(src, panel.at[d, h, us], send.at[side, k, h], recv.at[side, k, h],
                      {"col": right if side == 0 else left})

    def arrival(side, k, h):
        d = block(side, k + 1)
        return remote(panel.at[d, h, us], panel.at[d, h, us], send.at[side, k, h], recv.at[side, k, h],
                      {"col": right if side == 0 else left})

    def cross(d, o):
        to = partner if o == 0 else (my_row // 2 + o) % (R // 2) * 2 + (my_row + d) % 2
        return remote(panel.at[d, parity, us], cols.at[d, us], cross_send.at[d, o], cross_recv.at[d], {"row": to})

    def mine(d):
        return pltpu.make_async_copy(panel.at[d, parity, us], cols.at[d, us], self_sem.at[d])

    def forward(d, h):
        @pl.when(is_root & (parity == h))
        def _():
            for o in range(1, R // 2):
                cross(d, o).start()
            cross(d, 0).start()
            mine(d).start()

    last = n // 2 - 1
    used = [(side, k, h) for k in range(n // 2) for h in range(2) for side in range(2) if k < last or h == side]
    for side, k, h in used:
        if k > 0:
            arrival(side, k - 1, h).wait_recv()
        step(side, k, h).start()
        if k > 0:
            forward(block(side, k), h)
        elif side == 0 and h == 1:
            own.wait()
            forward(me, 0)
            forward(me, 1)
    for side in range(2):
        arrival(side, last - 1, 1 - side).wait_recv()
        forward(block(side, last), 1 - side)
    for side in range(2):
        arrival(side, last, side).wait_recv()
        forward(block(side, last + 1), side)

    order = [me] + [block(side, k) for k in range(1, n // 2) for side in range(2)] + [block(0, n // 2)]

    @pl.when(is_root)
    def _():
        for d in order:
            for o in range(R // 2):
                cross(d, o).wait_send()
            mine(d).wait()

    def relay(d):
        return remote(cols.at[d, us], cols.at[d, us], relay_send.at[d], cross_recv.at[d], {"row": partner})

    near = my_row // 2 == root // 2

    @pl.when(~is_root & near)
    def _():
        for d in order:
            relay(d).wait_recv()

    for d in order:
        @pl.when(~near & ((my_row + root + d) % 2 == 0))
        def _():
            relay(d).wait_recv()
            relay(d).start()

    for d in order:
        @pl.when(~near & ((my_row + root + d) % 2 != 0))
        def _():
            relay(d).wait_recv()

        @pl.when(~near & ((my_row + root + d) % 2 == 0))
        def _():
            relay(d).wait_send()

    for side, k, h in used:
        step(side, k, h).wait_send()


def gather_panel(u0, held):
    R, n = lax.axis_size("row"), lax.axis_size("col")
    per, S, tile, _ = held.shape
    return tuple(pl.pallas_call(
        lambda *refs: panel_kernel(u0, *refs),
        in_specs=[VMEM],
        out_specs=[VMEM, VMEM],
        out_shape=[jax.ShapeDtypeStruct((n,) + held.shape, f32), jax.ShapeDtypeStruct((n, S, tile, tile), f32)],
        scratch_shapes=[DMA((2, n // 2, 2)), DMA((2, n // 2, 2)), DMA, DMA((n,)), DMA((n, R // 2)), DMA((n,)), DMA((n,))],
        compiler_params=pltpu.CompilerParams(collective_id=2 + u0, has_side_effects=True),
        name=f"panel_{u0}",
    )(held))


def final_kernel(bmap, start, parent, payload, panel, cols, inverse, out, inv_top, inv_low, col_top, col_low, high, low):
    step = pl.program_id(0)
    per, bcols = parent.shape[0], parent.shape[2]
    tile = parent.shape[4]
    S = payload.shape[0]
    group = bcols // S
    spot = Layout(bmap, S)
    R, C = spot.R, spot.C
    first_active = start[0] + PANEL_T
    owner = [lax.rem(start[0] + k, C) for k in range(PANEL_T)]
    spare = [lax.rem(start[0] + k + C // 2, C) for k in range(PANEL_T)]

    @pl.when(step == 0)
    def _():
        top, rest = split(inverse[...])
        inv_top[...] = top
        inv_low[...] = rest
        for b in range(bcols):
            a = per * b + lax.div(spot.col, R)
            u = b * per // (2 * per)
            first = spot.first_row(u, lax.rem(spot.col, R))
            hit = (a >= first) & (a < first + per)
            for k in range(PANEL_T):
                top, rest = split(cols[jnp.where(hit, owner[k], spare[k]), u])
                col_top[b * tile : (b + 1) * tile, k * tile : (k + 1) * tile] = top
                col_low[b * tile : (b + 1) * tile, k * tile : (k + 1) * tile] = rest

    u = lax.div(step, 2)
    first = spot.first_row(u)
    places = [step * per + p - first for p in range(per)]
    hits = [(d >= 0) & (d < per) for d in places]
    big_rows = [spot.row + (step * per + p) * R for p in range(per)]
    big_cols = [spot.col + b * C for b in range(bcols)]

    for b in range(bcols):
        s = b // group
        reached = (spot.first_col(s) == b) & (s <= u)
        for p in range(per):
            out[p, 0, b, 0] = parent[p, 0, b, 0]

            @pl.when(hits[p] & reached)
            def _():
                out[p, 0, b, 0] = parent[p, 0, b, 0] + payload[s, u * per + places[p]]

    @pl.when(big_rows[-1] >= first_active)
    def _():
        stacked = [
            jnp.concatenate([panel[jnp.where(hits[p], owner[k], spare[k]), p, u] for k in range(PANEL_T)], axis=1)
            for p in range(per)
        ]
        scaled = dot3(split(jnp.concatenate(stacked, axis=0)), (inv_top[...], inv_low[...]), ((1,), (0,)))
        top, rest = split(scaled)
        high[...] = top
        low[...] = rest
        for g in range(S):
            @pl.when((big_rows[-1] >= big_cols[g * group]) & (big_cols[g * group + group - 1] >= first_active))
            def _():
                at = pl.ds(g * group * tile, group * tile)
                trailing = dot3((high[...], low[...]), (col_top[at, :], col_low[at, :]), ((1,), (1,)))
                for j in range(group):
                    b = g * group + j
                    for p in range(per):
                        active = (big_rows[p] >= big_cols[b]) & (big_cols[b] >= first_active)
                        part = trailing[p * tile : (p + 1) * tile, j * tile : (j + 1) * tile]
                        out[p, 0, b, 0] = out[p, 0, b, 0] - jnp.where(active, part, 0.0)


def finish(bmap, start, parent, payload, panel, cols, inverse, per):
    rows, _, bcols, _, tile, _ = parent.shape
    wide = PANEL_T * tile
    whole = lambda a: pl.BlockSpec(a.shape, lambda i, m, t: (0,) * a.ndim, pipeline_mode=pl.Buffered(1))
    big = pl.BlockSpec((per, 1, bcols, 1, tile, tile), lambda i, m, t: (i, 0, 0, 0, 0, 0))
    flops = 6 * rows * tile * wide * (wide + bcols * tile)
    return pl.pallas_call(
        final_kernel,
        grid_spec=pltpu.PrefetchScalarGridSpec(
            num_scalar_prefetch=2,
            grid=(rows // per,),
            in_specs=[big, whole(payload), whole(panel), whole(cols), whole(inverse)],
            out_specs=big,
            scratch_shapes=[pltpu.VMEM((wide, wide), bf16)] * 2 + [pltpu.VMEM((bcols * tile, wide), bf16)] * 2
            + [pltpu.VMEM((per * tile, wide), bf16)] * 2,
        ),
        out_shape=jax.ShapeDtypeStruct(parent.shape, f32),
        cost_estimate=pl.CostEstimate(flops=flops, bytes_accessed=10 * parent.size, transcendentals=0),
        name="finish",
    )(bmap, start, parent, payload, panel, cols, inverse)


def per_device(contribution, parent, row_basis, pivot_basis, ranks, block_map, panel_start, inverse):
    R, C = lax.axis_size("row"), lax.axis_size("col")
    S = contribution.shape[2]
    per = C // R
    shift = [block_map[u * C] - 2 * C * u for u in range(S)]

    rest = pick_rest(block_map, panel_start, parent, per, S)
    came = lax.ppermute(rest, "col", [(d, (d + C // 2) % C) for d in range(C)])

    ident = 2 + S
    moved = []
    for s in range(S):
        branches = []
        for h in range(C):
            branches.append(lambda *a, h=h, s=s, ident=ident: shift_columns(h, s, per, ident, *a))
            ident += 1
        if s == 0:
            first, all_piv, all_bas = lax.switch(shift[0], branches, contribution, pivot_basis, row_basis)
            moved.append(first)
        else:
            moved.append(lax.switch(shift[s], branches, contribution)[0])

    partial = products(block_map, all_piv, C, per)
    weights, landed = sum_and_rows(block_map, partial, moved, per)
    payload, held = updates(block_map, panel_start, ranks, weights, all_bas, landed, parent, came, C, per)

    top = S // 2 + 1
    needless = lax.div(panel_start[0] + PANEL_T, 2 * C)
    panel, cols = lax.switch(jnp.minimum(needless, top - 1), [lambda v, u=u: gather_panel(u, v) for u in range(top)], held)
    return finish(block_map, panel_start, parent, payload, panel, cols, inverse, per)


def solution(mesh):
    placed = (
        P(None, "row", None, "col", None, None),
        P(None, "row", None, "col", None, None),
        P(None, "row", None, None),
        P(None, "row", None, "col"),
        P(),
        P(),
        P(),
        P(),
    )
    return jax.shard_map(
        per_device,
        mesh=mesh,
        in_specs=placed,
        out_specs=P(None, "row", None, "col", None, None),
        check_vma=False,
    )
```

```python
import jax
import jax.numpy as jnp
from jax import lax
from jax.experimental import pallas as pl
from jax.experimental.pallas import tpu as pltpu
from jax.sharding import PartitionSpec as P

PANEL_T = 4
f32 = jnp.float32
bf16 = jnp.bfloat16
i32 = jnp.int32
MESH = pl.DeviceIdType.MESH
DMA = pltpu.SemaphoreType.DMA
SMEM = pl.BlockSpec(memory_space=pltpu.SMEM)
VMEM = pl.BlockSpec(memory_space=pltpu.VMEM)
ANY = pl.BlockSpec(memory_space=pl.ANY)
HBM = pl.BlockSpec(memory_space=pltpu.HBM)
ROOM = 32 << 20


def split(x):
    top = x.astype(bf16)
    return top, (x - top.astype(f32)).astype(bf16)


def dot3(a, b, dims):
    (ah, al), (bh, bl) = a, b
    one = lambda p, q: lax.dot_general(p, q, (dims, ((), ())), preferred_element_type=f32)
    return one(ah, bh) + (one(ah, bl) + one(al, bh))


def ring_place(p, n):
    return jnp.where(p < n // 2, 2 * p, 2 * (n - 1 - p) + 1)


def ring_spot(me, n):
    return jnp.where(me % 2 == 0, me // 2, n - 1 - me // 2)


def greet(targets):
    barrier = pltpu.get_barrier_semaphore()
    for target in targets:
        pl.semaphore_signal(barrier, inc=1, device_id=target, device_id_type=MESH)
    pl.semaphore_wait(barrier, len(targets))


def remote(src, dst, send, recv, to):
    return pltpu.make_async_remote_copy(src, dst, send, recv, device_id=to, device_id_type=MESH)


class Layout:
    def __init__(self, bmap, blocks):
        self.map = bmap
        self.S = blocks
        self.R, self.C = lax.axis_size("row"), lax.axis_size("col")
        self.row, self.col = lax.axis_index("row"), lax.axis_index("col")

    def shift(self, u):
        return self.map[u * self.C] - 2 * self.C * u

    def src_row(self, u, row=None):
        row = self.row if row is None else row
        return lax.rem(row + self.C * self.R - self.shift(u), self.R)

    def src_col(self, s, col=None):
        col = self.col if col is None else col
        return lax.rem(col + self.C - self.shift(s), self.C)

    def first_row(self, u, row=None):
        return lax.div(2 * self.C * u + self.shift(u) + self.src_row(u, row), self.R)

    def first_col(self, s):
        return lax.div(2 * self.C * s + self.shift(s) + self.src_col(s), self.C)


def own_column(start, col, C, bcols):
    k = lax.rem(col - start + C * bcols, C)
    return jnp.minimum(lax.div(start + k, C), bcols - 1)


def shift_kernel(h, s, per, *refs):
    R, n = lax.axis_size("row"), lax.axis_size("col")
    me, my_col = lax.axis_index("row"), lax.axis_index("col")
    gather = s == 0
    if gather:
        child, piv, bas, moved, all_piv, all_bas, send, recv, own_sem, d_send, d_recv, r_send, r_recv = refs
    else:
        child, moved, send, recv = refs
    blocks = moved.shape[0] // per
    pairs = R // 2
    other = me + 1 - 2 * (me % 2)

    signals = []
    if h:
        signals.append({"col": (my_col + n - h) % n})
    if gather:
        signals += [{"row": (me + k) % R} for k in range(1, R)]
    if signals:
        greet(signals)

    def part(i):
        src = child.at[pl.ds(per * (s + i), per), 0, s, 0]
        dst = moved.at[pl.ds(per * i, per)]
        if h:
            return remote(src, dst, send.at[i], recv.at[i], {"col": (my_col + h) % n})
        return pltpu.make_async_copy(src, dst, recv.at[i])

    if gather:
        T = piv.shape[0]
        cuts = [(piv, all_piv, j * T // 4, T // 4) for j in range(4)]
        cuts += [(bas, all_bas, j * T // 2, T // 2) for j in range(2)]

        def direct(o, j):
            src, dst, a, size = cuts[j]
            to = other if o == 0 else (me // 2 + o) % pairs * 2 + me % 2
            return remote(src.at[pl.ds(a, size), 0], dst.at[me, pl.ds(a, size)], d_send.at[o, j], d_recv.at[o, j],
                          {"row": to})

        def relay(o, j):
            _, dst, a, size = cuts[j]
            d = (me // 2 - o + pairs) % pairs * 2 + me % 2
            return remote(dst.at[d, pl.ds(a, size)], dst.at[d, pl.ds(a, size)], r_send.at[o, j], r_recv.at[o, j],
                          {"row": other})

        away = [(o, j) for j in range(len(cuts)) for o in range(1, pairs)]
        near = [(0, j) for j in range(len(cuts))]
        for o, j in away:
            direct(o, j).start()
    for i in range(blocks):
        part(i).start()
    if gather:
        own = [pltpu.make_async_copy(src.at[:, 0], dst.at[me], own_sem.at[j])
               for j, (src, dst) in enumerate(((piv, all_piv), (bas, all_bas)))]
        for copy in own:
            copy.start()
        for o, j in near:
            direct(o, j).start()
        for o, j in away:
            direct(o, j).wait_recv()
            relay(o, j).start()
        for o, j in near:
            direct(o, j).wait_recv()
        for o, j in away:
            relay(o, j).wait_recv()
            relay(o, j).wait_send()
        for o, j in away + near:
            direct(o, j).wait_send()
        for copy in own:
            copy.wait()
    for i in range(blocks):
        if h:
            part(i).wait_recv()
            part(i).wait_send()
        else:
            part(i).wait()


def shift_columns(h, s, per, ident, child, *factors):
    R = lax.axis_size("row")
    T, tile = child.shape[0], child.shape[-1]
    blocks = T // per - s
    moved = jax.ShapeDtypeStruct((per * blocks, tile, tile), f32)
    remote_ids = bool(h) or bool(factors)
    params = (
        pltpu.CompilerParams(collective_id=ident, has_side_effects=True, vmem_limit_bytes=ROOM)
        if remote_ids
        else pltpu.CompilerParams(vmem_limit_bytes=ROOM)
    )
    shapes, scratch = [moved], [DMA((blocks,)), DMA((blocks,))]
    if factors:
        shapes += [jax.ShapeDtypeStruct((R,) + (f.shape[0],) + f.shape[2:], f32) for f in factors]
        scratch += [DMA((2,))] + [DMA((R // 2, 6))] * 4
    out = pl.pallas_call(
        lambda *refs: shift_kernel(h, s, per, *refs),
        in_specs=[ANY] * (1 + len(factors)),
        out_specs=[VMEM] * len(shapes),
        out_shape=shapes,
        scratch_shapes=scratch,
        compiler_params=params,
        name=f"shift_{s}_{h}",
    )(child, *factors)
    return tuple(out)


def product_kernel(per, S, bmap, everyone, out, mine_top, mine_low, their_top, their_low):
    R, T, rank, width = everyone.shape
    C = out.shape[0]
    spot = Layout(bmap, S)
    for t in range(T):
        top, low = split(everyone[spot.src_row(t // per), t])
        mine_top[t * rank : (t + 1) * rank, :] = top
        mine_low[t * rank : (t + 1) * rank, :] = low
    at = 0
    for s in range(S):
        for c in range(C):
            src = spot.src_col(s, c)
            top, low = split(everyone[lax.rem(src, R), s * per + lax.div(src, R)])
            their_top[c * rank : (c + 1) * rank, :] = top
            their_low[c * rank : (c + 1) * rank, :] = low
        first = s * per * rank
        size = T * rank - first
        mine = (mine_top[first:, :], mine_low[first:, :])
        got = dot3((their_top[...], their_low[...]), mine, ((1,), (1,)))
        out[:, :, at : at + size] = got.reshape(C, rank, size)
        at += size


def products(bmap, everyone, C, per):
    R, T, rank, width = everyone.shape
    S = T // per
    total = sum((S - s) * per * rank for s in range(S))
    return pl.pallas_call(
        lambda *refs: product_kernel(per, S, *refs),
        in_specs=[SMEM, VMEM],
        out_specs=VMEM,
        out_shape=jax.ShapeDtypeStruct((C, rank, total), f32),
        scratch_shapes=[pltpu.VMEM((T * rank, width), bf16)] * 2 + [pltpu.VMEM((C * rank, width), bf16)] * 2,
        compiler_params=pltpu.CompilerParams(vmem_limit_bytes=ROOM),
        name="products",
    )(bmap, everyone)


PARTS = 4


def sum_kernel(per, bmap, partial, *refs):
    S = len(refs) - 9
    moved = refs[:S]
    out, landed, slots, outbox, send, recv, row_send, row_recv, own_sem = refs[S:]
    R, n = lax.axis_size("row"), lax.axis_size("col")
    my_row, me = lax.axis_index("row"), lax.axis_index("col")
    chunk = partial.shape[1] // (2 * PARTS)
    pos = ring_spot(me, n)
    right = ring_place((pos + 1) % n, n)
    left = ring_place((pos + n - 1) % n, n)
    greet([{"col": left}, {"col": right}] + [{"row": (my_row + k) % R} for k in range(1, R)])
    rows = lambda side, h: pl.ds((PARTS * side + h) * chunk, chunk)

    def part(side, k, h):
        q = (pos - 1 - k + n) % n if side == 0 else (pos + 1 + k) % n
        return partial.at[ring_place(q, n), rows(side, h)]

    def hop(side, k, h):
        src = part(side, 0, h) if k == 0 else slots.at[side, k - 1, h]
        return remote(src, slots.at[side, k, h], send.at[side, k, h], recv.at[side, k, h],
                      {"col": right if side == 0 else left})

    def cross(k):
        return remote(outbox.at[k - 1], landed.at[k], row_send.at[k - 1], row_recv.at[k - 1], {"row": (my_row + k) % R})

    for h in range(PARTS):
        for side in range(2):
            hop(side, 0, h).start()

    spot = Layout(bmap, S)
    for k in [R // 2] + [k for k in range(R) if k != R // 2]:
        block = sum(u * (lax.rem(spot.shift(u), R) == k).astype(i32) for u in range(S))
        for s in range(S):
            place = jnp.clip(block - s, 0, S - 1 - s)
            for p in range(per):
                tile = moved[s][place * per + p]
                if k == 0:
                    landed[0, s, p] = tile
                else:
                    outbox[k - 1, s, p] = tile
        if k:
            cross(k).start()

    every = [(k, h, side) for k in range(n - 1) for h in range(PARTS) for side in range(2)]
    for k, h, side in every:
        if k > 0:
            hop(side, k - 1, h).wait_recv()
            slots[side, k - 1, h] = slots[side, k - 1, h] + part(side, k, h)[...]
            hop(side, k, h).start()
    for h in range(PARTS):
        for side in range(2):
            hop(side, n - 2, h).wait_recv()
            out[rows(side, h), :] = slots[side, n - 2, h] + partial[me, rows(side, h), :]
    for k in range(1, R):
        cross(k).wait_recv()
        cross(k).wait_send()
    for k, h, side in every:
        hop(side, k, h).wait_send()


def sum_and_rows(bmap, partial, moved, per):
    R = lax.axis_size("row")
    n, rank, total = partial.shape
    S, tile = len(moved), moved[0].shape[-1]
    box = (S, per, tile, tile)
    return pl.pallas_call(
        lambda *refs: sum_kernel(per, *refs),
        in_specs=[SMEM] + [VMEM] * (1 + S),
        out_specs=[VMEM] * 2,
        out_shape=[jax.ShapeDtypeStruct((rank, total), f32), jax.ShapeDtypeStruct((R,) + box, f32)],
        scratch_shapes=[
            pltpu.VMEM((2, n - 1, PARTS, rank // (2 * PARTS), total), f32),
            pltpu.VMEM((R - 1,) + box, f32),
            DMA((2, n - 1, PARTS)), DMA((2, n - 1, PARTS)), DMA((R - 1,)), DMA((R - 1,)), DMA,
        ],
        compiler_params=pltpu.CompilerParams(collective_id=1, has_side_effects=True, vmem_limit_bytes=ROOM),
        name="sum_and_rows",
    )(bmap, partial, *moved)


def update_kernel(per, C, bmap, start, ranks, weights, bases, landed, parent, out, held, sems):
    S, T, tile = out.shape[:3]
    R, _, rank, _ = bases.shape
    bcols = parent.shape[2]
    spot = Layout(bmap, S)
    b = own_column(start[0], spot.col, C, bcols)
    copies = []
    for i in range(held.shape[1]):
        for q in range(per):
            copies.append(pltpu.make_async_copy(parent.at[per * i + q, 0, b, 0], held.at[q, i], sems.at[q, i]))
            copies[-1].start()

    depth = lax.broadcasted_iota(i32, (rank, tile), 0)

    def basis(row, t):
        return split(jnp.where(depth < ranks[t * R + row], bases[row, t], 0.0))

    at = 0
    for s in range(S):
        size = (S - s) * per * rank
        src = spot.src_col(s)
        j = s * C + src
        col_basis = basis(lax.rem(src, R), s * per + lax.div(src, R))
        half = dot3(split(weights[:, at : at + size]), col_basis, ((0,), (0,)))
        at += size
        for t in range(s * per, T):
            u, p = t // per, t % per
            i = t - s * per
            row = spot.src_row(u)
            update = dot3(basis(row, t), split(half[i * rank : (i + 1) * rank]), ((0,), (0,)))
            moved = landed[lax.rem(spot.shift(u), R), s, p]
            out[s, t] = jnp.where(t * R + row >= j, moved - update, 0.0)

    s_own = lax.div(b, bcols // S)
    reached = spot.first_col(s_own) == b
    for copy in copies:
        copy.wait()

    @pl.when(reached)
    def _():
        for u in range(S):
            @pl.when(s_own <= u)
            def _():
                for p in range(per):
                    a = spot.first_row(u) + p
                    q, i = lax.rem(a, per), lax.div(a, per)
                    held[q, i] = held[q, i] + out[s_own, u * per + p]


def updates(bmap, start, ranks, weights, bases, landed, parent, C, per):
    R, T, rank, tile = bases.shape
    S, rows = T // per, parent.shape[0]
    return pl.pallas_call(
        lambda *refs: update_kernel(per, C, *refs),
        in_specs=[SMEM, SMEM, SMEM, VMEM, VMEM, VMEM, HBM],
        out_specs=[VMEM, VMEM],
        out_shape=[
            jax.ShapeDtypeStruct((S, T, tile, tile), f32),
            jax.ShapeDtypeStruct((per, rows // per, tile, tile), f32),
        ],
        scratch_shapes=[DMA((per, rows // per))],
        compiler_params=pltpu.CompilerParams(vmem_limit_bytes=54 << 20),
        name="updates",
    )(bmap, start, ranks, weights, bases, landed, parent)


def panel_kernel(first, b0, held, panel, cols, recv, up, down, across, other, own_sem, self_sem, cross_send, cross_recv,
                 relay_send):
    R, n = lax.axis_size("row"), lax.axis_size("col")
    my_row, me = lax.axis_index("row"), lax.axis_index("col")
    Bn = held.shape[1]
    z, x, ends = me // 2, me % 2, n // 2 - 1
    side = me + 1 - 2 * x
    root, parity = me % R, me // R
    is_root = my_row == root
    partner = my_row + 1 - 2 * (my_row % 2)
    near = my_row // 2 == root // 2
    columns = range(PANEL_T)
    owner = [(first + k) % n for k in columns]

    barrier = pltpu.get_barrier_semaphore()
    for k in range(1, R):
        pl.semaphore_signal(barrier, inc=1, device_id={"row": (my_row + k) % R}, device_id_type=MESH)
    pl.semaphore_signal(barrier, inc=1, device_id={"col": side}, device_id_type=MESH)

    @pl.when(z > 0)
    def _():
        pl.semaphore_signal(barrier, inc=1, device_id={"col": me - 2}, device_id_type=MESH)

    @pl.when(z < ends)
    def _():
        pl.semaphore_signal(barrier, inc=1, device_id={"col": me + 2}, device_id_type=MESH)

    for k in columns:
        @pl.when(me == owner[k])
        def _():
            pltpu.make_async_copy(held, panel.at[k], own_sem).start()

    pl.semaphore_wait(barrier, R + jnp.minimum(z, 1) + jnp.minimum(ends - z, 1))

    for k in columns:
        @pl.when(me == owner[k])
        def _():
            pltpu.make_async_copy(held, panel.at[k], own_sem).wait()

    def hop(k, h, i, sem, to):
        ref = panel.at[k, h, i]
        return remote(ref, ref, sem.at[k, i], recv.at[k, h, i], {"col": to})

    def sends(k, i, act):
        zk, xk = owner[k] // 2, owner[k] % 2

        @pl.when(me == owner[k])
        def _():
            act(hop(k, 1 - x, i, other, side))

        @pl.when((z >= zk) & (z < ends))
        def _():
            act(hop(k, x, i, up, me + 2))

        @pl.when((z <= zk) & (z > 0))
        def _():
            act(hop(k, x, i, down, me - 2))

        @pl.when((z != zk) | (x == xk))
        def _():
            act(hop(k, x, i, across, side))

    def main(k, i):
        @pl.when(me != owner[k])
        def _():
            hop(k, x, i, up, side).wait_recv()

        sends(k, i, lambda copy: copy.start())

    def cross(k, i, o):
        to = partner if o == 0 else (my_row // 2 + o) % (R // 2) * 2 + (my_row + k) % 2
        return remote(panel.at[k, parity, i], cols.at[k, i], cross_send.at[k, i, o], cross_recv.at[k, i], {"row": to})

    def mine(k, i):
        return pltpu.make_async_copy(panel.at[k, parity, i], cols.at[k, i], self_sem.at[k, i])

    def late(k, i):
        @pl.when(me != owner[k])
        def _():
            hop(k, 1 - x, i, up, side).wait_recv()

        @pl.when(is_root)
        def _():
            for o in range(1, R // 2):
                cross(k, i, o).start()
            cross(k, i, 0).start()
            mine(k, i).start()

    def relay(k, i):
        return remote(cols.at[k, i], cols.at[k, i], relay_send.at[k, i], cross_recv.at[k, i], {"row": partner})

    def direct(k):
        return ~near & ((my_row + root + k) % 2 == 0)

    def pass_on(k, i):
        @pl.when(direct(k))
        def _():
            relay(k, i).wait_recv()
            relay(k, i).start()

    def body(j, _):
        @pl.when(j < Bn)
        def _():
            for k in columns:
                main(k, j)

        @pl.when((j > b0) & (j <= Bn))
        def _():
            for k in columns:
                late(k, j - 1)

        @pl.when(j > b0 + 1)
        def _():
            for k in columns:
                pass_on(k, j - 2)

        return 0

    lax.fori_loop(b0, Bn + 2, body, 0)

    def drain(i, _):
        for k in columns:
            sends(k, i, lambda copy: copy.wait_send())

            @pl.when(is_root)
            def _():
                for o in range(R // 2):
                    cross(k, i, o).wait_send()
                mine(k, i).wait()

            @pl.when(direct(k))
            def _():
                relay(k, i).wait_send()

            @pl.when(~direct(k) & ~is_root)
            def _():
                relay(k, i).wait_recv()

        return 0

    lax.fori_loop(b0, Bn, drain, 0)


def gather_panel(first, b0, ident, held):
    R = lax.axis_size("row")
    per, Bn, tile, _ = held.shape
    each = (PANEL_T, Bn)
    return tuple(pl.pallas_call(
        lambda *refs: panel_kernel(first, b0, *refs),
        in_specs=[VMEM],
        out_specs=[VMEM, VMEM],
        out_shape=[
            jax.ShapeDtypeStruct((PANEL_T,) + held.shape, f32),
            jax.ShapeDtypeStruct(each + (tile, tile), f32),
        ],
        scratch_shapes=[DMA((PANEL_T, per, Bn))] + [DMA(each)] * 4 + [DMA, DMA(each), DMA(each + (R // 2,)), DMA(each), DMA(each)],
        compiler_params=pltpu.CompilerParams(collective_id=ident, has_side_effects=True, vmem_limit_bytes=ROOM),
        name=f"panel_{first}_{b0}",
    )(held))


def final_kernel(bmap, start, parent, payload, panel, cols, inverse, out, inv_top, inv_low, col_top, col_low, high, low):
    step = pl.program_id(0)
    per, bcols = parent.shape[0], parent.shape[2]
    tile = parent.shape[4]
    S = payload.shape[0]
    group = bcols // S
    spot = Layout(bmap, S)
    R, C = spot.R, spot.C
    first_active = start[0] + PANEL_T

    @pl.when(step == 0)
    def _():
        top, rest = split(inverse[...])
        inv_top[...] = top
        inv_low[...] = rest
        for b in range(bcols):
            for k in range(PANEL_T):
                top, rest = split(cols[k, b])
                col_top[b * tile : (b + 1) * tile, k * tile : (k + 1) * tile] = top
                col_low[b * tile : (b + 1) * tile, k * tile : (k + 1) * tile] = rest

    u = lax.div(step, 2)
    first = spot.first_row(u)
    places = [step * per + p - first for p in range(per)]
    hits = [(d >= 0) & (d < per) for d in places]
    big_rows = [spot.row + (step * per + p) * R for p in range(per)]
    big_cols = [spot.col + b * C for b in range(bcols)]

    for b in range(bcols):
        s = b // group
        reached = (spot.first_col(s) == b) & (s <= u)
        for p in range(per):
            out[p, 0, b, 0] = parent[p, 0, b, 0]

            @pl.when(hits[p] & reached)
            def _():
                out[p, 0, b, 0] = parent[p, 0, b, 0] + payload[s, u * per + places[p]]

    @pl.when(big_rows[-1] >= first_active)
    def _():
        stacked = [jnp.concatenate([panel[k, p, step] for k in range(PANEL_T)], axis=1) for p in range(per)]
        scaled = dot3(split(jnp.concatenate(stacked, axis=0)), (inv_top[...], inv_low[...]), ((1,), (0,)))
        top, rest = split(scaled)
        high[...] = top
        low[...] = rest
        for g in range(S):
            @pl.when((big_rows[-1] >= big_cols[g * group]) & (big_cols[g * group + group - 1] >= first_active))
            def _():
                at = pl.ds(g * group * tile, group * tile)
                trailing = dot3((high[...], low[...]), (col_top[at, :], col_low[at, :]), ((1,), (1,)))
                for j in range(group):
                    b = g * group + j
                    for p in range(per):
                        active = (big_rows[p] >= big_cols[b]) & (big_cols[b] >= first_active)
                        part = trailing[p * tile : (p + 1) * tile, j * tile : (j + 1) * tile]
                        out[p, 0, b, 0] = out[p, 0, b, 0] - jnp.where(active, part, 0.0)


def finish(bmap, start, parent, payload, panel, cols, inverse, per):
    rows, _, bcols, _, tile, _ = parent.shape
    wide = PANEL_T * tile
    whole = lambda a: pl.BlockSpec(a.shape, lambda i, m, t: (0,) * a.ndim, pipeline_mode=pl.Buffered(1))
    big = pl.BlockSpec((per, 1, bcols, 1, tile, tile), lambda i, m, t: (i, 0, 0, 0, 0, 0))
    flops = 6 * rows * tile * wide * (wide + bcols * tile)
    return pl.pallas_call(
        final_kernel,
        grid_spec=pltpu.PrefetchScalarGridSpec(
            num_scalar_prefetch=2,
            grid=(rows // per,),
            in_specs=[big, whole(payload), whole(panel), whole(cols), whole(inverse)],
            out_specs=big,
            scratch_shapes=[pltpu.VMEM((wide, wide), bf16)] * 2 + [pltpu.VMEM((bcols * tile, wide), bf16)] * 2
            + [pltpu.VMEM((per * tile, wide), bf16)] * 2,
        ),
        out_shape=jax.ShapeDtypeStruct(parent.shape, f32),
        compiler_params=pltpu.CompilerParams(vmem_limit_bytes=48 << 20),
        cost_estimate=pl.CostEstimate(flops=flops, bytes_accessed=10 * parent.size, transcendentals=0),
        name="finish",
    )(bmap, start, parent, payload, panel, cols, inverse)


def per_device(contribution, parent, row_basis, pivot_basis, ranks, block_map, panel_start, inverse):
    R, C = lax.axis_size("row"), lax.axis_size("col")
    S = contribution.shape[2]
    per = C // R
    shift = [block_map[u * C] - 2 * C * u for u in range(S)]

    ident = 2
    moved = []
    for s in range(S):
        branches = []
        for h in range(C):
            branches.append(lambda *a, h=h, s=s, ident=ident: shift_columns(h, s, per, ident, *a))
            ident += 1
        if s == 0:
            first, all_piv, all_bas = lax.switch(shift[0], branches, contribution, pivot_basis, row_basis)
            moved.append(first)
        else:
            moved.append(lax.switch(shift[s], branches, contribution)[0])

    partial = products(block_map, all_piv, C, per)
    weights, landed = sum_and_rows(block_map, partial, moved, per)
    payload, held = updates(block_map, panel_start, ranks, weights, all_bas, landed, parent, C, per)

    branches = []
    pairs = parent.shape[0] // (2 * per)
    for first in range(C):
        for b0 in range(0, pairs, 2):
            b0 += (first + PANEL_T) // C
            branches.append(lambda v, first=first, b0=b0, ident=ident: gather_panel(first, b0, ident, v))
            ident += 1
    start = panel_start[0]
    which = lax.rem(start, C) * (pairs // 2) + jnp.minimum(lax.div(start, 2 * C), pairs // 2 - 1)
    panel, cols = lax.switch(which, branches, held)
    return finish(block_map, panel_start, parent, payload, panel, cols, inverse, per)


def solution(mesh):
    placed = (
        P(None, "row", None, "col", None, None),
        P(None, "row", None, "col", None, None),
        P(None, "row", None, None),
        P(None, "row", None, "col"),
        P(),
        P(),
        P(),
        P(),
    )
    return jax.shard_map(
        per_device,
        mesh=mesh,
        in_specs=placed,
        out_specs=P(None, "row", None, "col", None, None),
        check_vma=False,
    )
```

```python
import jax
import jax.numpy as jnp
from jax import lax
from jax.experimental import pallas as pl
from jax.experimental.pallas import tpu as pltpu
from jax.sharding import PartitionSpec as P

PANEL_T = 4
f32 = jnp.float32
bf16 = jnp.bfloat16
i32 = jnp.int32
MESH = pl.DeviceIdType.MESH
DMA = pltpu.SemaphoreType.DMA
SMEM = pl.BlockSpec(memory_space=pltpu.SMEM)
VMEM = pl.BlockSpec(memory_space=pltpu.VMEM)
ANY = pl.BlockSpec(memory_space=pl.ANY)
HBM = pl.BlockSpec(memory_space=pltpu.HBM)
ROOM = 32 << 20


def split(x):
    top = x.astype(bf16)
    return top, (x - top.astype(f32)).astype(bf16)


def dot3(a, b, dims):
    (ah, al), (bh, bl) = a, b
    one = lambda p, q: lax.dot_general(p, q, (dims, ((), ())), preferred_element_type=f32)
    return one(ah, bh) + (one(ah, bl) + one(al, bh))


def ring_place(p, n):
    return jnp.where(p < n // 2, 2 * p, 2 * (n - 1 - p) + 1)


def ring_spot(me, n):
    return jnp.where(me % 2 == 0, me // 2, n - 1 - me // 2)


def greet(targets):
    barrier = pltpu.get_barrier_semaphore()
    for target in targets:
        pl.semaphore_signal(barrier, inc=1, device_id=target, device_id_type=MESH)
    pl.semaphore_wait(barrier, len(targets))


def remote(src, dst, send, recv, to):
    return pltpu.make_async_remote_copy(src, dst, send, recv, device_id=to, device_id_type=MESH)


class Layout:
    def __init__(self, bmap, blocks):
        self.map = bmap
        self.S = blocks
        self.R, self.C = lax.axis_size("row"), lax.axis_size("col")
        self.row, self.col = lax.axis_index("row"), lax.axis_index("col")

    def shift(self, u):
        return self.map[u * self.C] - 2 * self.C * u

    def src_row(self, u, row=None):
        row = self.row if row is None else row
        return lax.rem(row + self.C * self.R - self.shift(u), self.R)

    def src_col(self, s, col=None):
        col = self.col if col is None else col
        return lax.rem(col + self.C - self.shift(s), self.C)

    def first_row(self, u, row=None):
        return lax.div(2 * self.C * u + self.shift(u) + self.src_row(u, row), self.R)

    def first_col(self, s):
        return lax.div(2 * self.C * s + self.shift(s) + self.src_col(s), self.C)


def own_column(start, col, C, bcols):
    k = lax.rem(col - start + C * bcols, C)
    return jnp.minimum(lax.div(start + k, C), bcols - 1)


def shift_kernel(h, s, per, *refs):
    R, n = lax.axis_size("row"), lax.axis_size("col")
    me, my_col = lax.axis_index("row"), lax.axis_index("col")
    gather = s == 0
    if gather:
        child, piv, bas, moved, all_piv, all_bas, send, recv, own_sem, d_send, d_recv, r_send, r_recv = refs
    else:
        child, moved, send, recv = refs
    blocks = moved.shape[0] // per
    pairs = R // 2
    other = me + 1 - 2 * (me % 2)

    signals = []
    if h:
        signals.append({"col": (my_col + n - h) % n})
    if gather:
        signals += [{"row": (me + k) % R} for k in range(1, R)]
    if signals:
        greet(signals)

    def part(i):
        src = child.at[pl.ds(per * (s + i), per), 0, s, 0]
        dst = moved.at[pl.ds(per * i, per)]
        if h:
            return remote(src, dst, send.at[i], recv.at[i], {"col": (my_col + h) % n})
        return pltpu.make_async_copy(src, dst, recv.at[i])

    if gather:
        T = piv.shape[0]
        cuts = [(piv, all_piv, j * T // 4, T // 4) for j in range(4)]
        cuts += [(bas, all_bas, j * T // 2, T // 2) for j in range(2)]

        def direct(o, j):
            src, dst, a, size = cuts[j]
            to = other if o == 0 else (me // 2 + o) % pairs * 2 + me % 2
            return remote(src.at[pl.ds(a, size), 0], dst.at[me, pl.ds(a, size)], d_send.at[o, j], d_recv.at[o, j],
                          {"row": to})

        def relay(o, j):
            _, dst, a, size = cuts[j]
            d = (me // 2 - o + pairs) % pairs * 2 + me % 2
            return remote(dst.at[d, pl.ds(a, size)], dst.at[d, pl.ds(a, size)], r_send.at[o, j], r_recv.at[o, j],
                          {"row": other})

        away = [(o, j) for j in range(len(cuts)) for o in range(1, pairs)]
        near = [(0, j) for j in range(len(cuts))]
        for o, j in away:
            direct(o, j).start()
    for i in range(blocks):
        part(i).start()
    if gather:
        own = [pltpu.make_async_copy(src.at[:, 0], dst.at[me], own_sem.at[j])
               for j, (src, dst) in enumerate(((piv, all_piv), (bas, all_bas)))]
        for copy in own:
            copy.start()
        for o, j in near:
            direct(o, j).start()
        for o, j in away:
            direct(o, j).wait_recv()
            relay(o, j).start()
        for o, j in near:
            direct(o, j).wait_recv()
        for o, j in away:
            relay(o, j).wait_recv()
            relay(o, j).wait_send()
        for o, j in away + near:
            direct(o, j).wait_send()
        for copy in own:
            copy.wait()
    for i in range(blocks):
        if h:
            part(i).wait_recv()
            part(i).wait_send()
        else:
            part(i).wait()


def shift_columns(h, s, per, ident, child, *factors):
    R = lax.axis_size("row")
    T, tile = child.shape[0], child.shape[-1]
    blocks = T // per - s
    moved = jax.ShapeDtypeStruct((per * blocks, tile, tile), f32)
    remote_ids = bool(h) or bool(factors)
    params = (
        pltpu.CompilerParams(collective_id=ident, has_side_effects=True, vmem_limit_bytes=ROOM)
        if remote_ids
        else pltpu.CompilerParams(vmem_limit_bytes=ROOM)
    )
    shapes, scratch = [moved], [DMA((blocks,)), DMA((blocks,))]
    if factors:
        shapes += [jax.ShapeDtypeStruct((R,) + (f.shape[0],) + f.shape[2:], f32) for f in factors]
        scratch += [DMA((2,))] + [DMA((R // 2, 6))] * 4
    out = pl.pallas_call(
        lambda *refs: shift_kernel(h, s, per, *refs),
        in_specs=[ANY] * (1 + len(factors)),
        out_specs=[VMEM] * len(shapes),
        out_shape=shapes,
        scratch_shapes=scratch,
        compiler_params=params,
        name=f"shift_{s}_{h}",
    )(child, *factors)
    return tuple(out)


def product_kernel(per, S, bmap, everyone, out, mine_top, mine_low, their_top, their_low):
    R, T, rank, width = everyone.shape
    C = out.shape[0]
    spot = Layout(bmap, S)
    for t in range(T):
        top, low = split(everyone[spot.src_row(t // per), t])
        mine_top[t * rank : (t + 1) * rank, :] = top
        mine_low[t * rank : (t + 1) * rank, :] = low
    at = 0
    for s in range(S):
        for c in range(C):
            src = spot.src_col(s, c)
            top, low = split(everyone[lax.rem(src, R), s * per + lax.div(src, R)])
            their_top[c * rank : (c + 1) * rank, :] = top
            their_low[c * rank : (c + 1) * rank, :] = low
        first = s * per * rank
        size = T * rank - first
        mine = (mine_top[first:, :], mine_low[first:, :])
        got = dot3((their_top[...], their_low[...]), mine, ((1,), (1,)))
        out[:, :, at : at + size] = got.reshape(C, rank, size)
        at += size


def products(bmap, everyone, C, per):
    R, T, rank, width = everyone.shape
    S = T // per
    total = sum((S - s) * per * rank for s in range(S))
    return pl.pallas_call(
        lambda *refs: product_kernel(per, S, *refs),
        in_specs=[SMEM, VMEM],
        out_specs=VMEM,
        out_shape=jax.ShapeDtypeStruct((C, rank, total), f32),
        scratch_shapes=[pltpu.VMEM((T * rank, width), bf16)] * 2 + [pltpu.VMEM((C * rank, width), bf16)] * 2,
        compiler_params=pltpu.CompilerParams(vmem_limit_bytes=ROOM),
        name="products",
    )(bmap, everyone)


PARTS = 4


def sum_kernel(per, bmap, partial, *refs):
    S = len(refs) - 9
    moved = refs[:S]
    out, landed, slots, outbox, send, recv, row_send, row_recv, own_sem = refs[S:]
    R, n = lax.axis_size("row"), lax.axis_size("col")
    my_row, me = lax.axis_index("row"), lax.axis_index("col")
    chunk = partial.shape[1] // (2 * PARTS)
    pos = ring_spot(me, n)
    right = ring_place((pos + 1) % n, n)
    left = ring_place((pos + n - 1) % n, n)
    greet([{"col": left}, {"col": right}] + [{"row": (my_row + k) % R} for k in range(1, R)])
    rows = lambda side, h: pl.ds((PARTS * side + h) * chunk, chunk)

    def part(side, k, h):
        q = (pos - 1 - k + n) % n if side == 0 else (pos + 1 + k) % n
        return partial.at[ring_place(q, n), rows(side, h)]

    def hop(side, k, h):
        src = part(side, 0, h) if k == 0 else slots.at[side, k - 1, h]
        return remote(src, slots.at[side, k, h], send.at[side, k, h], recv.at[side, k, h],
                      {"col": right if side == 0 else left})

    def cross(k):
        return remote(outbox.at[k - 1], landed.at[k], row_send.at[k - 1], row_recv.at[k - 1], {"row": (my_row + k) % R})

    for h in range(PARTS):
        for side in range(2):
            hop(side, 0, h).start()

    spot = Layout(bmap, S)
    for k in [R // 2] + [k for k in range(R) if k != R // 2]:
        block = sum(u * (lax.rem(spot.shift(u), R) == k).astype(i32) for u in range(S))
        for s in range(S):
            place = jnp.clip(block - s, 0, S - 1 - s)
            for p in range(per):
                tile = moved[s][place * per + p]
                if k == 0:
                    landed[0, s, p] = tile
                else:
                    outbox[k - 1, s, p] = tile
        if k:
            cross(k).start()

    every = [(k, h, side) for k in range(n - 1) for h in range(PARTS) for side in range(2)]
    for k, h, side in every:
        if k > 0:
            hop(side, k - 1, h).wait_recv()
            slots[side, k - 1, h] = slots[side, k - 1, h] + part(side, k, h)[...]
            hop(side, k, h).start()
    for h in range(PARTS):
        for side in range(2):
            hop(side, n - 2, h).wait_recv()
            out[rows(side, h), :] = slots[side, n - 2, h] + partial[me, rows(side, h), :]
    for k in range(1, R):
        cross(k).wait_recv()
        cross(k).wait_send()
    for k, h, side in every:
        hop(side, k, h).wait_send()


def sum_and_rows(bmap, partial, moved, per):
    R = lax.axis_size("row")
    n, rank, total = partial.shape
    S, tile = len(moved), moved[0].shape[-1]
    box = (S, per, tile, tile)
    return pl.pallas_call(
        lambda *refs: sum_kernel(per, *refs),
        in_specs=[SMEM] + [VMEM] * (1 + S),
        out_specs=[VMEM] * 2,
        out_shape=[jax.ShapeDtypeStruct((rank, total), f32), jax.ShapeDtypeStruct((R,) + box, f32)],
        scratch_shapes=[
            pltpu.VMEM((2, n - 1, PARTS, rank // (2 * PARTS), total), f32),
            pltpu.VMEM((R - 1,) + box, f32),
            DMA((2, n - 1, PARTS)), DMA((2, n - 1, PARTS)), DMA((R - 1,)), DMA((R - 1,)), DMA,
        ],
        compiler_params=pltpu.CompilerParams(collective_id=1, has_side_effects=True, vmem_limit_bytes=ROOM),
        name="sum_and_rows",
    )(bmap, partial, *moved)


def update_kernel(per, C, bmap, start, ranks, weights, bases, landed, parent, out, held, sems):
    S, T, tile = out.shape[:3]
    R, _, rank, _ = bases.shape
    bcols = parent.shape[2]
    spot = Layout(bmap, S)
    b = own_column(start[0], spot.col, C, bcols)
    copies = []
    for i in range(held.shape[1]):
        for q in range(per):
            copies.append(pltpu.make_async_copy(parent.at[per * i + q, 0, b, 0], held.at[q, i], sems.at[q, i]))
            copies[-1].start()

    depth = lax.broadcasted_iota(i32, (rank, tile), 0)

    def basis(row, t):
        return split(jnp.where(depth < ranks[t * R + row], bases[row, t], 0.0))

    at = 0
    for s in range(S):
        size = (S - s) * per * rank
        src = spot.src_col(s)
        j = s * C + src
        col_basis = basis(lax.rem(src, R), s * per + lax.div(src, R))
        half = dot3(split(weights[:, at : at + size]), col_basis, ((0,), (0,)))
        at += size
        for t in range(s * per, T):
            u, p = t // per, t % per
            i = t - s * per
            row = spot.src_row(u)
            update = dot3(basis(row, t), split(half[i * rank : (i + 1) * rank]), ((0,), (0,)))
            moved = landed[lax.rem(spot.shift(u), R), s, p]
            out[s, t] = jnp.where(t * R + row >= j, moved - update, 0.0)

    s_own = lax.div(b, bcols // S)
    reached = spot.first_col(s_own) == b
    for copy in copies:
        copy.wait()

    @pl.when(reached)
    def _():
        for u in range(S):
            @pl.when(s_own <= u)
            def _():
                for p in range(per):
                    a = spot.first_row(u) + p
                    q, i = lax.rem(a, per), lax.div(a, per)
                    held[q, i] = held[q, i] + out[s_own, u * per + p]


def updates(bmap, start, ranks, weights, bases, landed, parent, C, per):
    R, T, rank, tile = bases.shape
    S, rows = T // per, parent.shape[0]
    return pl.pallas_call(
        lambda *refs: update_kernel(per, C, *refs),
        in_specs=[SMEM, SMEM, SMEM, VMEM, VMEM, VMEM, HBM],
        out_specs=[VMEM, VMEM],
        out_shape=[
            jax.ShapeDtypeStruct((S, T, tile, tile), f32),
            jax.ShapeDtypeStruct((per, rows // per, tile, tile), f32),
        ],
        scratch_shapes=[DMA((per, rows // per))],
        compiler_params=pltpu.CompilerParams(vmem_limit_bytes=ROOM),
        name="updates",
    )(bmap, start, ranks, weights, bases, landed, parent)


def panel_kernel(first, b0, held, panel, cols, recv, up, down, across, other, own_sem, self_sem, cross_send, cross_recv,
                 relay_send):
    R, n = lax.axis_size("row"), lax.axis_size("col")
    my_row, me = lax.axis_index("row"), lax.axis_index("col")
    Bn = held.shape[1]
    z, x, ends = me // 2, me % 2, n // 2 - 1
    side = me + 1 - 2 * x
    root, parity = me % R, me // R
    is_root = my_row == root
    partner = my_row + 1 - 2 * (my_row % 2)
    near = my_row // 2 == root // 2
    owner = lambda k: (first + k) % n

    def hops(k, lane):
        zk, xk = owner(k) // 2, owner(k) % 2
        return jnp.maximum(z - zk, zk - z) + (lane + xk) % 2

    barrier = pltpu.get_barrier_semaphore()
    for k in range(1, R):
        pl.semaphore_signal(barrier, inc=1, device_id={"row": (my_row + k) % R}, device_id_type=MESH)
    pl.semaphore_signal(barrier, inc=1, device_id={"col": side}, device_id_type=MESH)

    @pl.when(z > 0)
    def _():
        pl.semaphore_signal(barrier, inc=1, device_id={"col": me - 2}, device_id_type=MESH)

    @pl.when(z < ends)
    def _():
        pl.semaphore_signal(barrier, inc=1, device_id={"col": me + 2}, device_id_type=MESH)

    for k in range(PANEL_T):
        @pl.when(me == owner(k))
        def _():
            pltpu.make_async_copy(held, panel.at[k], own_sem).start()

    pl.semaphore_wait(barrier, R + jnp.minimum(z, 1) + jnp.minimum(ends - z, 1))

    for k in range(PANEL_T):
        @pl.when(me == owner(k))
        def _():
            pltpu.make_async_copy(held, panel.at[k], own_sem).wait()

    def hop(k, h, i, sem, to):
        ref = panel.at[k, h, i]
        return remote(ref, ref, sem.at[k, i], recv.at[k, h, i], {"col": to})

    def sends(k, i, act):
        zk, xk = owner(k) // 2, owner(k) % 2

        @pl.when(me == owner(k))
        def _():
            act(hop(k, 1 - x, i, other, side))

        @pl.when((z >= zk) & (z < ends))
        def _():
            act(hop(k, x, i, up, me + 2))

        @pl.when((z <= zk) & (z > 0))
        def _():
            act(hop(k, x, i, down, me - 2))

        @pl.when((z != zk) | (x == xk))
        def _():
            act(hop(k, x, i, across, side))

    def main(k, i):
        @pl.when(me != owner(k))
        def _():
            hop(k, x, i, up, side).wait_recv()

        sends(k, i, lambda copy: copy.start())

    def cross(k, i, o):
        to = partner if o == 0 else (my_row // 2 + o) % (R // 2) * 2 + (my_row + k) % 2
        return remote(panel.at[k, parity, i], cols.at[k, i], cross_send.at[k, i, o], cross_recv.at[k, i], {"row": to})

    def mine(k, i):
        return pltpu.make_async_copy(panel.at[k, parity, i], cols.at[k, i], self_sem.at[k, i])

    def late(k, i):
        @pl.when(me != owner(k))
        def _():
            hop(k, 1 - x, i, up, side).wait_recv()

        @pl.when(is_root)
        def _():
            for o in range(1, R // 2):
                cross(k, i, o).start()
            cross(k, i, 0).start()
            mine(k, i).start()

    def relay(k, i):
        return remote(cols.at[k, i], cols.at[k, i], relay_send.at[k, i], cross_recv.at[k, i], {"row": partner})

    def direct(k):
        return ~near & ((my_row + root + k) % 2 == 0)

    def pass_on(k, i):
        @pl.when(direct(k))
        def _():
            relay(k, i).wait_recv()
            relay(k, i).start()

    def body(t, _):
        j, k = t // PANEL_T, t % PANEL_T

        def turn(lag, act):
            i = b0 + (j - lag + 2 * n) // 2 - n

            @pl.when(((j + lag) % 2 == 0) & (i >= b0) & (i < Bn))
            def _():
                act(k, i)

        there = hops(k, 1 - x)
        turn(hops(k, x), main)
        turn(there + 2, late)
        turn(there + 4, pass_on)
        return 0

    lax.fori_loop(0, (2 * (Bn - b0) + ends + 5) * PANEL_T, body, 0)

    def drain(t, _):
        i, k = b0 + t // PANEL_T, t % PANEL_T
        sends(k, i, lambda copy: copy.wait_send())

        @pl.when(is_root)
        def _():
            for o in range(R // 2):
                cross(k, i, o).wait_send()
            mine(k, i).wait()

        @pl.when(direct(k))
        def _():
            relay(k, i).wait_send()

        @pl.when(~direct(k) & ~is_root)
        def _():
            relay(k, i).wait_recv()

        return 0

    lax.fori_loop(0, (Bn - b0) * PANEL_T, drain, 0)


def gather_panel(first, b0, ident, held):
    R = lax.axis_size("row")
    per, Bn, tile, _ = held.shape
    each = (PANEL_T, Bn)
    return tuple(pl.pallas_call(
        lambda *refs: panel_kernel(first, b0, *refs),
        in_specs=[VMEM],
        out_specs=[VMEM, VMEM],
        out_shape=[
            jax.ShapeDtypeStruct((PANEL_T,) + held.shape, f32),
            jax.ShapeDtypeStruct(each + (tile, tile), f32),
        ],
        scratch_shapes=[DMA((PANEL_T, per, Bn))] + [DMA(each)] * 4 + [DMA, DMA(each), DMA(each + (R // 2,)), DMA(each), DMA(each)],
        compiler_params=pltpu.CompilerParams(collective_id=ident, has_side_effects=True, vmem_limit_bytes=ROOM),
        name=f"panel_{first}_{b0}",
    )(held))


def final_kernel(bmap, start, parent, payload, panel, cols, inverse, out, inv_top, inv_low, col_top, col_low, high, low):
    step = pl.program_id(0)
    per, bcols = parent.shape[0], parent.shape[2]
    tile = parent.shape[4]
    S = payload.shape[0]
    group = bcols // S
    spot = Layout(bmap, S)
    R, C = spot.R, spot.C
    first_active = start[0] + PANEL_T

    @pl.when(step == 0)
    def _():
        top, rest = split(inverse[...])
        inv_top[...] = top
        inv_low[...] = rest
        for b in range(bcols):
            for k in range(PANEL_T):
                top, rest = split(cols[k, b])
                col_top[b * tile : (b + 1) * tile, k * tile : (k + 1) * tile] = top
                col_low[b * tile : (b + 1) * tile, k * tile : (k + 1) * tile] = rest

    u = lax.div(step, 2)
    first = spot.first_row(u)
    places = [step * per + p - first for p in range(per)]
    hits = [(d >= 0) & (d < per) for d in places]
    big_rows = [spot.row + (step * per + p) * R for p in range(per)]
    big_cols = [spot.col + b * C for b in range(bcols)]

    for b in range(bcols):
        s = b // group
        reached = (spot.first_col(s) == b) & (s <= u)
        for p in range(per):
            out[p, 0, b, 0] = parent[p, 0, b, 0]

            @pl.when(hits[p] & reached)
            def _():
                out[p, 0, b, 0] = parent[p, 0, b, 0] + payload[s, u * per + places[p]]

    @pl.when(big_rows[-1] >= first_active)
    def _():
        stacked = [jnp.concatenate([panel[k, p, step] for k in range(PANEL_T)], axis=1) for p in range(per)]
        scaled = dot3(split(jnp.concatenate(stacked, axis=0)), (inv_top[...], inv_low[...]), ((1,), (0,)))
        top, rest = split(scaled)
        high[...] = top
        low[...] = rest
        for g in range(S):
            @pl.when((big_rows[-1] >= big_cols[g * group]) & (big_cols[g * group + group - 1] >= first_active))
            def _():
                at = pl.ds(g * group * tile, group * tile)
                trailing = dot3((high[...], low[...]), (col_top[at, :], col_low[at, :]), ((1,), (1,)))
                for j in range(group):
                    b = g * group + j
                    for p in range(per):
                        active = (big_rows[p] >= big_cols[b]) & (big_cols[b] >= first_active)
                        part = trailing[p * tile : (p + 1) * tile, j * tile : (j + 1) * tile]
                        out[p, 0, b, 0] = out[p, 0, b, 0] - jnp.where(active, part, 0.0)


def finish(bmap, start, parent, payload, panel, cols, inverse, per):
    rows, _, bcols, _, tile, _ = parent.shape
    wide = PANEL_T * tile
    whole = lambda a: pl.BlockSpec(a.shape, lambda i, m, t: (0,) * a.ndim, pipeline_mode=pl.Buffered(1))
    big = pl.BlockSpec((per, 1, bcols, 1, tile, tile), lambda i, m, t: (i, 0, 0, 0, 0, 0))
    flops = 6 * rows * tile * wide * (wide + bcols * tile)
    return pl.pallas_call(
        final_kernel,
        grid_spec=pltpu.PrefetchScalarGridSpec(
            num_scalar_prefetch=2,
            grid=(rows // per,),
            in_specs=[big, whole(payload), whole(panel), whole(cols), whole(inverse)],
            out_specs=big,
            scratch_shapes=[pltpu.VMEM((wide, wide), bf16)] * 2 + [pltpu.VMEM((bcols * tile, wide), bf16)] * 2
            + [pltpu.VMEM((per * tile, wide), bf16)] * 2,
        ),
        out_shape=jax.ShapeDtypeStruct(parent.shape, f32),
        compiler_params=pltpu.CompilerParams(vmem_limit_bytes=ROOM),
        cost_estimate=pl.CostEstimate(flops=flops, bytes_accessed=10 * parent.size, transcendentals=0),
        name="finish",
    )(bmap, start, parent, payload, panel, cols, inverse)


def per_device(contribution, parent, row_basis, pivot_basis, ranks, block_map, panel_start, inverse):
    R, C = lax.axis_size("row"), lax.axis_size("col")
    S = contribution.shape[2]
    per = C // R
    shift = [block_map[u * C] - 2 * C * u for u in range(S)]

    ident = 2
    moved = []
    for s in range(S):
        branches = []
        for h in range(C):
            branches.append(lambda *a, h=h, s=s, ident=ident: shift_columns(h, s, per, ident, *a))
            ident += 1
        if s == 0:
            first, all_piv, all_bas = lax.switch(shift[0], branches, contribution, pivot_basis, row_basis)
            moved.append(first)
        else:
            moved.append(lax.switch(shift[s], branches, contribution)[0])

    partial = products(block_map, all_piv, C, per)
    weights, landed = sum_and_rows(block_map, partial, moved, per)
    parent = pltpu.with_memory_space_constraint(parent, pltpu.HBM)
    payload, held = updates(block_map, panel_start, ranks, weights, all_bas, landed, parent, C, per)

    branches = []
    pairs = parent.shape[0] // (2 * per)
    for first in range(C):
        for b0 in range(0, pairs, 2):
            b0 += (first + PANEL_T) // C
            branches.append(lambda v, first=first, b0=b0, ident=ident: gather_panel(first, b0, ident, v))
            ident += 1
    start = panel_start[0]
    which = lax.rem(start, C) * (pairs // 2) + jnp.minimum(lax.div(start, 2 * C), pairs // 2 - 1)
    panel, cols = lax.switch(which, branches, held)
    return finish(block_map, panel_start, parent, payload, panel, cols, inverse, per)


def solution(mesh):
    placed = (
        P(None, "row", None, "col", None, None),
        P(None, "row", None, "col", None, None),
        P(None, "row", None, None),
        P(None, "row", None, "col"),
        P(),
        P(),
        P(),
        P(),
    )
    return jax.shard_map(
        per_device,
        mesh=mesh,
        in_specs=placed,
        out_specs=P(None, "row", None, "col", None, None),
        check_vma=False,
    )
```

```python
import jax
import jax.numpy as jnp
from jax import lax
from jax.experimental import pallas as pl
from jax.experimental.pallas import tpu as pltpu
from jax.sharding import PartitionSpec as P

PANEL_T = 4
f32 = jnp.float32
bf16 = jnp.bfloat16
i32 = jnp.int32
MESH = pl.DeviceIdType.MESH
DMA = pltpu.SemaphoreType.DMA
SMEM = pl.BlockSpec(memory_space=pltpu.SMEM)
VMEM = pl.BlockSpec(memory_space=pltpu.VMEM)
ANY = pl.BlockSpec(memory_space=pl.ANY)
HBM = pl.BlockSpec(memory_space=pltpu.HBM)
ROOM = 32 << 20


def split(x):
    top = x.astype(bf16)
    return top, (x - top.astype(f32)).astype(bf16)


def dot3(a, b, dims):
    (ah, al), (bh, bl) = a, b
    one = lambda p, q: lax.dot_general(p, q, (dims, ((), ())), preferred_element_type=f32)
    return one(ah, bh) + (one(ah, bl) + one(al, bh))


def ring_place(p, n):
    return jnp.where(p < n // 2, 2 * p, 2 * (n - 1 - p) + 1)


def ring_spot(me, n):
    return jnp.where(me % 2 == 0, me // 2, n - 1 - me // 2)


def greet(targets):
    barrier = pltpu.get_barrier_semaphore()
    for target in targets:
        pl.semaphore_signal(barrier, inc=1, device_id=target, device_id_type=MESH)
    pl.semaphore_wait(barrier, len(targets))


def remote(src, dst, send, recv, to):
    return pltpu.make_async_remote_copy(src, dst, send, recv, device_id=to, device_id_type=MESH)


class Layout:
    def __init__(self, bmap, blocks):
        self.map = bmap
        self.S = blocks
        self.R, self.C = lax.axis_size("row"), lax.axis_size("col")
        self.row, self.col = lax.axis_index("row"), lax.axis_index("col")

    def shift(self, u):
        return self.map[u * self.C] - 2 * self.C * u

    def src_row(self, u, row=None):
        row = self.row if row is None else row
        return lax.rem(row + self.C * self.R - self.shift(u), self.R)

    def src_col(self, s, col=None):
        col = self.col if col is None else col
        return lax.rem(col + self.C - self.shift(s), self.C)

    def first_row(self, u, row=None):
        return lax.div(2 * self.C * u + self.shift(u) + self.src_row(u, row), self.R)

    def first_col(self, s):
        return lax.div(2 * self.C * s + self.shift(s) + self.src_col(s), self.C)


def own_column(start, col, C, bcols):
    k = lax.rem(col - start + C * bcols, C)
    return jnp.minimum(lax.div(start + k, C), bcols - 1)


def shift_kernel(h, s, per, *refs):
    R, n = lax.axis_size("row"), lax.axis_size("col")
    me, my_col = lax.axis_index("row"), lax.axis_index("col")
    gather = s == 0
    if gather:
        child, piv, bas, moved, all_piv, all_bas, send, recv, own_sem, d_send, d_recv, r_send, r_recv = refs
    else:
        child, moved, send, recv = refs
    blocks = moved.shape[0] // per
    pairs = R // 2
    other = me + 1 - 2 * (me % 2)

    signals = []
    if h:
        signals.append({"col": (my_col + n - h) % n})
    if gather:
        signals += [{"row": (me + k) % R} for k in range(1, R)]
    if signals:
        greet(signals)

    def part(i):
        src = child.at[pl.ds(per * (s + i), per), 0, s, 0]
        dst = moved.at[pl.ds(per * i, per)]
        if h:
            return remote(src, dst, send.at[i], recv.at[i], {"col": (my_col + h) % n})
        return pltpu.make_async_copy(src, dst, recv.at[i])

    if gather:
        T = piv.shape[0]
        cuts = [(piv, all_piv, j * T // 4, T // 4) for j in range(4)]
        cuts += [(bas, all_bas, j * T // 2, T // 2) for j in range(2)]

        def direct(o, j):
            src, dst, a, size = cuts[j]
            to = other if o == 0 else (me // 2 + o) % pairs * 2 + me % 2
            return remote(src.at[pl.ds(a, size), 0], dst.at[me, pl.ds(a, size)], d_send.at[o, j], d_recv.at[o, j],
                          {"row": to})

        def relay(o, j):
            _, dst, a, size = cuts[j]
            d = (me // 2 - o + pairs) % pairs * 2 + me % 2
            return remote(dst.at[d, pl.ds(a, size)], dst.at[d, pl.ds(a, size)], r_send.at[o, j], r_recv.at[o, j],
                          {"row": other})

        away = [(o, j) for j in range(len(cuts)) for o in range(1, pairs)]
        near = [(0, j) for j in range(len(cuts))]
        for o, j in away:
            direct(o, j).start()
    for i in range(blocks):
        part(i).start()
    if gather:
        own = [pltpu.make_async_copy(src.at[:, 0], dst.at[me], own_sem.at[j])
               for j, (src, dst) in enumerate(((piv, all_piv), (bas, all_bas)))]
        for copy in own:
            copy.start()
        for o, j in near:
            direct(o, j).start()
        for o, j in away:
            direct(o, j).wait_recv()
            relay(o, j).start()
        for o, j in near:
            direct(o, j).wait_recv()
        for o, j in away:
            relay(o, j).wait_recv()
            relay(o, j).wait_send()
        for o, j in away + near:
            direct(o, j).wait_send()
        for copy in own:
            copy.wait()
    for i in range(blocks):
        if h:
            part(i).wait_recv()
            part(i).wait_send()
        else:
            part(i).wait()


def shift_columns(h, s, per, ident, child, *factors):
    R = lax.axis_size("row")
    T, tile = child.shape[0], child.shape[-1]
    blocks = T // per - s
    moved = jax.ShapeDtypeStruct((per * blocks, tile, tile), f32)
    remote_ids = bool(h) or bool(factors)
    params = (
        pltpu.CompilerParams(collective_id=ident, has_side_effects=True, vmem_limit_bytes=ROOM)
        if remote_ids
        else pltpu.CompilerParams(vmem_limit_bytes=ROOM)
    )
    shapes, scratch = [moved], [DMA((blocks,)), DMA((blocks,))]
    if factors:
        shapes += [jax.ShapeDtypeStruct((R,) + (f.shape[0],) + f.shape[2:], f32) for f in factors]
        scratch += [DMA((2,))] + [DMA((R // 2, 6))] * 4
    out = pl.pallas_call(
        lambda *refs: shift_kernel(h, s, per, *refs),
        in_specs=[ANY] * (1 + len(factors)),
        out_specs=[VMEM] * len(shapes),
        out_shape=shapes,
        scratch_shapes=scratch,
        compiler_params=params,
        name=f"shift_{s}_{h}",
    )(child, *factors)
    return tuple(out)


def product_kernel(per, S, bmap, everyone, out, mine_top, mine_low, their_top, their_low):
    R, T, rank, width = everyone.shape
    C = out.shape[0]
    spot = Layout(bmap, S)
    for t in range(T):
        top, low = split(everyone[spot.src_row(t // per), t])
        mine_top[t * rank : (t + 1) * rank, :] = top
        mine_low[t * rank : (t + 1) * rank, :] = low
    at = 0
    for s in range(S):
        for c in range(C):
            src = spot.src_col(s, c)
            top, low = split(everyone[lax.rem(src, R), s * per + lax.div(src, R)])
            their_top[c * rank : (c + 1) * rank, :] = top
            their_low[c * rank : (c + 1) * rank, :] = low
        first = s * per * rank
        size = T * rank - first
        mine = (mine_top[first:, :], mine_low[first:, :])
        got = dot3((their_top[...], their_low[...]), mine, ((1,), (1,)))
        out[:, :, at : at + size] = got.reshape(C, rank, size)
        at += size


def products(bmap, everyone, C, per):
    R, T, rank, width = everyone.shape
    S = T // per
    total = sum((S - s) * per * rank for s in range(S))
    return pl.pallas_call(
        lambda *refs: product_kernel(per, S, *refs),
        in_specs=[SMEM, VMEM],
        out_specs=VMEM,
        out_shape=jax.ShapeDtypeStruct((C, rank, total), f32),
        scratch_shapes=[pltpu.VMEM((T * rank, width), bf16)] * 2 + [pltpu.VMEM((C * rank, width), bf16)] * 2,
        compiler_params=pltpu.CompilerParams(vmem_limit_bytes=ROOM),
        name="products",
    )(bmap, everyone)


PARTS = 4


def sum_kernel(per, bmap, partial, inverse, *refs):
    S = len(refs) - 11
    moved = refs[:S]
    out, landed, inv_top, inv_low, slots, outbox, send, recv, row_send, row_recv, own_sem = refs[S:]
    R, n = lax.axis_size("row"), lax.axis_size("col")
    my_row, me = lax.axis_index("row"), lax.axis_index("col")
    chunk = partial.shape[1] // (2 * PARTS)
    pos = ring_spot(me, n)
    right = ring_place((pos + 1) % n, n)
    left = ring_place((pos + n - 1) % n, n)
    greet([{"col": left}, {"col": right}] + [{"row": (my_row + k) % R} for k in range(1, R)])
    rows = lambda side, h: pl.ds((PARTS * side + h) * chunk, chunk)

    def part(side, k, h):
        q = (pos - 1 - k + n) % n if side == 0 else (pos + 1 + k) % n
        return partial.at[ring_place(q, n), rows(side, h)]

    def hop(side, k, h):
        src = part(side, 0, h) if k == 0 else slots.at[side, k - 1, h]
        return remote(src, slots.at[side, k, h], send.at[side, k, h], recv.at[side, k, h],
                      {"col": right if side == 0 else left})

    def cross(k):
        return remote(outbox.at[k - 1], landed.at[k], row_send.at[k - 1], row_recv.at[k - 1], {"row": (my_row + k) % R})

    for h in range(PARTS):
        for side in range(2):
            hop(side, 0, h).start()

    spot = Layout(bmap, S)
    for k in [R // 2] + [k for k in range(R) if k != R // 2]:
        block = sum(u * (lax.rem(spot.shift(u), R) == k).astype(i32) for u in range(S))
        for s in range(S):
            place = jnp.clip(block - s, 0, S - 1 - s)
            for p in range(per):
                tile = moved[s][place * per + p]
                if k == 0:
                    landed[0, s, p] = tile
                else:
                    outbox[k - 1, s, p] = tile
        if k:
            cross(k).start()

    top, rest = split(inverse[...])
    inv_top[...] = top
    inv_low[...] = rest

    every = [(k, h, side) for k in range(n - 1) for h in range(PARTS) for side in range(2)]
    for k, h, side in every:
        if k > 0:
            hop(side, k - 1, h).wait_recv()
            slots[side, k - 1, h] = slots[side, k - 1, h] + part(side, k, h)[...]
            hop(side, k, h).start()
    for h in range(PARTS):
        for side in range(2):
            hop(side, n - 2, h).wait_recv()
            out[rows(side, h), :] = slots[side, n - 2, h] + partial[me, rows(side, h), :]
    for k in range(1, R):
        cross(k).wait_recv()
        cross(k).wait_send()
    for k, h, side in every:
        hop(side, k, h).wait_send()


def sum_and_rows(bmap, partial, inverse, moved, per):
    R = lax.axis_size("row")
    n, rank, total = partial.shape
    S, tile = len(moved), moved[0].shape[-1]
    box = (S, per, tile, tile)
    return pl.pallas_call(
        lambda *refs: sum_kernel(per, *refs),
        in_specs=[SMEM] + [VMEM] * (2 + S),
        out_specs=[VMEM] * 4,
        out_shape=[jax.ShapeDtypeStruct((rank, total), f32), jax.ShapeDtypeStruct((R,) + box, f32)]
        + [jax.ShapeDtypeStruct(inverse.shape, bf16)] * 2,
        scratch_shapes=[
            pltpu.VMEM((2, n - 1, PARTS, rank // (2 * PARTS), total), f32),
            pltpu.VMEM((R - 1,) + box, f32),
            DMA((2, n - 1, PARTS)), DMA((2, n - 1, PARTS)), DMA((R - 1,)), DMA((R - 1,)), DMA,
        ],
        compiler_params=pltpu.CompilerParams(collective_id=1, has_side_effects=True, vmem_limit_bytes=ROOM),
        name="sum_and_rows",
    )(bmap, partial, inverse, *moved)


def update_kernel(per, C, bmap, start, ranks, weights, bases, landed, parent, out, held, sems):
    S, T, tile = out.shape[:3]
    R, _, rank, _ = bases.shape
    bcols = parent.shape[2]
    spot = Layout(bmap, S)
    b = own_column(start[0], spot.col, C, bcols)
    copies = []
    for i in range(held.shape[1]):
        for q in range(per):
            copies.append(pltpu.make_async_copy(parent.at[per * i + q, 0, b, 0], held.at[q, i], sems.at[q, i]))
            copies[-1].start()

    depth = lax.broadcasted_iota(i32, (rank, tile), 0)

    def basis(row, t):
        return split(jnp.where(depth < ranks[t * R + row], bases[row, t], 0.0))

    at = 0
    for s in range(S):
        size = (S - s) * per * rank
        src = spot.src_col(s)
        j = s * C + src
        col_basis = basis(lax.rem(src, R), s * per + lax.div(src, R))
        half = dot3(split(weights[:, at : at + size]), col_basis, ((0,), (0,)))
        at += size
        for t in range(s * per, T):
            u, p = t // per, t % per
            i = t - s * per
            row = spot.src_row(u)
            update = dot3(basis(row, t), split(half[i * rank : (i + 1) * rank]), ((0,), (0,)))
            moved = landed[lax.rem(spot.shift(u), R), s, p]
            out[s, t] = jnp.where(t * R + row >= j, moved - update, 0.0)

    s_own = lax.div(b, bcols // S)
    reached = spot.first_col(s_own) == b
    for copy in copies:
        copy.wait()

    @pl.when(reached)
    def _():
        for u in range(S):
            @pl.when(s_own <= u)
            def _():
                for p in range(per):
                    a = spot.first_row(u) + p
                    q, i = lax.rem(a, per), lax.div(a, per)
                    held[q, i] = held[q, i] + out[s_own, u * per + p]


def updates(bmap, start, ranks, weights, bases, landed, parent, C, per):
    R, T, rank, tile = bases.shape
    S, rows = T // per, parent.shape[0]
    return pl.pallas_call(
        lambda *refs: update_kernel(per, C, *refs),
        in_specs=[SMEM, SMEM, SMEM, VMEM, VMEM, VMEM, HBM],
        out_specs=[VMEM, VMEM],
        out_shape=[
            jax.ShapeDtypeStruct((S, T, tile, tile), f32),
            jax.ShapeDtypeStruct((per, rows // per, tile, tile), f32),
        ],
        scratch_shapes=[DMA((per, rows // per))],
        compiler_params=pltpu.CompilerParams(vmem_limit_bytes=ROOM),
        name="updates",
    )(bmap, start, ranks, weights, bases, landed, parent)


def panel_kernel(first, b0, held, inv_top, inv_low, row_top, row_low, col_top, col_low, panel, cols, recv, up, down, across,
                 other, own_sem, cross_send, cross_recv, relay_send):
    R, n = lax.axis_size("row"), lax.axis_size("col")
    my_row, me = lax.axis_index("row"), lax.axis_index("col")
    Bn = held.shape[1]
    z, x, ends = me // 2, me % 2, n // 2 - 1
    side = me + 1 - 2 * x
    root, parity = me % R, me // R
    is_root = my_row == root
    partner = my_row + 1 - 2 * (my_row % 2)
    near = my_row // 2 == root // 2
    owner = lambda k: (first + k) % n

    def hops(k, lane):
        zk, xk = owner(k) // 2, owner(k) % 2
        return jnp.maximum(z - zk, zk - z) + (lane + xk) % 2

    barrier = pltpu.get_barrier_semaphore()
    for k in range(1, R):
        pl.semaphore_signal(barrier, inc=1, device_id={"row": (my_row + k) % R}, device_id_type=MESH)
    pl.semaphore_signal(barrier, inc=1, device_id={"col": side}, device_id_type=MESH)

    @pl.when(z > 0)
    def _():
        pl.semaphore_signal(barrier, inc=1, device_id={"col": me - 2}, device_id_type=MESH)

    @pl.when(z < ends)
    def _():
        pl.semaphore_signal(barrier, inc=1, device_id={"col": me + 2}, device_id_type=MESH)

    for k in range(PANEL_T):
        @pl.when(me == owner(k))
        def _():
            pltpu.make_async_copy(held, panel.at[k], own_sem).start()

    pl.semaphore_wait(barrier, R + jnp.minimum(z, 1) + jnp.minimum(ends - z, 1))

    for k in range(PANEL_T):
        @pl.when(me == owner(k))
        def _():
            pltpu.make_async_copy(held, panel.at[k], own_sem).wait()

    def hop(k, h, i, sem, to):
        ref = panel.at[k, h, i]
        return remote(ref, ref, sem.at[k, i], recv.at[k, h, i], {"col": to})

    def sends(k, i, act):
        zk, xk = owner(k) // 2, owner(k) % 2

        @pl.when(me == owner(k))
        def _():
            act(hop(k, 1 - x, i, other, side))

        @pl.when((z >= zk) & (z < ends))
        def _():
            act(hop(k, x, i, up, me + 2))

        @pl.when((z <= zk) & (z > 0))
        def _():
            act(hop(k, x, i, down, me - 2))

        @pl.when((z != zk) | (x == xk))
        def _():
            act(hop(k, x, i, across, side))

    def main(k, i):
        @pl.when(me != owner(k))
        def _():
            hop(k, x, i, up, side).wait_recv()

        sends(k, i, lambda copy: copy.start())

    def cross(k, i, o):
        to = partner if o == 0 else (my_row // 2 + o) % (R // 2) * 2 + (my_row + k) % 2
        return remote(panel.at[k, parity, i], cols.at[k, i], cross_send.at[k, i, o], cross_recv.at[k, i], {"row": to})

    def late(k, i):
        @pl.when(me != owner(k))
        def _():
            hop(k, 1 - x, i, up, side).wait_recv()

        @pl.when(is_root)
        def _():
            for o in range(1, R // 2):
                cross(k, i, o).start()
            cross(k, i, 0).start()

    def relay(k, i):
        return remote(cols.at[k, i], cols.at[k, i], relay_send.at[k, i], cross_recv.at[k, i], {"row": partner})

    def direct(k):
        return ~near & ((my_row + root + k) % 2 == 0)

    def pass_on(k, i):
        @pl.when(direct(k))
        def _():
            relay(k, i).wait_recv()
            relay(k, i).start()

    tile = held.shape[-1]

    def settle(k, i):
        @pl.when(~direct(k) & ~is_root)
        def _():
            relay(k, i).wait_recv()

        at = pl.ds(pl.multiple_of(k * tile, tile), tile)
        top, rest = split(jnp.where(is_root, panel[k, parity, i], cols[k, i]))
        col_top[i, :, at] = top
        col_low[i, :, at] = rest

    def scale(i):
        rows = [jnp.concatenate([panel[k, q, i] for k in range(PANEL_T)], axis=1) for q in range(held.shape[0])]
        scaled = dot3(split(jnp.concatenate(rows, axis=0)), (inv_top[...], inv_low[...]), ((1,), (0,)))
        top, rest = split(scaled)
        row_top[i] = top
        row_low[i] = rest

    full = ends + 2

    def body(t, _):
        j, k = t // PANEL_T, t % PANEL_T

        def turn(lag, act, also=True):
            i = b0 + (j - lag + 2 * n) // 2 - n

            @pl.when(((j + lag) % 2 == 0) & (i >= b0) & (i < Bn) & also)
            def _():
                act(i)

        there = hops(k, 1 - x)
        turn(hops(k, x), lambda i: main(k, i))
        turn(there + 1, lambda i: late(k, i))
        turn(there + 2, lambda i: pass_on(k, i))
        turn(there + 3, lambda i: settle(k, i))
        turn(full, scale, k == PANEL_T - 1)
        return 0

    lax.fori_loop(0, (2 * (Bn - b0) + ends + 3) * PANEL_T, body, 0)

    def drain(t, _):
        i, k = b0 + t // PANEL_T, t % PANEL_T
        sends(k, i, lambda copy: copy.wait_send())

        @pl.when(is_root)
        def _():
            for o in range(R // 2):
                cross(k, i, o).wait_send()

        @pl.when(direct(k))
        def _():
            relay(k, i).wait_send()

        return 0

    lax.fori_loop(0, (Bn - b0) * PANEL_T, drain, 0)


def gather_panel(first, b0, ident, held, *inverse):
    R = lax.axis_size("row")
    per, Bn, tile, _ = held.shape
    each = (PANEL_T, Bn)
    wide = PANEL_T * tile
    return tuple(pl.pallas_call(
        lambda *refs: panel_kernel(first, b0, *refs),
        in_specs=[VMEM] * 3,
        out_specs=[VMEM] * 4,
        out_shape=[jax.ShapeDtypeStruct((Bn, per * tile, wide), bf16)] * 2
        + [jax.ShapeDtypeStruct((Bn, tile, wide), bf16)] * 2,
        scratch_shapes=[pltpu.VMEM((PANEL_T,) + held.shape, f32), pltpu.VMEM(each + (tile, tile), f32)]
        + [DMA((PANEL_T, per, Bn))] + [DMA(each)] * 4 + [DMA, DMA(each + (R // 2,)), DMA(each), DMA(each)],
        compiler_params=pltpu.CompilerParams(collective_id=ident, has_side_effects=True, vmem_limit_bytes=ROOM),
        name=f"panel_{first}_{b0}",
    )(held, *inverse))


def final_kernel(bmap, start, parent, payload, row_top, row_low, col_top, col_low, out):
    step = pl.program_id(0)
    per, bcols = parent.shape[0], parent.shape[2]
    tile = parent.shape[4]
    S = payload.shape[0]
    group = bcols // S
    spot = Layout(bmap, S)
    R, C = spot.R, spot.C
    first_active = start[0] + PANEL_T

    u = lax.div(step, 2)
    first = spot.first_row(u)
    places = [step * per + p - first for p in range(per)]
    hits = [(d >= 0) & (d < per) for d in places]
    big_rows = [spot.row + (step * per + p) * R for p in range(per)]
    big_cols = [spot.col + b * C for b in range(bcols)]

    for b in range(bcols):
        s = b // group
        reached = (spot.first_col(s) == b) & (s <= u)
        for p in range(per):
            out[p, 0, b, 0] = parent[p, 0, b, 0]

            @pl.when(hits[p] & reached)
            def _():
                out[p, 0, b, 0] = parent[p, 0, b, 0] + payload[s, u * per + places[p]]

    for g in range(S):
        @pl.when((big_rows[-1] >= big_cols[g * group]) & (big_cols[g * group + group - 1] >= first_active))
        def _():
            pair = lambda ref: ref[g * group : (g + 1) * group].reshape(group * tile, -1)
            trailing = dot3((row_top[step], row_low[step]), (pair(col_top), pair(col_low)), ((1,), (1,)))
            for j in range(group):
                b = g * group + j
                for p in range(per):
                    active = (big_rows[p] >= big_cols[b]) & (big_cols[b] >= first_active)
                    part = trailing[p * tile : (p + 1) * tile, j * tile : (j + 1) * tile]
                    out[p, 0, b, 0] = out[p, 0, b, 0] - jnp.where(active, part, 0.0)


def finish(bmap, start, parent, payload, factors, per):
    rows, _, bcols, _, tile, _ = parent.shape
    whole = lambda a: pl.BlockSpec(a.shape, lambda i, m, t: (0,) * a.ndim, pipeline_mode=pl.Buffered(1))
    big = pl.BlockSpec((per, 1, bcols, 1, tile, tile), lambda i, m, t: (i, 0, 0, 0, 0, 0))
    flops = 6 * rows * tile * PANEL_T * tile * bcols * tile
    return pl.pallas_call(
        final_kernel,
        grid_spec=pltpu.PrefetchScalarGridSpec(
            num_scalar_prefetch=2,
            grid=(rows // per,),
            in_specs=[big, whole(payload)] + [whole(f) for f in factors],
            out_specs=big,
        ),
        out_shape=jax.ShapeDtypeStruct(parent.shape, f32),
        compiler_params=pltpu.CompilerParams(vmem_limit_bytes=ROOM),
        cost_estimate=pl.CostEstimate(flops=flops, bytes_accessed=10 * parent.size, transcendentals=0),
        name="finish",
    )(bmap, start, parent, payload, *factors)


def per_device(contribution, parent, row_basis, pivot_basis, ranks, block_map, panel_start, inverse):
    R, C = lax.axis_size("row"), lax.axis_size("col")
    S = contribution.shape[2]
    per = C // R
    shift = [block_map[u * C] - 2 * C * u for u in range(S)]

    ident = 2
    moved = []
    for s in range(S):
        branches = []
        for h in range(C):
            branches.append(lambda *a, h=h, s=s, ident=ident: shift_columns(h, s, per, ident, *a))
            ident += 1
        if s == 0:
            first, all_piv, all_bas = lax.switch(shift[0], branches, contribution, pivot_basis, row_basis)
            moved.append(first)
        else:
            moved.append(lax.switch(shift[s], branches, contribution)[0])

    partial = products(block_map, all_piv, C, per)
    weights, landed, *halves = sum_and_rows(block_map, partial, inverse, moved, per)
    parent = pltpu.with_memory_space_constraint(parent, pltpu.HBM)
    payload, held = updates(block_map, panel_start, ranks, weights, all_bas, landed, parent, C, per)

    branches = []
    pairs = parent.shape[0] // (2 * per)
    for first in range(C):
        for b0 in range(0, pairs, 2):
            b0 += (first + PANEL_T) // C
            branches.append(lambda *v, first=first, b0=b0, ident=ident: gather_panel(first, b0, ident, *v))
            ident += 1
    start = panel_start[0]
    which = lax.rem(start, C) * (pairs // 2) + jnp.minimum(lax.div(start, 2 * C), pairs // 2 - 1)
    factors = lax.switch(which, branches, held, *halves)
    return finish(block_map, panel_start, parent, payload, factors, per)


def solution(mesh):
    placed = (
        P(None, "row", None, "col", None, None),
        P(None, "row", None, "col", None, None),
        P(None, "row", None, None),
        P(None, "row", None, "col"),
        P(),
        P(),
        P(),
        P(),
    )
    return jax.shard_map(
        per_device,
        mesh=mesh,
        in_specs=placed,
        out_specs=P(None, "row", None, "col", None, None),
        check_vma=False,
    )
```

```python
import jax
import jax.numpy as jnp
from jax import lax
from jax.experimental import pallas as pl
from jax.experimental.pallas import tpu as pltpu
from jax.sharding import PartitionSpec as P

PANEL_T = 4
f32 = jnp.float32
bf16 = jnp.bfloat16
i32 = jnp.int32
MESH = pl.DeviceIdType.MESH
DMA = pltpu.SemaphoreType.DMA
SMEM = pl.BlockSpec(memory_space=pltpu.SMEM)
VMEM = pl.BlockSpec(memory_space=pltpu.VMEM)
ANY = pl.BlockSpec(memory_space=pl.ANY)
HBM = pl.BlockSpec(memory_space=pltpu.HBM)
ROOM = 32 << 20
GATHERS = 2


def split(x):
    top = x.astype(bf16)
    return top, (x - top.astype(f32)).astype(bf16)


def dot3(a, b, dims):
    (ah, al), (bh, bl) = a, b
    one = lambda p, q: lax.dot_general(p, q, (dims, ((), ())), preferred_element_type=f32)
    return one(ah, bh) + (one(ah, bl) + one(al, bh))


def ring_place(p, n):
    return jnp.where(p < n // 2, 2 * p, 2 * (n - 1 - p) + 1)


def ring_spot(me, n):
    return jnp.where(me % 2 == 0, me // 2, n - 1 - me // 2)


def greet(targets):
    barrier = pltpu.get_barrier_semaphore()
    for target in targets:
        pl.semaphore_signal(barrier, inc=1, device_id=target, device_id_type=MESH)
    pl.semaphore_wait(barrier, len(targets))


def remote(src, dst, send, recv, to):
    return pltpu.make_async_remote_copy(src, dst, send, recv, device_id=to, device_id_type=MESH)


class Layout:
    def __init__(self, bmap, blocks):
        self.map = bmap
        self.S = blocks
        self.R, self.C = lax.axis_size("row"), lax.axis_size("col")
        self.row, self.col = lax.axis_index("row"), lax.axis_index("col")

    def shift(self, u):
        return self.map[u * self.C] - 2 * self.C * u

    def src_row(self, u, row=None):
        row = self.row if row is None else row
        return lax.rem(row + self.C * self.R - self.shift(u), self.R)

    def src_col(self, s, col=None):
        col = self.col if col is None else col
        return lax.rem(col + self.C - self.shift(s), self.C)

    def first_row(self, u, row=None):
        return lax.div(2 * self.C * u + self.shift(u) + self.src_row(u, row), self.R)

    def first_col(self, s):
        return lax.div(2 * self.C * s + self.shift(s) + self.src_col(s), self.C)


def own_column(start, col, C, bcols):
    k = lax.rem(col - start + C * bcols, C)
    return jnp.minimum(lax.div(start + k, C), bcols - 1)


def shift_kernel(h, s, per, *refs):
    R, n = lax.axis_size("row"), lax.axis_size("col")
    me, my_col = lax.axis_index("row"), lax.axis_index("col")
    gather = s < GATHERS
    if gather:
        child, piv, bas, moved, all_piv, all_bas, send, recv, own_sem, d_send, d_recv, r_send, r_recv = refs
    else:
        child, moved, send, recv = refs
    blocks = moved.shape[0] // per
    pairs = R // 2
    other = me + 1 - 2 * (me % 2)

    signals = []
    if h:
        signals.append({"col": (my_col + n - h) % n})
    if gather:
        signals += [{"row": (me + k) % R} for k in range(1, R)]
    if signals:
        greet(signals)

    def part(i):
        src = child.at[pl.ds(per * (s + i), per), 0, s, 0]
        dst = moved.at[pl.ds(per * i, per)]
        if h:
            return remote(src, dst, send.at[i], recv.at[i], {"col": (my_col + h) % n})
        return pltpu.make_async_copy(src, dst, recv.at[i])

    if gather:
        half = piv.shape[0] // GATHERS
        cuts = [(src, dst, half * s + j * half // m, j * half // m, half // m)
                for src, dst, m in ((piv, all_piv, 2), (bas, all_bas, 1)) for j in range(m)]

        def direct(o, j):
            src, dst, a, b, size = cuts[j]
            to = other if o == 0 else (me // 2 + o) % pairs * 2 + me % 2
            return remote(src.at[pl.ds(a, size), 0], dst.at[me, pl.ds(b, size)], d_send.at[o, j], d_recv.at[o, j],
                          {"row": to})

        def relay(o, j):
            _, dst, _, b, size = cuts[j]
            d = (me // 2 - o + pairs) % pairs * 2 + me % 2
            return remote(dst.at[d, pl.ds(b, size)], dst.at[d, pl.ds(b, size)], r_send.at[o, j], r_recv.at[o, j],
                          {"row": other})

        away = [(o, j) for j in range(len(cuts)) for o in range(1, pairs)]
        near = [(0, j) for j in range(len(cuts))]
        for o, j in away:
            direct(o, j).start()
    for i in range(blocks):
        part(i).start()
    if gather:
        own = [pltpu.make_async_copy(src.at[pl.ds(half * s, half), 0], dst.at[me], own_sem.at[j])
               for j, (src, dst) in enumerate(((piv, all_piv), (bas, all_bas)))]
        for copy in own:
            copy.start()
        for o, j in near:
            direct(o, j).start()
        for o, j in away:
            direct(o, j).wait_recv()
            relay(o, j).start()
        for o, j in near:
            direct(o, j).wait_recv()
        for o, j in away:
            relay(o, j).wait_recv()
            relay(o, j).wait_send()
        for o, j in away + near:
            direct(o, j).wait_send()
        for copy in own:
            copy.wait()
    for i in range(blocks):
        if h:
            part(i).wait_recv()
            part(i).wait_send()
        else:
            part(i).wait()


def shift_columns(h, s, per, ident, child, *factors):
    R = lax.axis_size("row")
    T, tile = child.shape[0], child.shape[-1]
    blocks = T // per - s
    moved = jax.ShapeDtypeStruct((per * blocks, tile, tile), f32)
    remote_ids = bool(h) or bool(factors)
    params = (
        pltpu.CompilerParams(collective_id=ident, has_side_effects=True, vmem_limit_bytes=ROOM)
        if remote_ids
        else pltpu.CompilerParams(vmem_limit_bytes=ROOM)
    )
    shapes, scratch = [moved], [DMA((blocks,)), DMA((blocks,))]
    if factors:
        shapes += [jax.ShapeDtypeStruct((R,) + (f.shape[0] // GATHERS,) + f.shape[2:], f32) for f in factors]
        scratch += [DMA((2,))] + [DMA((R // 2, 3))] * 4
    out = pl.pallas_call(
        lambda *refs: shift_kernel(h, s, per, *refs),
        in_specs=[ANY] * (1 + len(factors)),
        out_specs=[VMEM] * len(shapes),
        out_shape=shapes,
        scratch_shapes=scratch,
        compiler_params=params,
        name=f"shift_{s}_{h}",
    )(child, *factors)
    return tuple(out)


def product_kernel(per, S, bmap, *refs):
    everyone, (out, mine_top, mine_low, their_top, their_low) = refs[:GATHERS], refs[GATHERS:]
    part = everyone[0].shape[1]
    rank = everyone[0].shape[2]
    T = part * GATHERS
    R, C = lax.axis_size("row"), out.shape[0]
    spot = Layout(bmap, S)
    for t in range(T):
        top, low = split(everyone[t // part][spot.src_row(t // per), t % part])
        mine_top[t * rank : (t + 1) * rank, :] = top
        mine_low[t * rank : (t + 1) * rank, :] = low
    at = 0
    for s in range(S):
        for c in range(C):
            src = spot.src_col(s, c)
            top, low = split(everyone[s * per // part][lax.rem(src, R), s * per % part + lax.div(src, R)])
            their_top[c * rank : (c + 1) * rank, :] = top
            their_low[c * rank : (c + 1) * rank, :] = low
        first = s * per * rank
        size = T * rank - first
        mine = (mine_top[first:, :], mine_low[first:, :])
        got = dot3((their_top[...], their_low[...]), mine, ((1,), (1,)))
        out[:, :, at : at + size] = got.reshape(C, rank, size)
        at += size


def products(bmap, everyone, C, per):
    R, part, rank, width = everyone[0].shape
    T = part * GATHERS
    S = T // per
    total = sum((S - s) * per * rank for s in range(S))
    return pl.pallas_call(
        lambda *refs: product_kernel(per, S, *refs),
        in_specs=[SMEM] + [VMEM] * GATHERS,
        out_specs=VMEM,
        out_shape=jax.ShapeDtypeStruct((C, rank, total), f32),
        scratch_shapes=[pltpu.VMEM((T * rank, width), bf16)] * 2 + [pltpu.VMEM((C * rank, width), bf16)] * 2,
        compiler_params=pltpu.CompilerParams(vmem_limit_bytes=ROOM),
        name="products",
    )(bmap, *everyone)


PARTS = 4


def sum_kernel(per, bmap, partial, inverse, *refs):
    S = len(refs) - 11
    moved = refs[:S]
    out, landed, inv_top, inv_low, slots, outbox, send, recv, row_send, row_recv, own_sem = refs[S:]
    R, n = lax.axis_size("row"), lax.axis_size("col")
    my_row, me = lax.axis_index("row"), lax.axis_index("col")
    chunk = partial.shape[1] // (2 * PARTS)
    pos = ring_spot(me, n)
    right = ring_place((pos + 1) % n, n)
    left = ring_place((pos + n - 1) % n, n)
    greet([{"col": left}, {"col": right}] + [{"row": (my_row + k) % R} for k in range(1, R)])
    rows = lambda side, h: pl.ds((PARTS * side + h) * chunk, chunk)

    def part(side, k, h):
        q = (pos - 1 - k + n) % n if side == 0 else (pos + 1 + k) % n
        return partial.at[ring_place(q, n), rows(side, h)]

    def hop(side, k, h):
        src = part(side, 0, h) if k == 0 else slots.at[side, k - 1, h]
        return remote(src, slots.at[side, k, h], send.at[side, k, h], recv.at[side, k, h],
                      {"col": right if side == 0 else left})

    def cross(k):
        return remote(outbox.at[k - 1], landed.at[k], row_send.at[k - 1], row_recv.at[k - 1], {"row": (my_row + k) % R})

    for h in range(PARTS):
        for side in range(2):
            hop(side, 0, h).start()

    spot = Layout(bmap, S)
    for k in [R // 2] + [k for k in range(R) if k != R // 2]:
        block = sum(u * (lax.rem(spot.shift(u), R) == k).astype(i32) for u in range(S))
        for s in range(S):
            place = jnp.clip(block - s, 0, S - 1 - s)
            for p in range(per):
                tile = moved[s][place * per + p]
                if k == 0:
                    landed[0, s, p] = tile
                else:
                    outbox[k - 1, s, p] = tile
        if k:
            cross(k).start()

    top, rest = split(inverse[...])
    inv_top[...] = top
    inv_low[...] = rest

    every = [(k, h, side) for k in range(n - 1) for h in range(PARTS) for side in range(2)]
    for k, h, side in every:
        if k > 0:
            hop(side, k - 1, h).wait_recv()
            slots[side, k - 1, h] = slots[side, k - 1, h] + part(side, k, h)[...]
            hop(side, k, h).start()
    for h in range(PARTS):
        for side in range(2):
            hop(side, n - 2, h).wait_recv()
            out[rows(side, h), :] = slots[side, n - 2, h] + partial[me, rows(side, h), :]
    for k in range(1, R):
        cross(k).wait_recv()
        cross(k).wait_send()
    for k, h, side in every:
        hop(side, k, h).wait_send()


def sum_and_rows(bmap, partial, inverse, moved, per):
    R = lax.axis_size("row")
    n, rank, total = partial.shape
    S, tile = len(moved), moved[0].shape[-1]
    box = (S, per, tile, tile)
    return pl.pallas_call(
        lambda *refs: sum_kernel(per, *refs),
        in_specs=[SMEM] + [VMEM] * (2 + S),
        out_specs=[VMEM] * 4,
        out_shape=[jax.ShapeDtypeStruct((rank, total), f32), jax.ShapeDtypeStruct((R,) + box, f32)]
        + [jax.ShapeDtypeStruct(inverse.shape, bf16)] * 2,
        scratch_shapes=[
            pltpu.VMEM((2, n - 1, PARTS, rank // (2 * PARTS), total), f32),
            pltpu.VMEM((R - 1,) + box, f32),
            DMA((2, n - 1, PARTS)), DMA((2, n - 1, PARTS)), DMA((R - 1,)), DMA((R - 1,)), DMA,
        ],
        compiler_params=pltpu.CompilerParams(collective_id=1, has_side_effects=True, vmem_limit_bytes=ROOM),
        name="sum_and_rows",
    )(bmap, partial, inverse, *moved)


def update_kernel(per, C, bmap, start, ranks, weights, *refs):
    bases, (landed, parent, out, held, sems) = refs[:GATHERS], refs[GATHERS:]
    S, T, tile = out.shape[:3]
    R, part, rank, _ = bases[0].shape
    bcols = parent.shape[2]
    spot = Layout(bmap, S)
    b = own_column(start[0], spot.col, C, bcols)
    copies = []
    for i in range(held.shape[1]):
        for q in range(per):
            copies.append(pltpu.make_async_copy(parent.at[per * i + q, 0, b, 0], held.at[q, i], sems.at[q, i]))
            copies[-1].start()

    depth = lax.broadcasted_iota(i32, (rank, tile), 0)

    def basis(row, block, p):
        t = block * per + p
        return split(jnp.where(depth < ranks[t * R + row], bases[block * per // part][row, block * per % part + p], 0.0))

    at = 0
    for s in range(S):
        size = (S - s) * per * rank
        src = spot.src_col(s)
        j = s * C + src
        col_basis = basis(lax.rem(src, R), s, lax.div(src, R))
        half = dot3(split(weights[:, at : at + size]), col_basis, ((0,), (0,)))
        at += size
        for t in range(s * per, T):
            u, p = t // per, t % per
            i = t - s * per
            row = spot.src_row(u)
            update = dot3(basis(row, u, p), split(half[i * rank : (i + 1) * rank]), ((0,), (0,)))
            moved = landed[lax.rem(spot.shift(u), R), s, p]
            out[s, t] = jnp.where(t * R + row >= j, moved - update, 0.0)

    s_own = lax.div(b, bcols // S)
    reached = spot.first_col(s_own) == b
    for copy in copies:
        copy.wait()

    @pl.when(reached)
    def _():
        for u in range(S):
            @pl.when(s_own <= u)
            def _():
                for p in range(per):
                    a = spot.first_row(u) + p
                    q, i = lax.rem(a, per), lax.div(a, per)
                    held[q, i] = held[q, i] + out[s_own, u * per + p]


def updates(bmap, start, ranks, weights, bases, landed, parent, C, per):
    R, part, rank, tile = bases[0].shape
    T, rows = part * GATHERS, parent.shape[0]
    S = T // per
    return pl.pallas_call(
        lambda *refs: update_kernel(per, C, *refs),
        in_specs=[SMEM] * 3 + [VMEM] * (2 + GATHERS) + [HBM],
        out_specs=[VMEM, VMEM],
        out_shape=[
            jax.ShapeDtypeStruct((S, T, tile, tile), f32),
            jax.ShapeDtypeStruct((per, rows // per, tile, tile), f32),
        ],
        scratch_shapes=[DMA((per, rows // per))],
        compiler_params=pltpu.CompilerParams(vmem_limit_bytes=ROOM),
        name="updates",
    )(bmap, start, ranks, weights, *bases, landed, parent)


def panel_kernel(first, b0, held, inv_top, inv_low, row_top, row_low, col_top, col_low, panel, cols, recv, up, down, across,
                 other, own_sem, cross_send, cross_recv, relay_send):
    R, n = lax.axis_size("row"), lax.axis_size("col")
    my_row, me = lax.axis_index("row"), lax.axis_index("col")
    Bn = held.shape[1]
    z, x, ends = me // 2, me % 2, n // 2 - 1
    side = me + 1 - 2 * x
    root, parity = me % R, me // R
    is_root = my_row == root
    partner = my_row + 1 - 2 * (my_row % 2)
    near = my_row // 2 == root // 2
    owner = lambda k: (first + k) % n

    def lone(k):
        return ((k == 0) | (k == PANEL_T - 1)) & (first % 2 == 1)

    def beside(k):
        return owner(k) + 1 - 2 * (owner(k) % 2)

    def behind(k):
        return lone(k) & (me == jnp.where(beside(k) < 2, beside(k) + 2, beside(k) - 2))

    def hops(k, lane):
        zk, xk = owner(k) // 2, owner(k) % 2
        return jnp.maximum(z - zk, zk - z) + (lane + xk) % 2

    barrier = pltpu.get_barrier_semaphore()
    for k in range(1, R):
        pl.semaphore_signal(barrier, inc=1, device_id={"row": (my_row + k) % R}, device_id_type=MESH)
    pl.semaphore_signal(barrier, inc=1, device_id={"col": side}, device_id_type=MESH)

    @pl.when(z > 0)
    def _():
        pl.semaphore_signal(barrier, inc=1, device_id={"col": me - 2}, device_id_type=MESH)

    @pl.when(z < ends)
    def _():
        pl.semaphore_signal(barrier, inc=1, device_id={"col": me + 2}, device_id_type=MESH)

    for k in range(PANEL_T):
        @pl.when(me == owner(k))
        def _():
            pltpu.make_async_copy(held, panel.at[k], own_sem).start()

    pl.semaphore_wait(barrier, R + jnp.minimum(z, 1) + jnp.minimum(ends - z, 1))

    for k in range(PANEL_T):
        @pl.when(me == owner(k))
        def _():
            pltpu.make_async_copy(held, panel.at[k], own_sem).wait()

    def hop(k, h, i, sem, to):
        ref = panel.at[k, h, i]
        return remote(ref, ref, sem.at[k, i], recv.at[k, h, i], {"col": to})

    def sends(k, i, act):
        zk, xk = owner(k) // 2, owner(k) % 2

        @pl.when(me == owner(k))
        def _():
            act(hop(k, 1 - x, i, other, side))

        @pl.when((z >= zk) & (z < ends))
        def _():
            act(hop(k, x, i, up, me + 2))

        @pl.when((z <= zk) & (z > 0))
        def _():
            act(hop(k, x, i, down, me - 2))

        @pl.when(((z != zk) | (x == xk)) & ~((me == owner(k)) & lone(k)))
        def _():
            act(hop(k, x, i, across, side))

    def main(k, i):
        @pl.when(me != owner(k))
        def _():
            hop(k, x, i, up, side).wait_recv()

        sends(k, i, lambda copy: copy.start())

    def cross(k, i, o):
        to = partner if o == 0 else (my_row // 2 + o) % (R // 2) * 2 + (my_row + k) % 2
        return remote(panel.at[k, parity, i], cols.at[k, i], cross_send.at[k, i, o], cross_recv.at[k, i], {"row": to})

    def late(k, i):
        @pl.when(me != owner(k))
        def _():
            hop(k, 1 - x, i, up, side).wait_recv()

        @pl.when(behind(k))
        def _():
            hop(k, 1 - x, i, other, beside(k)).start()

        @pl.when(is_root)
        def _():
            for o in range(1, R // 2):
                cross(k, i, o).start()
            cross(k, i, 0).start()

    def relay(k, i):
        return remote(cols.at[k, i], cols.at[k, i], relay_send.at[k, i], cross_recv.at[k, i], {"row": partner})

    def direct(k):
        return ~near & ((my_row + root + k) % 2 == 0)

    def pass_on(k, i):
        @pl.when(direct(k))
        def _():
            relay(k, i).wait_recv()
            relay(k, i).start()

    tile = held.shape[-1]

    def settle(k, i):
        @pl.when(~direct(k) & ~is_root)
        def _():
            relay(k, i).wait_recv()

        at = pl.ds(pl.multiple_of(k * tile, tile), tile)
        top, rest = split(jnp.where(is_root, panel[k, parity, i], cols[k, i]))
        col_top[i, :, at] = top
        col_low[i, :, at] = rest

    def scale(i):
        rows = [jnp.concatenate([panel[k, q, i] for k in range(PANEL_T)], axis=1) for q in range(held.shape[0])]
        scaled = dot3(split(jnp.concatenate(rows, axis=0)), (inv_top[...], inv_low[...]), ((1,), (0,)))
        top, rest = split(scaled)
        row_top[i] = top
        row_low[i] = rest

    full = ends + 2

    def body(t, _):
        j, k = t // PANEL_T, t % PANEL_T

        def turn(lag, act, also=True):
            i = b0 + (j - lag + 2 * n) // 2 - n

            @pl.when(((j + lag) % 2 == 0) & (i >= b0) & (i < Bn) & also)
            def _():
                act(i)

        there = hops(k, 1 - x) + 2 * (lone(k) & (me == beside(k))).astype(i32)
        turn(hops(k, x), lambda i: main(k, i))
        turn(there + 1, lambda i: late(k, i))
        turn(there + 2, lambda i: pass_on(k, i))
        turn(there + 3, lambda i: settle(k, i))
        turn(full, scale, k == PANEL_T - 1)
        return 0

    lax.fori_loop(0, (2 * (Bn - b0) + ends + 3) * PANEL_T, body, 0)

    def drain(t, _):
        i, k = b0 + t // PANEL_T, t % PANEL_T
        sends(k, i, lambda copy: copy.wait_send())

        @pl.when(behind(k))
        def _():
            hop(k, 1 - x, i, other, beside(k)).wait_send()

        @pl.when(is_root)
        def _():
            for o in range(R // 2):
                cross(k, i, o).wait_send()

        @pl.when(direct(k))
        def _():
            relay(k, i).wait_send()

        return 0

    lax.fori_loop(0, (Bn - b0) * PANEL_T, drain, 0)


def gather_panel(first, b0, ident, held, *inverse):
    R = lax.axis_size("row")
    per, Bn, tile, _ = held.shape
    each = (PANEL_T, Bn)
    wide = PANEL_T * tile
    return tuple(pl.pallas_call(
        lambda *refs: panel_kernel(first, b0, *refs),
        in_specs=[VMEM] * 3,
        out_specs=[VMEM] * 4,
        out_shape=[jax.ShapeDtypeStruct((Bn, per * tile, wide), bf16)] * 2
        + [jax.ShapeDtypeStruct((Bn, tile, wide), bf16)] * 2,
        scratch_shapes=[pltpu.VMEM((PANEL_T,) + held.shape, f32), pltpu.VMEM(each + (tile, tile), f32)]
        + [DMA((PANEL_T, per, Bn))] + [DMA(each)] * 4 + [DMA, DMA(each + (R // 2,)), DMA(each), DMA(each)],
        compiler_params=pltpu.CompilerParams(collective_id=ident, has_side_effects=True, vmem_limit_bytes=ROOM),
        name=f"panel_{first}_{b0}",
    )(held, *inverse))


def final_kernel(bmap, start, parent, payload, row_top, row_low, col_top, col_low, out):
    step = pl.program_id(0)
    per, bcols = parent.shape[0], parent.shape[2]
    tile = parent.shape[4]
    S = payload.shape[0]
    group = bcols // S
    spot = Layout(bmap, S)
    R, C = spot.R, spot.C
    first_active = start[0] + PANEL_T

    u = lax.div(step, 2)
    first = spot.first_row(u)
    places = [step * per + p - first for p in range(per)]
    hits = [(d >= 0) & (d < per) for d in places]
    big_rows = [spot.row + (step * per + p) * R for p in range(per)]
    big_cols = [spot.col + b * C for b in range(bcols)]

    for b in range(bcols):
        s = b // group
        reached = (spot.first_col(s) == b) & (s <= u)
        for p in range(per):
            out[p, 0, b, 0] = parent[p, 0, b, 0]

            @pl.when(hits[p] & reached)
            def _():
                out[p, 0, b, 0] = parent[p, 0, b, 0] + payload[s, u * per + places[p]]

    for g in range(S):
        @pl.when((big_rows[-1] >= big_cols[g * group]) & (big_cols[g * group + group - 1] >= first_active))
        def _():
            pair = lambda ref: ref[g * group : (g + 1) * group].reshape(group * tile, -1)
            trailing = dot3((row_top[step], row_low[step]), (pair(col_top), pair(col_low)), ((1,), (1,)))
            for j in range(group):
                b = g * group + j
                for p in range(per):
                    active = (big_rows[p] >= big_cols[b]) & (big_cols[b] >= first_active)
                    part = trailing[p * tile : (p + 1) * tile, j * tile : (j + 1) * tile]
                    out[p, 0, b, 0] = out[p, 0, b, 0] - jnp.where(active, part, 0.0)


def finish(bmap, start, parent, payload, factors, per):
    rows, _, bcols, _, tile, _ = parent.shape
    whole = lambda a: pl.BlockSpec(a.shape, lambda i, m, t: (0,) * a.ndim, pipeline_mode=pl.Buffered(1))
    big = pl.BlockSpec((per, 1, bcols, 1, tile, tile), lambda i, m, t: (i, 0, 0, 0, 0, 0))
    flops = 6 * rows * tile * PANEL_T * tile * bcols * tile
    return pl.pallas_call(
        final_kernel,
        grid_spec=pltpu.PrefetchScalarGridSpec(
            num_scalar_prefetch=2,
            grid=(rows // per,),
            in_specs=[big, whole(payload)] + [whole(f) for f in factors],
            out_specs=big,
        ),
        out_shape=jax.ShapeDtypeStruct(parent.shape, f32),
        compiler_params=pltpu.CompilerParams(vmem_limit_bytes=ROOM),
        cost_estimate=pl.CostEstimate(flops=flops, bytes_accessed=10 * parent.size, transcendentals=0),
        name="finish",
    )(bmap, start, parent, payload, *factors)


def per_device(contribution, parent, row_basis, pivot_basis, ranks, block_map, panel_start, inverse):
    R, C = lax.axis_size("row"), lax.axis_size("col")
    S = contribution.shape[2]
    per = C // R
    shift = [block_map[u * C] - 2 * C * u for u in range(S)]

    ident = 2
    moved, all_piv, all_bas = [], [], []
    for s in range(S):
        branches = []
        for h in range(C):
            if s < GATHERS:
                branches.append(lambda *a, h=h, s=s, ident=ident: shift_columns(h, s, per, ident, *a))
                ident += 1
            else:
                pairs = [(d, (d + h) % C) for d in range(C)]
                branches.append(lambda v, p=pairs, h=h: lax.ppermute(v, "col", p) if h else v)
        if s < GATHERS:
            came, piv, bas = lax.switch(shift[s], branches, contribution, pivot_basis, row_basis)
            all_piv.append(piv)
            all_bas.append(bas)
        else:
            came = lax.switch(shift[s], branches, contribution[per * s :, 0, s, 0])
        moved.append(came)

    partial = products(block_map, all_piv, C, per)
    weights, landed, *halves = sum_and_rows(block_map, partial, inverse, moved, per)
    parent = pltpu.with_memory_space_constraint(parent, pltpu.HBM)
    payload, held = updates(block_map, panel_start, ranks, weights, all_bas, landed, parent, C, per)

    branches = []
    pairs = parent.shape[0] // (2 * per)
    for first in range(C):
        for b0 in range(0, pairs, 2):
            b0 += (first + PANEL_T) // C
            branches.append(lambda *v, first=first, b0=b0, ident=ident: gather_panel(first, b0, ident, *v))
            ident += 1
    start = panel_start[0]
    which = lax.rem(start, C) * (pairs // 2) + jnp.minimum(lax.div(start, 2 * C), pairs // 2 - 1)
    factors = lax.switch(which, branches, held, *halves)
    return finish(block_map, panel_start, parent, payload, factors, per)


def solution(mesh):
    placed = (
        P(None, "row", None, "col", None, None),
        P(None, "row", None, "col", None, None),
        P(None, "row", None, None),
        P(None, "row", None, "col"),
        P(),
        P(),
        P(),
        P(),
    )
    return jax.shard_map(
        per_device,
        mesh=mesh,
        in_specs=placed,
        out_specs=P(None, "row", None, "col", None, None),
        check_vma=False,
    )
```

```python
import jax
import jax.numpy as jnp
from jax import lax
from jax.experimental import pallas as pl
from jax.experimental.pallas import tpu as pltpu
from jax.sharding import PartitionSpec as P

PANEL_T = 4
f32 = jnp.float32
bf16 = jnp.bfloat16
i32 = jnp.int32
MESH = pl.DeviceIdType.MESH
DMA = pltpu.SemaphoreType.DMA
SMEM = pl.BlockSpec(memory_space=pltpu.SMEM)
VMEM = pl.BlockSpec(memory_space=pltpu.VMEM)
ANY = pl.BlockSpec(memory_space=pl.ANY)
HBM = pl.BlockSpec(memory_space=pltpu.HBM)
ROOM = 32 << 20
GATHERS = 2
LAG = 2


def split(x):
    top = x.astype(bf16)
    return top, (x - top.astype(f32)).astype(bf16)


def dot3(a, b, dims):
    (ah, al), (bh, bl) = a, b
    one = lambda p, q: lax.dot_general(p, q, (dims, ((), ())), preferred_element_type=f32)
    return one(ah, bh) + (one(ah, bl) + one(al, bh))


def ring_place(p, n):
    return jnp.where(p < n // 2, 2 * p, 2 * (n - 1 - p) + 1)


def ring_spot(me, n):
    return jnp.where(me % 2 == 0, me // 2, n - 1 - me // 2)


def greet(targets):
    barrier = pltpu.get_barrier_semaphore()
    for target in targets:
        pl.semaphore_signal(barrier, inc=1, device_id=target, device_id_type=MESH)
    pl.semaphore_wait(barrier, len(targets))


def remote(src, dst, send, recv, to):
    return pltpu.make_async_remote_copy(src, dst, send, recv, device_id=to, device_id_type=MESH)


class Layout:
    def __init__(self, bmap, blocks):
        self.map = bmap
        self.S = blocks
        self.R, self.C = lax.axis_size("row"), lax.axis_size("col")
        self.row, self.col = lax.axis_index("row"), lax.axis_index("col")

    def shift(self, u):
        return self.map[u * self.C] - 2 * self.C * u

    def src_row(self, u, row=None):
        row = self.row if row is None else row
        return lax.rem(row + self.C * self.R - self.shift(u), self.R)

    def src_col(self, s, col=None):
        col = self.col if col is None else col
        return lax.rem(col + self.C - self.shift(s), self.C)

    def first_row(self, u, row=None):
        return lax.div(2 * self.C * u + self.shift(u) + self.src_row(u, row), self.R)

    def first_col(self, s):
        return lax.div(2 * self.C * s + self.shift(s) + self.src_col(s), self.C)


def own_column(start, col, C, bcols):
    k = lax.rem(col - start + C * bcols, C)
    return jnp.minimum(lax.div(start + k, C), bcols - 1)


def shift_kernel(h, s, per, *refs):
    R, n = lax.axis_size("row"), lax.axis_size("col")
    me, my_col = lax.axis_index("row"), lax.axis_index("col")
    gather = s < GATHERS
    if gather:
        child, piv, bas, moved, all_piv, all_bas, send, recv, own_sem, d_send, d_recv, r_send, r_recv = refs
    else:
        child, moved, send, recv = refs
    blocks = moved.shape[0] // per
    pairs = R // 2
    other = me + 1 - 2 * (me % 2)

    signals = []
    if h:
        signals.append({"col": (my_col + n - h) % n})
    if gather:
        signals += [{"row": (me + k) % R} for k in range(1, R)]
    if signals:
        greet(signals)

    def part(i):
        src = child.at[pl.ds(per * (s + i), per), 0, s, 0]
        dst = moved.at[pl.ds(per * i, per)]
        if h:
            return remote(src, dst, send.at[i], recv.at[i], {"col": (my_col + h) % n})
        return pltpu.make_async_copy(src, dst, recv.at[i])

    if gather:
        half = piv.shape[0] // GATHERS
        cuts = [(src, dst, half * s + j * half // m, j * half // m, half // m)
                for src, dst, m in ((piv, all_piv, 2), (bas, all_bas, 1)) for j in range(m)]

        def direct(o, j):
            src, dst, a, b, size = cuts[j]
            to = other if o == 0 else (me // 2 + o) % pairs * 2 + me % 2
            return remote(src.at[pl.ds(a, size), 0], dst.at[me, pl.ds(b, size)], d_send.at[o, j], d_recv.at[o, j],
                          {"row": to})

        def relay(o, j):
            _, dst, _, b, size = cuts[j]
            d = (me // 2 - o + pairs) % pairs * 2 + me % 2
            return remote(dst.at[d, pl.ds(b, size)], dst.at[d, pl.ds(b, size)], r_send.at[o, j], r_recv.at[o, j],
                          {"row": other})

        away = [(o, j) for j in range(len(cuts)) for o in range(1, pairs)]
        near = [(0, j) for j in range(len(cuts))]
        for o, j in away:
            direct(o, j).start()
    for i in range(blocks):
        part(i).start()
    if gather:
        own = [pltpu.make_async_copy(src.at[pl.ds(half * s, half), 0], dst.at[me], own_sem.at[j])
               for j, (src, dst) in enumerate(((piv, all_piv), (bas, all_bas)))]
        for copy in own:
            copy.start()
        for o, j in near:
            direct(o, j).start()
        for o, j in away:
            direct(o, j).wait_recv()
            relay(o, j).start()
        for o, j in near:
            direct(o, j).wait_recv()
        for o, j in away:
            relay(o, j).wait_recv()
            relay(o, j).wait_send()
        for o, j in away + near:
            direct(o, j).wait_send()
        for copy in own:
            copy.wait()
    for i in range(blocks):
        if h:
            part(i).wait_recv()
            part(i).wait_send()
        else:
            part(i).wait()


def shift_columns(h, s, per, ident, child, *factors):
    R = lax.axis_size("row")
    T, tile = child.shape[0], child.shape[-1]
    blocks = T // per - s
    moved = jax.ShapeDtypeStruct((per * blocks, tile, tile), f32)
    remote_ids = bool(h) or bool(factors)
    params = (
        pltpu.CompilerParams(collective_id=ident, has_side_effects=True, vmem_limit_bytes=ROOM)
        if remote_ids
        else pltpu.CompilerParams(vmem_limit_bytes=ROOM)
    )
    shapes, scratch = [moved], [DMA((blocks,)), DMA((blocks,))]
    if factors:
        shapes += [jax.ShapeDtypeStruct((R,) + (f.shape[0] // GATHERS,) + f.shape[2:], f32) for f in factors]
        scratch += [DMA((2,))] + [DMA((R // 2, 3))] * 4
    out = pl.pallas_call(
        lambda *refs: shift_kernel(h, s, per, *refs),
        in_specs=[ANY] * (1 + len(factors)),
        out_specs=[VMEM] * len(shapes),
        out_shape=shapes,
        scratch_shapes=scratch,
        compiler_params=params,
        name=f"shift_{s}_{h}",
    )(child, *factors)
    return tuple(out)


def product_kernel(per, S, bmap, *refs):
    everyone, (out, mine_top, mine_low, their_top, their_low) = refs[:GATHERS], refs[GATHERS:]
    part = everyone[0].shape[1]
    rank = everyone[0].shape[2]
    T = part * GATHERS
    R, C = lax.axis_size("row"), out.shape[0]
    spot = Layout(bmap, S)
    for t in range(T):
        top, low = split(everyone[t // part][spot.src_row(t // per), t % part])
        mine_top[t * rank : (t + 1) * rank, :] = top
        mine_low[t * rank : (t + 1) * rank, :] = low
    at = 0
    for s in range(S):
        for c in range(C):
            src = spot.src_col(s, c)
            top, low = split(everyone[s * per // part][lax.rem(src, R), s * per % part + lax.div(src, R)])
            their_top[c * rank : (c + 1) * rank, :] = top
            their_low[c * rank : (c + 1) * rank, :] = low
        first = s * per * rank
        size = T * rank - first
        mine = (mine_top[first:, :], mine_low[first:, :])
        got = dot3((their_top[...], their_low[...]), mine, ((1,), (1,)))
        out[:, :, at : at + size] = got.reshape(C, rank, size)
        at += size


def products(bmap, everyone, C, per):
    R, part, rank, width = everyone[0].shape
    T = part * GATHERS
    S = T // per
    total = sum((S - s) * per * rank for s in range(S))
    return pl.pallas_call(
        lambda *refs: product_kernel(per, S, *refs),
        in_specs=[SMEM] + [VMEM] * GATHERS,
        out_specs=VMEM,
        out_shape=jax.ShapeDtypeStruct((C, rank, total), f32),
        scratch_shapes=[pltpu.VMEM((T * rank, width), bf16)] * 2 + [pltpu.VMEM((C * rank, width), bf16)] * 2,
        compiler_params=pltpu.CompilerParams(vmem_limit_bytes=ROOM),
        name="products",
    )(bmap, *everyone)


PARTS = 4


def sum_kernel(per, bmap, partial, inverse, *refs):
    S = len(refs) - 11
    moved = refs[:S]
    out, landed, inv_top, inv_low, slots, outbox, send, recv, row_send, row_recv, own_sem = refs[S:]
    R, n = lax.axis_size("row"), lax.axis_size("col")
    my_row, me = lax.axis_index("row"), lax.axis_index("col")
    chunk = partial.shape[1] // (2 * PARTS)
    pos = ring_spot(me, n)
    right = ring_place((pos + 1) % n, n)
    left = ring_place((pos + n - 1) % n, n)
    greet([{"col": left}, {"col": right}] + [{"row": (my_row + k) % R} for k in range(1, R)])
    rows = lambda side, h: pl.ds((PARTS * side + h) * chunk, chunk)

    def part(side, k, h):
        q = (pos - 1 - k + n) % n if side == 0 else (pos + 1 + k) % n
        return partial.at[ring_place(q, n), rows(side, h)]

    def hop(side, k, h):
        src = part(side, 0, h) if k == 0 else slots.at[side, k - 1, h]
        return remote(src, slots.at[side, k, h], send.at[side, k, h], recv.at[side, k, h],
                      {"col": right if side == 0 else left})

    def cross(k):
        return remote(outbox.at[k - 1], landed.at[k], row_send.at[k - 1], row_recv.at[k - 1], {"row": (my_row + k) % R})

    for h in range(PARTS):
        for side in range(2):
            hop(side, 0, h).start()

    spot = Layout(bmap, S)
    for k in [R // 2] + [k for k in range(R) if k != R // 2]:
        block = sum(u * (lax.rem(spot.shift(u), R) == k).astype(i32) for u in range(S))
        for s in range(S):
            place = jnp.clip(block - s, 0, S - 1 - s)
            for p in range(per):
                tile = moved[s][place * per + p]
                if k == 0:
                    landed[0, s, p] = tile
                else:
                    outbox[k - 1, s, p] = tile
        if k:
            cross(k).start()

    top, rest = split(inverse[...])
    inv_top[...] = top
    inv_low[...] = rest

    every = [(k, h, side) for k in range(n - 1) for h in range(PARTS) for side in range(2)]
    for k, h, side in every:
        if k > 0:
            hop(side, k - 1, h).wait_recv()
            slots[side, k - 1, h] = slots[side, k - 1, h] + part(side, k, h)[...]
            hop(side, k, h).start()
    for h in range(PARTS):
        for side in range(2):
            hop(side, n - 2, h).wait_recv()
            out[rows(side, h), :] = slots[side, n - 2, h] + partial[me, rows(side, h), :]
    for k in range(1, R):
        cross(k).wait_recv()
        cross(k).wait_send()
    for k, h, side in every:
        hop(side, k, h).wait_send()


def sum_and_rows(bmap, partial, inverse, moved, per):
    R = lax.axis_size("row")
    n, rank, total = partial.shape
    S, tile = len(moved), moved[0].shape[-1]
    box = (S, per, tile, tile)
    return pl.pallas_call(
        lambda *refs: sum_kernel(per, *refs),
        in_specs=[SMEM] + [VMEM] * (2 + S),
        out_specs=[VMEM] * 4,
        out_shape=[jax.ShapeDtypeStruct((rank, total), f32), jax.ShapeDtypeStruct((R,) + box, f32)]
        + [jax.ShapeDtypeStruct(inverse.shape, bf16)] * 2,
        scratch_shapes=[
            pltpu.VMEM((2, n - 1, PARTS, rank // (2 * PARTS), total), f32),
            pltpu.VMEM((R - 1,) + box, f32),
            DMA((2, n - 1, PARTS)), DMA((2, n - 1, PARTS)), DMA((R - 1,)), DMA((R - 1,)), DMA,
        ],
        compiler_params=pltpu.CompilerParams(collective_id=1, has_side_effects=True, vmem_limit_bytes=ROOM),
        name="sum_and_rows",
    )(bmap, partial, inverse, *moved)


def update_kernel(per, C, bmap, start, ranks, weights, *refs):
    bases, (landed, parent, out, held, sems) = refs[:GATHERS], refs[GATHERS:]
    S, T, tile = out.shape[:3]
    R, part, rank, _ = bases[0].shape
    bcols = parent.shape[2]
    spot = Layout(bmap, S)
    b = own_column(start[0], spot.col, C, bcols)
    copies = []
    for i in range(held.shape[1]):
        for q in range(per):
            copies.append(pltpu.make_async_copy(parent.at[per * i + q, 0, b, 0], held.at[q, i], sems.at[q, i]))
            copies[-1].start()

    depth = lax.broadcasted_iota(i32, (rank, tile), 0)

    def basis(row, block, p):
        t = block * per + p
        return split(jnp.where(depth < ranks[t * R + row], bases[block * per // part][row, block * per % part + p], 0.0))

    at = 0
    for s in range(S):
        size = (S - s) * per * rank
        src = spot.src_col(s)
        j = s * C + src
        col_basis = basis(lax.rem(src, R), s, lax.div(src, R))
        half = dot3(split(weights[:, at : at + size]), col_basis, ((0,), (0,)))
        at += size
        for t in range(s * per, T):
            u, p = t // per, t % per
            i = t - s * per
            row = spot.src_row(u)
            update = dot3(basis(row, u, p), split(half[i * rank : (i + 1) * rank]), ((0,), (0,)))
            moved = landed[lax.rem(spot.shift(u), R), s, p]
            out[s, t] = jnp.where(t * R + row >= j, moved - update, 0.0)

    s_own = lax.div(b, bcols // S)
    reached = spot.first_col(s_own) == b
    for copy in copies:
        copy.wait()

    @pl.when(reached)
    def _():
        for u in range(S):
            @pl.when(s_own <= u)
            def _():
                for p in range(per):
                    a = spot.first_row(u) + p
                    q, i = lax.rem(a, per), lax.div(a, per)
                    held[q, i] = held[q, i] + out[s_own, u * per + p]


def updates(bmap, start, ranks, weights, bases, landed, parent, C, per):
    R, part, rank, tile = bases[0].shape
    T, rows = part * GATHERS, parent.shape[0]
    S = T // per
    return pl.pallas_call(
        lambda *refs: update_kernel(per, C, *refs),
        in_specs=[SMEM] * 3 + [VMEM] * (2 + GATHERS) + [HBM],
        out_specs=[VMEM, VMEM],
        out_shape=[
            jax.ShapeDtypeStruct((S, T, tile, tile), f32),
            jax.ShapeDtypeStruct((per, rows // per, tile, tile), f32),
        ],
        scratch_shapes=[DMA((per, rows // per))],
        compiler_params=pltpu.CompilerParams(vmem_limit_bytes=ROOM),
        name="updates",
    )(bmap, start, ranks, weights, *bases, landed, parent)


def panel_kernel(first, b0, held, inv_top, inv_low, row_top, row_low, col_top, col_low, panel, cols, recv, up, down, across,
                 other, own_sem, cross_send, cross_recv, relay_send):
    R, n = lax.axis_size("row"), lax.axis_size("col")
    my_row, me = lax.axis_index("row"), lax.axis_index("col")
    Bn = held.shape[1]
    z, x, ends = me // 2, me % 2, n // 2 - 1
    side = me + 1 - 2 * x
    root, parity = me % R, me // R
    is_root = my_row == root
    partner = my_row + 1 - 2 * (my_row % 2)
    near = my_row // 2 == root // 2
    owner = lambda k: (first + k) % n

    def lone(k):
        return ((k == 0) | (k == PANEL_T - 1)) & (first % 2 == 1)

    def beside(k):
        return owner(k) + 1 - 2 * (owner(k) % 2)

    def behind(k):
        return lone(k) & (me == jnp.where(beside(k) < 2, beside(k) + 2, beside(k) - 2))

    def hops(k, lane):
        zk, xk = owner(k) // 2, owner(k) % 2
        return jnp.maximum(z - zk, zk - z) + (lane + xk) % 2

    barrier = pltpu.get_barrier_semaphore()
    for k in range(1, R):
        pl.semaphore_signal(barrier, inc=1, device_id={"row": (my_row + k) % R}, device_id_type=MESH)
    pl.semaphore_signal(barrier, inc=1, device_id={"col": side}, device_id_type=MESH)

    @pl.when(z > 0)
    def _():
        pl.semaphore_signal(barrier, inc=1, device_id={"col": me - 2}, device_id_type=MESH)

    @pl.when(z < ends)
    def _():
        pl.semaphore_signal(barrier, inc=1, device_id={"col": me + 2}, device_id_type=MESH)

    for k in range(PANEL_T):
        @pl.when(me == owner(k))
        def _():
            pltpu.make_async_copy(held, panel.at[k], own_sem).start()

    pl.semaphore_wait(barrier, R + jnp.minimum(z, 1) + jnp.minimum(ends - z, 1))

    for k in range(PANEL_T):
        @pl.when(me == owner(k))
        def _():
            pltpu.make_async_copy(held, panel.at[k], own_sem).wait()

    def hop(k, h, i, sem, to):
        ref = panel.at[k, h, i]
        return remote(ref, ref, sem.at[k, i], recv.at[k, h, i], {"col": to})

    def sends(k, i, act):
        zk, xk = owner(k) // 2, owner(k) % 2

        @pl.when(me == owner(k))
        def _():
            act(hop(k, 1 - x, i, other, side))

        @pl.when((z >= zk) & (z < ends))
        def _():
            act(hop(k, x, i, up, me + 2))

        @pl.when((z <= zk) & (z > 0))
        def _():
            act(hop(k, x, i, down, me - 2))

        @pl.when(((z != zk) | (x == xk)) & ~((me == owner(k)) & lone(k)))
        def _():
            act(hop(k, x, i, across, side))

    def main(k, i):
        @pl.when(me != owner(k))
        def _():
            hop(k, x, i, up, side).wait_recv()

        sends(k, i, lambda copy: copy.start())

    def cross(k, i, o):
        to = partner if o == 0 else (my_row // 2 + o) % (R // 2) * 2 + (my_row + k) % 2
        return remote(panel.at[k, parity, i], cols.at[k, i], cross_send.at[k, i, o], cross_recv.at[k, i], {"row": to})

    def late(k, i):
        @pl.when(me != owner(k))
        def _():
            hop(k, 1 - x, i, up, side).wait_recv()

        @pl.when(behind(k))
        def _():
            hop(k, 1 - x, i, other, beside(k)).start()

        @pl.when(is_root)
        def _():
            for o in range(1, R // 2):
                cross(k, i, o).start()
            cross(k, i, 0).start()

    def relay(k, i):
        return remote(cols.at[k, i], cols.at[k, i], relay_send.at[k, i], cross_recv.at[k, i], {"row": partner})

    def direct(k):
        return ~near & ((my_row + root + k) % 2 == 0)

    def pass_on(k, i):
        @pl.when(direct(k))
        def _():
            relay(k, i).wait_recv()
            relay(k, i).start()

    tile = held.shape[-1]

    def settle(k, i):
        @pl.when(~direct(k) & ~is_root)
        def _():
            relay(k, i).wait_recv()

        at = pl.ds(pl.multiple_of(k * tile, tile), tile)
        top, rest = split(jnp.where(is_root, panel[k, parity, i], cols[k, i]))
        col_top[i, :, at] = top
        col_low[i, :, at] = rest

    def scale(i):
        rows = [jnp.concatenate([panel[k, q, i] for k in range(PANEL_T)], axis=1) for q in range(held.shape[0])]
        scaled = dot3(split(jnp.concatenate(rows, axis=0)), (inv_top[...], inv_low[...]), ((1,), (0,)))
        top, rest = split(scaled)
        row_top[i] = top
        row_low[i] = rest

    size = Bn - b0
    levels = 0
    for k in range(PANEL_T):
        levels = jnp.maximum(levels, jnp.maximum(hops(k, x), hops(k, 1 - x)))

    def body(t, _):
        g, k = t // PANEL_T, t % PANEL_T

        def turn(at, act, also=True):
            i = g - at

            @pl.when((i >= 0) & (i < size) & also)
            def _():
                act(b0 + i)

        here = hops(k, x)
        turn(here * size, lambda i: main(k, i))
        there = jnp.maximum(here, hops(k, 1 - x)) * size + LAG + (size + LAG) * (lone(k) & (me == beside(k))).astype(i32)
        turn(there, lambda i: late(k, i))
        turn(there + LAG, lambda i: pass_on(k, i))
        turn(there + 2 * LAG, lambda i: settle(k, i))
        turn(levels * size + 2 * LAG, scale, k == PANEL_T - 1)
        return 0

    lax.fori_loop(0, ((levels + 1) * size + 4 * LAG) * PANEL_T, body, 0)

    def drain(t, _):
        i, k = b0 + t // PANEL_T, t % PANEL_T
        sends(k, i, lambda copy: copy.wait_send())

        @pl.when(behind(k))
        def _():
            hop(k, 1 - x, i, other, beside(k)).wait_send()

        @pl.when(is_root)
        def _():
            for o in range(R // 2):
                cross(k, i, o).wait_send()

        @pl.when(direct(k))
        def _():
            relay(k, i).wait_send()

        return 0

    lax.fori_loop(0, (Bn - b0) * PANEL_T, drain, 0)


def gather_panel(first, b0, ident, held, *inverse):
    R = lax.axis_size("row")
    per, Bn, tile, _ = held.shape
    each = (PANEL_T, Bn)
    wide = PANEL_T * tile
    return tuple(pl.pallas_call(
        lambda *refs: panel_kernel(first, b0, *refs),
        in_specs=[VMEM] * 3,
        out_specs=[VMEM] * 4,
        out_shape=[jax.ShapeDtypeStruct((Bn, per * tile, wide), bf16)] * 2
        + [jax.ShapeDtypeStruct((Bn, tile, wide), bf16)] * 2,
        scratch_shapes=[pltpu.VMEM((PANEL_T,) + held.shape, f32), pltpu.VMEM(each + (tile, tile), f32)]
        + [DMA((PANEL_T, per, Bn))] + [DMA(each)] * 4 + [DMA, DMA(each + (R // 2,)), DMA(each), DMA(each)],
        compiler_params=pltpu.CompilerParams(collective_id=ident, has_side_effects=True, vmem_limit_bytes=ROOM),
        name=f"panel_{first}_{b0}",
    )(held, *inverse))


def final_kernel(bmap, start, parent, payload, row_top, row_low, col_top, col_low, out):
    step = pl.program_id(0)
    per, bcols = parent.shape[0], parent.shape[2]
    tile = parent.shape[4]
    S = payload.shape[0]
    group = bcols // S
    spot = Layout(bmap, S)
    R, C = spot.R, spot.C
    first_active = start[0] + PANEL_T

    u = lax.div(step, 2)
    first = spot.first_row(u)
    places = [step * per + p - first for p in range(per)]
    hits = [(d >= 0) & (d < per) for d in places]
    big_rows = [spot.row + (step * per + p) * R for p in range(per)]
    big_cols = [spot.col + b * C for b in range(bcols)]

    for b in range(bcols):
        s = b // group
        reached = (spot.first_col(s) == b) & (s <= u)
        for p in range(per):
            out[p, 0, b, 0] = parent[p, 0, b, 0]

            @pl.when(hits[p] & reached)
            def _():
                out[p, 0, b, 0] = parent[p, 0, b, 0] + payload[s, u * per + places[p]]

    for g in range(S):
        @pl.when((big_rows[-1] >= big_cols[g * group]) & (big_cols[g * group + group - 1] >= first_active))
        def _():
            pair = lambda ref: ref[g * group : (g + 1) * group].reshape(group * tile, -1)
            trailing = dot3((row_top[step], row_low[step]), (pair(col_top), pair(col_low)), ((1,), (1,)))
            for j in range(group):
                b = g * group + j
                for p in range(per):
                    active = (big_rows[p] >= big_cols[b]) & (big_cols[b] >= first_active)
                    part = trailing[p * tile : (p + 1) * tile, j * tile : (j + 1) * tile]
                    out[p, 0, b, 0] = out[p, 0, b, 0] - jnp.where(active, part, 0.0)


def finish(bmap, start, parent, payload, factors, per):
    rows, _, bcols, _, tile, _ = parent.shape
    whole = lambda a: pl.BlockSpec(a.shape, lambda i, m, t: (0,) * a.ndim, pipeline_mode=pl.Buffered(1))
    big = pl.BlockSpec((per, 1, bcols, 1, tile, tile), lambda i, m, t: (i, 0, 0, 0, 0, 0))
    flops = 6 * rows * tile * PANEL_T * tile * bcols * tile
    return pl.pallas_call(
        final_kernel,
        grid_spec=pltpu.PrefetchScalarGridSpec(
            num_scalar_prefetch=2,
            grid=(rows // per,),
            in_specs=[big, whole(payload)] + [whole(f) for f in factors],
            out_specs=big,
        ),
        out_shape=jax.ShapeDtypeStruct(parent.shape, f32),
        compiler_params=pltpu.CompilerParams(vmem_limit_bytes=ROOM),
        cost_estimate=pl.CostEstimate(flops=flops, bytes_accessed=10 * parent.size, transcendentals=0),
        name="finish",
    )(bmap, start, parent, payload, *factors)


def per_device(contribution, parent, row_basis, pivot_basis, ranks, block_map, panel_start, inverse):
    R, C = lax.axis_size("row"), lax.axis_size("col")
    S = contribution.shape[2]
    per = C // R
    shift = [block_map[u * C] - 2 * C * u for u in range(S)]

    ident = 2
    moved, all_piv, all_bas = [], [], []
    for s in range(S):
        branches = []
        for h in range(C):
            if s < GATHERS:
                branches.append(lambda *a, h=h, s=s, ident=ident: shift_columns(h, s, per, ident, *a))
                ident += 1
            else:
                pairs = [(d, (d + h) % C) for d in range(C)]
                branches.append(lambda v, p=pairs, h=h: lax.ppermute(v, "col", p) if h else v)
        if s < GATHERS:
            came, piv, bas = lax.switch(shift[s], branches, contribution, pivot_basis, row_basis)
            all_piv.append(piv)
            all_bas.append(bas)
        else:
            came = lax.switch(shift[s], branches, contribution[per * s :, 0, s, 0])
        moved.append(came)

    partial = products(block_map, all_piv, C, per)
    weights, landed, *halves = sum_and_rows(block_map, partial, inverse, moved, per)
    parent = pltpu.with_memory_space_constraint(parent, pltpu.HBM)
    payload, held = updates(block_map, panel_start, ranks, weights, all_bas, landed, parent, C, per)

    branches = []
    pairs = parent.shape[0] // (2 * per)
    for first in range(C):
        for b0 in range(0, pairs, 2):
            b0 += (first + PANEL_T) // C
            branches.append(lambda *v, first=first, b0=b0, ident=ident: gather_panel(first, b0, ident, *v))
            ident += 1
    start = panel_start[0]
    which = lax.rem(start, C) * (pairs // 2) + jnp.minimum(lax.div(start, 2 * C), pairs // 2 - 1)
    factors = lax.switch(which, branches, held, *halves)
    return finish(block_map, panel_start, parent, payload, factors, per)


def solution(mesh):
    placed = (
        P(None, "row", None, "col", None, None),
        P(None, "row", None, "col", None, None),
        P(None, "row", None, None),
        P(None, "row", None, "col"),
        P(),
        P(),
        P(),
        P(),
    )
    return jax.shard_map(
        per_device,
        mesh=mesh,
        in_specs=placed,
        out_specs=P(None, "row", None, "col", None, None),
        check_vma=False,
    )
```

```python
import jax
import jax.numpy as jnp
from jax import lax
from jax.experimental import pallas as pl
from jax.experimental.pallas import tpu as pltpu
from jax.sharding import PartitionSpec as P

PANEL_T = 4
f32 = jnp.float32
bf16 = jnp.bfloat16
i32 = jnp.int32
MESH = pl.DeviceIdType.MESH
DMA = pltpu.SemaphoreType.DMA
SMEM = pl.BlockSpec(memory_space=pltpu.SMEM)
VMEM = pl.BlockSpec(memory_space=pltpu.VMEM)
ANY = pl.BlockSpec(memory_space=pl.ANY)
HBM = pl.BlockSpec(memory_space=pltpu.HBM)
ROOM = 32 << 20
GATHERS = 2
LAG = 2
CHUNK = 1
STRIDE = 2


def split(x):
    top = x.astype(bf16)
    return top, (x - top.astype(f32)).astype(bf16)


def dot3(a, b, dims):
    (ah, al), (bh, bl) = a, b
    one = lambda p, q: lax.dot_general(p, q, (dims, ((), ())), preferred_element_type=f32)
    return one(ah, bh) + (one(ah, bl) + one(al, bh))


def ring_place(p, n):
    return jnp.where(p < n // 2, 2 * p, 2 * (n - 1 - p) + 1)


def ring_spot(me, n):
    return jnp.where(me % 2 == 0, me // 2, n - 1 - me // 2)


def greet(targets):
    barrier = pltpu.get_barrier_semaphore()
    for target in targets:
        pl.semaphore_signal(barrier, inc=1, device_id=target, device_id_type=MESH)
    pl.semaphore_wait(barrier, len(targets))


def remote(src, dst, send, recv, to):
    return pltpu.make_async_remote_copy(src, dst, send, recv, device_id=to, device_id_type=MESH)


class Layout:
    def __init__(self, bmap, blocks):
        self.map = bmap
        self.S = blocks
        self.R, self.C = lax.axis_size("row"), lax.axis_size("col")
        self.row, self.col = lax.axis_index("row"), lax.axis_index("col")

    def shift(self, u):
        return self.map[u * self.C] - 2 * self.C * u

    def src_row(self, u, row=None):
        row = self.row if row is None else row
        return lax.rem(row + self.C * self.R - self.shift(u), self.R)

    def src_col(self, s, col=None):
        col = self.col if col is None else col
        return lax.rem(col + self.C - self.shift(s), self.C)

    def first_row(self, u, row=None):
        return lax.div(2 * self.C * u + self.shift(u) + self.src_row(u, row), self.R)

    def first_col(self, s):
        return lax.div(2 * self.C * s + self.shift(s) + self.src_col(s), self.C)


def own_column(start, col, C, bcols):
    k = lax.rem(col - start + C * bcols, C)
    return jnp.minimum(lax.div(start + k, C), bcols - 1)


def shift_kernel(h, s, per, *refs):
    R, n = lax.axis_size("row"), lax.axis_size("col")
    me, my_col = lax.axis_index("row"), lax.axis_index("col")
    gather = s < GATHERS
    if gather:
        child, piv, bas, moved, all_piv, all_bas, send, recv, own_sem, d_send, d_recv, r_send, r_recv = refs
    else:
        child, moved, send, recv = refs
    blocks = moved.shape[0] // per
    pairs = R // 2
    other = me + 1 - 2 * (me % 2)

    signals = []
    if h:
        signals.append({"col": (my_col + n - h) % n})
    if gather:
        signals += [{"row": (me + k) % R} for k in range(1, R)]
    if signals:
        greet(signals)

    def part(i):
        src = child.at[pl.ds(per * (s + i), per), 0, s, 0]
        dst = moved.at[pl.ds(per * i, per)]
        if h:
            return remote(src, dst, send.at[i], recv.at[i], {"col": (my_col + h) % n})
        return pltpu.make_async_copy(src, dst, recv.at[i])

    if gather:
        half = piv.shape[0] // GATHERS
        cuts = [(src, dst, half * s + j * half // m, j * half // m, half // m)
                for src, dst, m in ((piv, all_piv, 2), (bas, all_bas, 1)) for j in range(m)]

        def direct(o, j):
            src, dst, a, b, size = cuts[j]
            to = other if o == 0 else (me // 2 + o) % pairs * 2 + me % 2
            return remote(src.at[pl.ds(a, size), 0], dst.at[me, pl.ds(b, size)], d_send.at[o, j], d_recv.at[o, j],
                          {"row": to})

        def relay(o, j):
            _, dst, _, b, size = cuts[j]
            d = (me // 2 - o + pairs) % pairs * 2 + me % 2
            return remote(dst.at[d, pl.ds(b, size)], dst.at[d, pl.ds(b, size)], r_send.at[o, j], r_recv.at[o, j],
                          {"row": other})

        away = [(o, j) for j in range(len(cuts)) for o in range(1, pairs)]
        near = [(0, j) for j in range(len(cuts))]
        for o, j in away:
            direct(o, j).start()
    for i in range(blocks):
        part(i).start()
    if gather:
        own = [pltpu.make_async_copy(src.at[pl.ds(half * s, half), 0], dst.at[me], own_sem.at[j])
               for j, (src, dst) in enumerate(((piv, all_piv), (bas, all_bas)))]
        for copy in own:
            copy.start()
        for o, j in near:
            direct(o, j).start()
        for o, j in away:
            direct(o, j).wait_recv()
            relay(o, j).start()
        for o, j in near:
            direct(o, j).wait_recv()
        for o, j in away:
            relay(o, j).wait_recv()
            relay(o, j).wait_send()
        for o, j in away + near:
            direct(o, j).wait_send()
        for copy in own:
            copy.wait()
    for i in range(blocks):
        if h:
            part(i).wait_recv()
            part(i).wait_send()
        else:
            part(i).wait()


def shift_columns(h, s, per, ident, child, *factors):
    R = lax.axis_size("row")
    T, tile = child.shape[0], child.shape[-1]
    blocks = T // per - s
    moved = jax.ShapeDtypeStruct((per * blocks, tile, tile), f32)
    remote_ids = bool(h) or bool(factors)
    params = (
        pltpu.CompilerParams(collective_id=ident, has_side_effects=True, vmem_limit_bytes=ROOM)
        if remote_ids
        else pltpu.CompilerParams(vmem_limit_bytes=ROOM)
    )
    shapes, scratch = [moved], [DMA((blocks,)), DMA((blocks,))]
    if factors:
        shapes += [jax.ShapeDtypeStruct((R,) + (f.shape[0] // GATHERS,) + f.shape[2:], f32) for f in factors]
        scratch += [DMA((2,))] + [DMA((R // 2, 3))] * 4
    out = pl.pallas_call(
        lambda *refs: shift_kernel(h, s, per, *refs),
        in_specs=[ANY] * (1 + len(factors)),
        out_specs=[VMEM] * len(shapes),
        out_shape=shapes,
        scratch_shapes=scratch,
        compiler_params=params,
        name=f"shift_{s}_{h}",
    )(child, *factors)
    return tuple(out)


def product_kernel(per, S, bmap, *refs):
    everyone, (out, mine_top, mine_low, their_top, their_low) = refs[:GATHERS], refs[GATHERS:]
    part = everyone[0].shape[1]
    rank = everyone[0].shape[2]
    T = part * GATHERS
    R, C = lax.axis_size("row"), out.shape[0]
    spot = Layout(bmap, S)
    for t in range(T):
        top, low = split(everyone[t // part][spot.src_row(t // per), t % part])
        mine_top[t * rank : (t + 1) * rank, :] = top
        mine_low[t * rank : (t + 1) * rank, :] = low
    at = 0
    for s in range(S):
        for c in range(C):
            src = spot.src_col(s, c)
            top, low = split(everyone[s * per // part][lax.rem(src, R), s * per % part + lax.div(src, R)])
            their_top[c * rank : (c + 1) * rank, :] = top
            their_low[c * rank : (c + 1) * rank, :] = low
        first = s * per * rank
        size = T * rank - first
        mine = (mine_top[first:, :], mine_low[first:, :])
        got = dot3((their_top[...], their_low[...]), mine, ((1,), (1,)))
        out[:, :, at : at + size] = got.reshape(C, rank, size)
        at += size


def products(bmap, everyone, C, per):
    R, part, rank, width = everyone[0].shape
    T = part * GATHERS
    S = T // per
    total = sum((S - s) * per * rank for s in range(S))
    return pl.pallas_call(
        lambda *refs: product_kernel(per, S, *refs),
        in_specs=[SMEM] + [VMEM] * GATHERS,
        out_specs=VMEM,
        out_shape=jax.ShapeDtypeStruct((C, rank, total), f32),
        scratch_shapes=[pltpu.VMEM((T * rank, width), bf16)] * 2 + [pltpu.VMEM((C * rank, width), bf16)] * 2,
        compiler_params=pltpu.CompilerParams(vmem_limit_bytes=ROOM),
        name="products",
    )(bmap, *everyone)


PARTS = 4


def sum_kernel(per, bmap, partial, inverse, *refs):
    S = len(refs) - 11
    moved = refs[:S]
    out, landed, inv_top, inv_low, slots, outbox, send, recv, row_send, row_recv, own_sem = refs[S:]
    R, n = lax.axis_size("row"), lax.axis_size("col")
    my_row, me = lax.axis_index("row"), lax.axis_index("col")
    chunk = partial.shape[1] // (2 * PARTS)
    pos = ring_spot(me, n)
    right = ring_place((pos + 1) % n, n)
    left = ring_place((pos + n - 1) % n, n)
    greet([{"col": left}, {"col": right}] + [{"row": (my_row + k) % R} for k in range(1, R)])
    rows = lambda side, h: pl.ds((PARTS * side + h) * chunk, chunk)

    def part(side, k, h):
        q = (pos - 1 - k + n) % n if side == 0 else (pos + 1 + k) % n
        return partial.at[ring_place(q, n), rows(side, h)]

    def hop(side, k, h):
        src = part(side, 0, h) if k == 0 else slots.at[side, k - 1, h]
        return remote(src, slots.at[side, k, h], send.at[side, k, h], recv.at[side, k, h],
                      {"col": right if side == 0 else left})

    def cross(k):
        return remote(outbox.at[k - 1], landed.at[k], row_send.at[k - 1], row_recv.at[k - 1], {"row": (my_row + k) % R})

    for h in range(PARTS):
        for side in range(2):
            hop(side, 0, h).start()

    spot = Layout(bmap, S)
    for k in [R // 2] + [k for k in range(R) if k != R // 2]:
        block = sum(u * (lax.rem(spot.shift(u), R) == k).astype(i32) for u in range(S))
        for s in range(S):
            place = jnp.clip(block - s, 0, S - 1 - s)
            for p in range(per):
                tile = moved[s][place * per + p]
                if k == 0:
                    landed[0, s, p] = tile
                else:
                    outbox[k - 1, s, p] = tile
        if k:
            cross(k).start()

    top, rest = split(inverse[...])
    inv_top[...] = top
    inv_low[...] = rest

    every = [(k, h, side) for k in range(n - 1) for h in range(PARTS) for side in range(2)]
    for k, h, side in every:
        if k > 0:
            hop(side, k - 1, h).wait_recv()
            slots[side, k - 1, h] = slots[side, k - 1, h] + part(side, k, h)[...]
            hop(side, k, h).start()
    for h in range(PARTS):
        for side in range(2):
            hop(side, n - 2, h).wait_recv()
            out[rows(side, h), :] = slots[side, n - 2, h] + partial[me, rows(side, h), :]
    for k in range(1, R):
        cross(k).wait_recv()
        cross(k).wait_send()
    for k, h, side in every:
        hop(side, k, h).wait_send()


def sum_and_rows(bmap, partial, inverse, moved, per):
    R = lax.axis_size("row")
    n, rank, total = partial.shape
    S, tile = len(moved), moved[0].shape[-1]
    box = (S, per, tile, tile)
    return pl.pallas_call(
        lambda *refs: sum_kernel(per, *refs),
        in_specs=[SMEM] + [VMEM] * (2 + S),
        out_specs=[VMEM] * 4,
        out_shape=[jax.ShapeDtypeStruct((rank, total), f32), jax.ShapeDtypeStruct((R,) + box, f32)]
        + [jax.ShapeDtypeStruct(inverse.shape, bf16)] * 2,
        scratch_shapes=[
            pltpu.VMEM((2, n - 1, PARTS, rank // (2 * PARTS), total), f32),
            pltpu.VMEM((R - 1,) + box, f32),
            DMA((2, n - 1, PARTS)), DMA((2, n - 1, PARTS)), DMA((R - 1,)), DMA((R - 1,)), DMA,
        ],
        compiler_params=pltpu.CompilerParams(collective_id=1, has_side_effects=True, vmem_limit_bytes=ROOM),
        name="sum_and_rows",
    )(bmap, partial, inverse, *moved)


def update_kernel(per, C, bmap, start, ranks, weights, *refs):
    bases, (landed, parent, out, held, sems) = refs[:GATHERS], refs[GATHERS:]
    S, T, tile = out.shape[:3]
    R, part, rank, _ = bases[0].shape
    bcols = parent.shape[2]
    spot = Layout(bmap, S)
    b = own_column(start[0], spot.col, C, bcols)
    copies = []
    for i in range(held.shape[1]):
        for q in range(per):
            copies.append(pltpu.make_async_copy(parent.at[per * i + q, 0, b, 0], held.at[q, i], sems.at[q, i]))
            copies[-1].start()

    depth = lax.broadcasted_iota(i32, (rank, tile), 0)

    def basis(row, block, p):
        t = block * per + p
        return split(jnp.where(depth < ranks[t * R + row], bases[block * per // part][row, block * per % part + p], 0.0))

    at = 0
    for s in range(S):
        size = (S - s) * per * rank
        src = spot.src_col(s)
        j = s * C + src
        col_basis = basis(lax.rem(src, R), s, lax.div(src, R))
        half = dot3(split(weights[:, at : at + size]), col_basis, ((0,), (0,)))
        at += size
        for t in range(s * per, T):
            u, p = t // per, t % per
            i = t - s * per
            row = spot.src_row(u)
            update = dot3(basis(row, u, p), split(half[i * rank : (i + 1) * rank]), ((0,), (0,)))
            moved = landed[lax.rem(spot.shift(u), R), s, p]
            out[s, t] = jnp.where(t * R + row >= j, moved - update, 0.0)

    s_own = lax.div(b, bcols // S)
    reached = spot.first_col(s_own) == b
    for copy in copies:
        copy.wait()

    @pl.when(reached)
    def _():
        for u in range(S):
            @pl.when(s_own <= u)
            def _():
                for p in range(per):
                    a = spot.first_row(u) + p
                    q, i = lax.rem(a, per), lax.div(a, per)
                    held[q, i] = held[q, i] + out[s_own, u * per + p]


def updates(bmap, start, ranks, weights, bases, landed, parent, C, per):
    R, part, rank, tile = bases[0].shape
    T, rows = part * GATHERS, parent.shape[0]
    S = T // per
    return pl.pallas_call(
        lambda *refs: update_kernel(per, C, *refs),
        in_specs=[SMEM] * 3 + [VMEM] * (2 + GATHERS) + [HBM],
        out_specs=[VMEM, VMEM],
        out_shape=[
            jax.ShapeDtypeStruct((S, T, tile, tile), f32),
            jax.ShapeDtypeStruct((per, rows // per, tile, tile), f32),
        ],
        scratch_shapes=[DMA((per, rows // per))],
        compiler_params=pltpu.CompilerParams(vmem_limit_bytes=ROOM),
        name="updates",
    )(bmap, start, ranks, weights, *bases, landed, parent)


def panel_kernel(first, b0, held, inv_top, inv_low, row_top, row_low, col_top, col_low, panel, cols, recv, up, down, across,
                 other, own_sem, cross_send, cross_recv, relay_send):
    R, n = lax.axis_size("row"), lax.axis_size("col")
    my_row, me = lax.axis_index("row"), lax.axis_index("col")
    Bn = held.shape[1]
    z, x, ends = me // 2, me % 2, n // 2 - 1
    side = me + 1 - 2 * x
    root, parity = me % R, me // R
    is_root = my_row == root
    partner = my_row + 1 - 2 * (my_row % 2)
    near = my_row // 2 == root // 2
    owner = lambda k: (first + k) % n
    c = CHUNK if (Bn - b0) % CHUNK == 0 else 1

    def lone(k):
        return ((k == 0) | (k == PANEL_T - 1)) & (first % 2 == 1)

    def beside(k):
        return owner(k) + 1 - 2 * (owner(k) % 2)

    def behind(k):
        return lone(k) & (me == jnp.where(beside(k) < 2, beside(k) + 2, beside(k) - 2))

    def hops(k, lane):
        zk, xk = owner(k) // 2, owner(k) % 2
        return jnp.maximum(z - zk, zk - z) + (lane + xk) % 2

    barrier = pltpu.get_barrier_semaphore()
    for k in range(1, R):
        pl.semaphore_signal(barrier, inc=1, device_id={"row": (my_row + k) % R}, device_id_type=MESH)
    pl.semaphore_signal(barrier, inc=1, device_id={"col": side}, device_id_type=MESH)

    @pl.when(z > 0)
    def _():
        pl.semaphore_signal(barrier, inc=1, device_id={"col": me - 2}, device_id_type=MESH)

    @pl.when(z < ends)
    def _():
        pl.semaphore_signal(barrier, inc=1, device_id={"col": me + 2}, device_id_type=MESH)

    for k in range(PANEL_T):
        @pl.when(me == owner(k))
        def _():
            pltpu.make_async_copy(held, panel.at[k], own_sem).start()

    pl.semaphore_wait(barrier, R + jnp.minimum(z, 1) + jnp.minimum(ends - z, 1))

    for k in range(PANEL_T):
        @pl.when(me == owner(k))
        def _():
            pltpu.make_async_copy(held, panel.at[k], own_sem).wait()

    def hop(k, h, i, sem, to):
        ref = panel.at[k, h, pl.ds(i, c)]
        return remote(ref, ref, sem.at[k, i], recv.at[k, h, i], {"col": to})

    def sends(k, i, act):
        zk = owner(k) // 2

        @pl.when(me == owner(k))
        def _():
            act(hop(k, 1 - x, i, other, side))

        @pl.when((z >= zk) & (z < ends))
        def _():
            act(hop(k, x, i, up, me + 2))

        @pl.when((z <= zk) & (z > 0))
        def _():
            act(hop(k, x, i, down, me - 2))

    def swaps(k, i, act):
        @pl.when(((z != owner(k) // 2) | (x == owner(k) % 2)) & ~((me == owner(k)) & lone(k)))
        def _():
            act(hop(k, x, i, across, side))

    def main(k, i):
        @pl.when(me != owner(k))
        def _():
            hop(k, x, i, up, side).wait_recv()

        sends(k, i, lambda copy: copy.start())
        swaps(k, i, lambda copy: copy.start())

    def cross(k, i, o):
        to = partner if o == 0 else (my_row // 2 + o) % (R // 2) * 2 + (my_row + k) % 2
        return remote(panel.at[k, parity, pl.ds(i, c)], cols.at[k, pl.ds(i, c)], cross_send.at[k, i, o], cross_recv.at[k, i], {"row": to})

    def late(k, i):
        @pl.when(me != owner(k))
        def _():
            hop(k, 1 - x, i, up, side).wait_recv()

        @pl.when(behind(k))
        def _():
            hop(k, 1 - x, i, other, beside(k)).start()

        @pl.when(is_root)
        def _():
            for o in range(1, R // 2):
                cross(k, i, o).start()
            cross(k, i, 0).start()

    def relay(k, i):
        return remote(cols.at[k, pl.ds(i, c)], cols.at[k, pl.ds(i, c)], relay_send.at[k, i], cross_recv.at[k, i], {"row": partner})

    def direct(k):
        return ~near & ((my_row + root + k) % 2 == 0)

    def pass_on(k, i):
        @pl.when(direct(k))
        def _():
            relay(k, i).wait_recv()
            relay(k, i).start()

    tile = held.shape[-1]

    def settle(k, i):
        @pl.when(~direct(k) & ~is_root)
        def _():
            relay(k, i).wait_recv()

        at = pl.ds(pl.multiple_of(k * tile, tile), tile)
        for j in range(c):
            top, rest = split(jnp.where(is_root, panel[k, parity, i + j], cols[k, i + j]))
            col_top[i + j, :, at] = top
            col_low[i + j, :, at] = rest

    def scale(start):
        lax.fori_loop(start, start + c, scale_one, 0)

    def scale_one(i, _):
        rows = [jnp.concatenate([panel[k, q, i] for k in range(PANEL_T)], axis=1) for q in range(held.shape[0])]
        scaled = dot3(split(jnp.concatenate(rows, axis=0)), (inv_top[...], inv_low[...]), ((1,), (0,)))
        top, rest = split(scaled)
        row_top[i] = top
        row_low[i] = rest
        return 0

    size = (Bn - b0) // c
    levels = 0
    for k in range(PANEL_T):
        levels = jnp.maximum(levels, jnp.maximum(hops(k, x), hops(k, 1 - x)))

    def body(t, _):
        g, k = t // PANEL_T, t % PANEL_T

        def turn(at, act, also=True):
            i = g - at

            @pl.when((i >= 0) & (i < size) & also)
            def _():
                act(b0 + i * c)

        here = hops(k, x)
        turn(here * STRIDE, lambda i: main(k, i))
        there = jnp.maximum(here, hops(k, 1 - x)) * STRIDE + LAG + (STRIDE + LAG) * (lone(k) & (me == beside(k))).astype(i32)
        turn(there, lambda i: late(k, i))
        turn(there + LAG, lambda i: pass_on(k, i))
        turn(there + 2 * LAG, lambda i: settle(k, i))
        turn(levels * STRIDE + 2 * LAG, scale, k == PANEL_T - 1)
        return 0

    lax.fori_loop(0, (levels * STRIDE + size + 4 * LAG) * PANEL_T, body, 0)

    def drain(t, _):
        i, k = b0 + t // PANEL_T * c, t % PANEL_T
        sends(k, i, lambda copy: copy.wait_send())
        swaps(k, i, lambda copy: copy.wait_send())

        @pl.when(behind(k))
        def _():
            hop(k, 1 - x, i, other, beside(k)).wait_send()

        @pl.when(is_root)
        def _():
            for o in range(R // 2):
                cross(k, i, o).wait_send()

        @pl.when(direct(k))
        def _():
            relay(k, i).wait_send()

        return 0

    lax.fori_loop(0, size * PANEL_T, drain, 0)


def gather_panel(first, b0, ident, held, *inverse):
    R = lax.axis_size("row")
    per, Bn, tile, _ = held.shape
    each = (PANEL_T, Bn)
    wide = PANEL_T * tile
    return tuple(pl.pallas_call(
        lambda *refs: panel_kernel(first, b0, *refs),
        in_specs=[VMEM] * 3,
        out_specs=[VMEM] * 4,
        out_shape=[jax.ShapeDtypeStruct((Bn, per * tile, wide), bf16)] * 2
        + [jax.ShapeDtypeStruct((Bn, tile, wide), bf16)] * 2,
        scratch_shapes=[pltpu.VMEM((PANEL_T,) + held.shape, f32), pltpu.VMEM(each + (tile, tile), f32)]
        + [DMA((PANEL_T, per, Bn))] + [DMA(each)] * 4 + [DMA, DMA(each + (R // 2,)), DMA(each), DMA(each)],
        compiler_params=pltpu.CompilerParams(collective_id=ident, has_side_effects=True, vmem_limit_bytes=ROOM),
        name=f"panel_{first}_{b0}",
    )(held, *inverse))


def final_kernel(bmap, start, parent, payload, row_top, row_low, col_top, col_low, out):
    step = pl.program_id(0)
    per, bcols = parent.shape[0], parent.shape[2]
    tile = parent.shape[4]
    S = payload.shape[0]
    group = bcols // S
    spot = Layout(bmap, S)
    R, C = spot.R, spot.C
    first_active = start[0] + PANEL_T

    u = lax.div(step, 2)
    first = spot.first_row(u)
    places = [step * per + p - first for p in range(per)]
    hits = [(d >= 0) & (d < per) for d in places]
    big_rows = [spot.row + (step * per + p) * R for p in range(per)]
    big_cols = [spot.col + b * C for b in range(bcols)]

    for b in range(bcols):
        s = b // group
        reached = (spot.first_col(s) == b) & (s <= u)
        for p in range(per):
            out[p, 0, b, 0] = parent[p, 0, b, 0]

            @pl.when(hits[p] & reached)
            def _():
                out[p, 0, b, 0] = parent[p, 0, b, 0] + payload[s, u * per + places[p]]

    for g in range(S):
        @pl.when((big_rows[-1] >= big_cols[g * group]) & (big_cols[g * group + group - 1] >= first_active))
        def _():
            pair = lambda ref: ref[g * group : (g + 1) * group].reshape(group * tile, -1)
            trailing = dot3((row_top[step], row_low[step]), (pair(col_top), pair(col_low)), ((1,), (1,)))
            for j in range(group):
                b = g * group + j
                for p in range(per):
                    active = (big_rows[p] >= big_cols[b]) & (big_cols[b] >= first_active)
                    part = trailing[p * tile : (p + 1) * tile, j * tile : (j + 1) * tile]
                    out[p, 0, b, 0] = out[p, 0, b, 0] - jnp.where(active, part, 0.0)


def finish(bmap, start, parent, payload, factors, per):
    rows, _, bcols, _, tile, _ = parent.shape
    whole = lambda a: pl.BlockSpec(a.shape, lambda i, m, t: (0,) * a.ndim, pipeline_mode=pl.Buffered(1))
    big = pl.BlockSpec((per, 1, bcols, 1, tile, tile), lambda i, m, t: (i, 0, 0, 0, 0, 0))
    flops = 6 * rows * tile * PANEL_T * tile * bcols * tile
    return pl.pallas_call(
        final_kernel,
        grid_spec=pltpu.PrefetchScalarGridSpec(
            num_scalar_prefetch=2,
            grid=(rows // per,),
            in_specs=[big, whole(payload)] + [whole(f) for f in factors],
            out_specs=big,
        ),
        out_shape=jax.ShapeDtypeStruct(parent.shape, f32),
        compiler_params=pltpu.CompilerParams(vmem_limit_bytes=ROOM),
        cost_estimate=pl.CostEstimate(flops=flops, bytes_accessed=10 * parent.size, transcendentals=0),
        name="finish",
    )(bmap, start, parent, payload, *factors)


def per_device(contribution, parent, row_basis, pivot_basis, ranks, block_map, panel_start, inverse):
    R, C = lax.axis_size("row"), lax.axis_size("col")
    S = contribution.shape[2]
    per = C // R
    shift = [block_map[u * C] - 2 * C * u for u in range(S)]

    ident = 2
    moved, all_piv, all_bas = [], [], []
    for s in range(S):
        branches = []
        for h in range(C):
            if s < GATHERS:
                branches.append(lambda *a, h=h, s=s, ident=ident: shift_columns(h, s, per, ident, *a))
                ident += 1
            else:
                pairs = [(d, (d + h) % C) for d in range(C)]
                branches.append(lambda v, p=pairs, h=h: lax.ppermute(v, "col", p) if h else v)
        if s < GATHERS:
            came, piv, bas = lax.switch(shift[s], branches, contribution, pivot_basis, row_basis)
            all_piv.append(piv)
            all_bas.append(bas)
        else:
            came = lax.switch(shift[s], branches, contribution[per * s :, 0, s, 0])
        moved.append(came)

    partial = products(block_map, all_piv, C, per)
    weights, landed, *halves = sum_and_rows(block_map, partial, inverse, moved, per)
    parent = pltpu.with_memory_space_constraint(parent, pltpu.HBM)
    payload, held = updates(block_map, panel_start, ranks, weights, all_bas, landed, parent, C, per)

    branches = []
    pairs = parent.shape[0] // (2 * per)
    for first in range(C):
        for b0 in range(0, pairs, 2):
            b0 += (first + PANEL_T) // C
            branches.append(lambda *v, first=first, b0=b0, ident=ident: gather_panel(first, b0, ident, *v))
            ident += 1
    start = panel_start[0]
    which = lax.rem(start, C) * (pairs // 2) + jnp.minimum(lax.div(start, 2 * C), pairs // 2 - 1)
    factors = lax.switch(which, branches, held, *halves)
    return finish(block_map, panel_start, parent, payload, factors, per)


def solution(mesh):
    placed = (
        P(None, "row", None, "col", None, None),
        P(None, "row", None, "col", None, None),
        P(None, "row", None, None),
        P(None, "row", None, "col"),
        P(),
        P(),
        P(),
        P(),
    )
    return jax.shard_map(
        per_device,
        mesh=mesh,
        in_specs=placed,
        out_specs=P(None, "row", None, "col", None, None),
        check_vma=False,
    )
```

```python
import jax
import jax.numpy as jnp
from jax import lax
from jax.experimental import pallas as pl
from jax.experimental.pallas import tpu as pltpu
from jax.sharding import PartitionSpec as P

PANEL_T = 4
f32 = jnp.float32
bf16 = jnp.bfloat16
i32 = jnp.int32
MESH = pl.DeviceIdType.MESH
DMA = pltpu.SemaphoreType.DMA
SMEM = pl.BlockSpec(memory_space=pltpu.SMEM)
VMEM = pl.BlockSpec(memory_space=pltpu.VMEM)
ANY = pl.BlockSpec(memory_space=pl.ANY)
HBM = pl.BlockSpec(memory_space=pltpu.HBM)
ROOM = 32 << 20
GATHERS = 1
LAG = 2
CHUNK = 1
STRIDE = 2


def split(x):
    top = x.astype(bf16)
    return top, (x - top.astype(f32)).astype(bf16)


def dot3(a, b, dims):
    (ah, al), (bh, bl) = a, b
    one = lambda p, q: lax.dot_general(p, q, (dims, ((), ())), preferred_element_type=f32)
    return one(ah, bh) + (one(ah, bl) + one(al, bh))


def ring_place(p, n):
    return jnp.where(p < n // 2, 2 * p, 2 * (n - 1 - p) + 1)


def ring_spot(me, n):
    return jnp.where(me % 2 == 0, me // 2, n - 1 - me // 2)


def greet(targets):
    barrier = pltpu.get_barrier_semaphore()
    for target in targets:
        pl.semaphore_signal(barrier, inc=1, device_id=target, device_id_type=MESH)
    pl.semaphore_wait(barrier, len(targets))


def remote(src, dst, send, recv, to):
    return pltpu.make_async_remote_copy(src, dst, send, recv, device_id=to, device_id_type=MESH)


class Layout:
    def __init__(self, bmap, blocks):
        self.map = bmap
        self.S = blocks
        self.R, self.C = lax.axis_size("row"), lax.axis_size("col")
        self.row, self.col = lax.axis_index("row"), lax.axis_index("col")

    def shift(self, u):
        return self.map[u * self.C] - 2 * self.C * u

    def src_row(self, u, row=None):
        row = self.row if row is None else row
        return lax.rem(row + self.C * self.R - self.shift(u), self.R)

    def src_col(self, s, col=None):
        col = self.col if col is None else col
        return lax.rem(col + self.C - self.shift(s), self.C)

    def first_row(self, u, row=None):
        return lax.div(2 * self.C * u + self.shift(u) + self.src_row(u, row), self.R)

    def first_col(self, s):
        return lax.div(2 * self.C * s + self.shift(s) + self.src_col(s), self.C)


def own_column(start, col, C, bcols):
    k = lax.rem(col - start + C * bcols, C)
    return jnp.minimum(lax.div(start + k, C), bcols - 1)


def shift_kernel(h, s, per, *refs):
    R, n = lax.axis_size("row"), lax.axis_size("col")
    me, my_col = lax.axis_index("row"), lax.axis_index("col")
    gather = s < GATHERS
    if gather:
        child, piv, bas, moved, all_piv, all_bas, send, recv, own_sem, d_send, d_recv, r_send, r_recv = refs
    else:
        child, moved, send, recv = refs
    blocks = moved.shape[0] // per
    pairs = R // 2
    other = me + 1 - 2 * (me % 2)

    signals = []
    if h:
        signals.append({"col": (my_col + n - h) % n})
    if gather:
        signals += [{"row": (me + k) % R} for k in range(1, R)]
    if signals:
        greet(signals)

    def part(i):
        src = child.at[pl.ds(per * (s + i), per), 0, s, 0]
        dst = moved.at[pl.ds(per * i, per)]
        if h:
            return remote(src, dst, send.at[i], recv.at[i], {"col": (my_col + h) % n})
        return pltpu.make_async_copy(src, dst, recv.at[i])

    if gather:
        half = piv.shape[0] // GATHERS
        cuts = [(src, dst, half * s + j * half // m, j * half // m, half // m)
                for src, dst, m in ((piv, all_piv, 4), (bas, all_bas, 2)) for j in range(m)]

        def direct(o, j):
            src, dst, a, b, size = cuts[j]
            to = other if o == 0 else (me // 2 + o) % pairs * 2 + me % 2
            return remote(src.at[pl.ds(a, size), 0], dst.at[me, pl.ds(b, size)], d_send.at[o, j], d_recv.at[o, j],
                          {"row": to})

        def relay(o, j):
            _, dst, _, b, size = cuts[j]
            d = (me // 2 - o + pairs) % pairs * 2 + me % 2
            return remote(dst.at[d, pl.ds(b, size)], dst.at[d, pl.ds(b, size)], r_send.at[o, j], r_recv.at[o, j],
                          {"row": other})

        away = [(o, j) for j in range(len(cuts)) for o in range(1, pairs)]
        near = [(0, j) for j in range(len(cuts))]
        for o, j in away:
            direct(o, j).start()
    for i in range(blocks):
        part(i).start()
    if gather:
        own = [pltpu.make_async_copy(src.at[pl.ds(half * s, half), 0], dst.at[me], own_sem.at[j])
               for j, (src, dst) in enumerate(((piv, all_piv), (bas, all_bas)))]
        for copy in own:
            copy.start()
        for o, j in near:
            direct(o, j).start()
        for o, j in away:
            direct(o, j).wait_recv()
            relay(o, j).start()
        for o, j in near:
            direct(o, j).wait_recv()
        for o, j in away:
            relay(o, j).wait_recv()
            relay(o, j).wait_send()
        for o, j in away + near:
            direct(o, j).wait_send()
        for copy in own:
            copy.wait()
    for i in range(blocks):
        if h:
            part(i).wait_recv()
            part(i).wait_send()
        else:
            part(i).wait()


def shift_columns(h, s, per, ident, child, *factors):
    R = lax.axis_size("row")
    T, tile = child.shape[0], child.shape[-1]
    blocks = T // per - s
    moved = jax.ShapeDtypeStruct((per * blocks, tile, tile), f32)
    remote_ids = bool(h) or bool(factors)
    params = (
        pltpu.CompilerParams(collective_id=ident, has_side_effects=True, vmem_limit_bytes=ROOM)
        if remote_ids
        else pltpu.CompilerParams(vmem_limit_bytes=ROOM)
    )
    shapes, scratch = [moved], [DMA((blocks,)), DMA((blocks,))]
    if factors:
        shapes += [jax.ShapeDtypeStruct((R,) + (f.shape[0] // GATHERS,) + f.shape[2:], f32) for f in factors]
        scratch += [DMA((2,))] + [DMA((R // 2, 6))] * 4
    out = pl.pallas_call(
        lambda *refs: shift_kernel(h, s, per, *refs),
        in_specs=[ANY] * (1 + len(factors)),
        out_specs=[VMEM] * len(shapes),
        out_shape=shapes,
        scratch_shapes=scratch,
        compiler_params=params,
        name=f"shift_{s}_{h}",
    )(child, *factors)
    return tuple(out)


def product_kernel(per, S, bmap, *refs):
    everyone, (out, mine_top, mine_low, their_top, their_low) = refs[:GATHERS], refs[GATHERS:]
    part = everyone[0].shape[1]
    rank = everyone[0].shape[2]
    T = part * GATHERS
    R, C = lax.axis_size("row"), out.shape[0]
    spot = Layout(bmap, S)
    for t in range(T):
        top, low = split(everyone[t // part][spot.src_row(t // per), t % part])
        mine_top[t * rank : (t + 1) * rank, :] = top
        mine_low[t * rank : (t + 1) * rank, :] = low
    at = 0
    for s in range(S):
        for c in range(C):
            src = spot.src_col(s, c)
            top, low = split(everyone[s * per // part][lax.rem(src, R), s * per % part + lax.div(src, R)])
            their_top[c * rank : (c + 1) * rank, :] = top
            their_low[c * rank : (c + 1) * rank, :] = low
        first = s * per * rank
        size = T * rank - first
        mine = (mine_top[first:, :], mine_low[first:, :])
        got = dot3((their_top[...], their_low[...]), mine, ((1,), (1,)))
        out[:, :, at : at + size] = got.reshape(C, rank, size)
        at += size


def products(bmap, everyone, C, per):
    R, part, rank, width = everyone[0].shape
    T = part * GATHERS
    S = T // per
    total = sum((S - s) * per * rank for s in range(S))
    return pl.pallas_call(
        lambda *refs: product_kernel(per, S, *refs),
        in_specs=[SMEM] + [VMEM] * GATHERS,
        out_specs=VMEM,
        out_shape=jax.ShapeDtypeStruct((C, rank, total), f32),
        scratch_shapes=[pltpu.VMEM((T * rank, width), bf16)] * 2 + [pltpu.VMEM((C * rank, width), bf16)] * 2,
        compiler_params=pltpu.CompilerParams(vmem_limit_bytes=ROOM),
        name="products",
    )(bmap, *everyone)


PARTS = 4


def sum_kernel(per, bmap, partial, inverse, *refs):
    S = len(refs) - 11
    moved = refs[:S]
    out, landed, inv_top, inv_low, slots, outbox, send, recv, row_send, row_recv, own_sem = refs[S:]
    R, n = lax.axis_size("row"), lax.axis_size("col")
    my_row, me = lax.axis_index("row"), lax.axis_index("col")
    chunk = partial.shape[1] // (2 * PARTS)
    pos = ring_spot(me, n)
    right = ring_place((pos + 1) % n, n)
    left = ring_place((pos + n - 1) % n, n)
    greet([{"col": left}, {"col": right}] + [{"row": (my_row + k) % R} for k in range(1, R)])
    rows = lambda side, h: pl.ds((PARTS * side + h) * chunk, chunk)

    def part(side, k, h):
        q = (pos - 1 - k + n) % n if side == 0 else (pos + 1 + k) % n
        return partial.at[ring_place(q, n), rows(side, h)]

    def hop(side, k, h):
        src = part(side, 0, h) if k == 0 else slots.at[side, k - 1, h]
        return remote(src, slots.at[side, k, h], send.at[side, k, h], recv.at[side, k, h],
                      {"col": right if side == 0 else left})

    def cross(k):
        return remote(outbox.at[k - 1], landed.at[k], row_send.at[k - 1], row_recv.at[k - 1], {"row": (my_row + k) % R})

    for h in range(PARTS):
        for side in range(2):
            hop(side, 0, h).start()

    spot = Layout(bmap, S)
    for k in [R // 2] + [k for k in range(R) if k != R // 2]:
        block = sum(u * (lax.rem(spot.shift(u), R) == k).astype(i32) for u in range(S))
        for s in range(S):
            place = jnp.clip(block - s, 0, S - 1 - s)
            for p in range(per):
                tile = moved[s][place * per + p]
                if k == 0:
                    landed[0, s, p] = tile
                else:
                    outbox[k - 1, s, p] = tile
        if k:
            cross(k).start()

    top, rest = split(inverse[...])
    inv_top[...] = top
    inv_low[...] = rest

    every = [(k, h, side) for k in range(n - 1) for h in range(PARTS) for side in range(2)]
    for k, h, side in every:
        if k > 0:
            hop(side, k - 1, h).wait_recv()
            slots[side, k - 1, h] = slots[side, k - 1, h] + part(side, k, h)[...]
            hop(side, k, h).start()
    for h in range(PARTS):
        for side in range(2):
            hop(side, n - 2, h).wait_recv()
            out[rows(side, h), :] = slots[side, n - 2, h] + partial[me, rows(side, h), :]
    for k in range(1, R):
        cross(k).wait_recv()
        cross(k).wait_send()
    for k, h, side in every:
        hop(side, k, h).wait_send()


def sum_and_rows(bmap, partial, inverse, moved, per):
    R = lax.axis_size("row")
    n, rank, total = partial.shape
    S, tile = len(moved), moved[0].shape[-1]
    box = (S, per, tile, tile)
    return pl.pallas_call(
        lambda *refs: sum_kernel(per, *refs),
        in_specs=[SMEM] + [VMEM] * (2 + S),
        out_specs=[VMEM] * 4,
        out_shape=[jax.ShapeDtypeStruct((rank, total), f32), jax.ShapeDtypeStruct((R,) + box, f32)]
        + [jax.ShapeDtypeStruct(inverse.shape, bf16)] * 2,
        scratch_shapes=[
            pltpu.VMEM((2, n - 1, PARTS, rank // (2 * PARTS), total), f32),
            pltpu.VMEM((R - 1,) + box, f32),
            DMA((2, n - 1, PARTS)), DMA((2, n - 1, PARTS)), DMA((R - 1,)), DMA((R - 1,)), DMA,
        ],
        compiler_params=pltpu.CompilerParams(collective_id=1, has_side_effects=True, vmem_limit_bytes=ROOM),
        name="sum_and_rows",
    )(bmap, partial, inverse, *moved)


def update_kernel(per, C, bmap, start, ranks, weights, *refs):
    bases, (landed, parent, out, held, sems) = refs[:GATHERS], refs[GATHERS:]
    S, T, tile = out.shape[:3]
    R, part, rank, _ = bases[0].shape
    bcols = parent.shape[2]
    spot = Layout(bmap, S)
    b = own_column(start[0], spot.col, C, bcols)
    copies = []
    for i in range(held.shape[1]):
        for q in range(per):
            copies.append(pltpu.make_async_copy(parent.at[per * i + q, 0, b, 0], held.at[q, i], sems.at[q, i]))
            copies[-1].start()

    depth = lax.broadcasted_iota(i32, (rank, tile), 0)

    def basis(row, block, p):
        t = block * per + p
        return split(jnp.where(depth < ranks[t * R + row], bases[block * per // part][row, block * per % part + p], 0.0))

    at = 0
    for s in range(S):
        size = (S - s) * per * rank
        src = spot.src_col(s)
        j = s * C + src
        col_basis = basis(lax.rem(src, R), s, lax.div(src, R))
        half = dot3(split(weights[:, at : at + size]), col_basis, ((0,), (0,)))
        at += size
        for t in range(s * per, T):
            u, p = t // per, t % per
            i = t - s * per
            row = spot.src_row(u)
            update = dot3(basis(row, u, p), split(half[i * rank : (i + 1) * rank]), ((0,), (0,)))
            moved = landed[lax.rem(spot.shift(u), R), s, p]
            out[s, t] = jnp.where(t * R + row >= j, moved - update, 0.0)

    s_own = lax.div(b, bcols // S)
    reached = spot.first_col(s_own) == b
    for copy in copies:
        copy.wait()

    @pl.when(reached)
    def _():
        for u in range(S):
            @pl.when(s_own <= u)
            def _():
                for p in range(per):
                    a = spot.first_row(u) + p
                    q, i = lax.rem(a, per), lax.div(a, per)
                    held[q, i] = held[q, i] + out[s_own, u * per + p]


def updates(bmap, start, ranks, weights, bases, landed, parent, C, per):
    R, part, rank, tile = bases[0].shape
    T, rows = part * GATHERS, parent.shape[0]
    S = T // per
    return pl.pallas_call(
        lambda *refs: update_kernel(per, C, *refs),
        in_specs=[SMEM] * 3 + [VMEM] * (2 + GATHERS) + [HBM],
        out_specs=[VMEM, VMEM],
        out_shape=[
            jax.ShapeDtypeStruct((S, T, tile, tile), f32),
            jax.ShapeDtypeStruct((per, rows // per, tile, tile), f32),
        ],
        scratch_shapes=[DMA((per, rows // per))],
        compiler_params=pltpu.CompilerParams(vmem_limit_bytes=ROOM),
        name="updates",
    )(bmap, start, ranks, weights, *bases, landed, parent)


def panel_kernel(first, b0, held, inv_top, inv_low, factors, panel, cols, recv, up, down, across,
                 other, own_sem, cross_send, cross_recv, relay_send):
    R, n = lax.axis_size("row"), lax.axis_size("col")
    my_row, me = lax.axis_index("row"), lax.axis_index("col")
    Bn = held.shape[1]
    z, x, ends = me // 2, me % 2, n // 2 - 1
    side = me + 1 - 2 * x
    root, parity = me % R, me // R
    is_root = my_row == root
    partner = my_row + 1 - 2 * (my_row % 2)
    near = my_row // 2 == root // 2
    owner = lambda k: (first + k) % n
    c = CHUNK if (Bn - b0) % CHUNK == 0 else 1

    def lone(k):
        return ((k == 0) | (k == PANEL_T - 1)) & (first % 2 == 1)

    def beside(k):
        return owner(k) + 1 - 2 * (owner(k) % 2)

    def behind(k):
        return lone(k) & (me == jnp.where(beside(k) < 2, beside(k) + 2, beside(k) - 2))

    def hops(k, lane):
        zk, xk = owner(k) // 2, owner(k) % 2
        return jnp.maximum(z - zk, zk - z) + (lane + xk) % 2

    barrier = pltpu.get_barrier_semaphore()
    for k in range(1, R):
        pl.semaphore_signal(barrier, inc=1, device_id={"row": (my_row + k) % R}, device_id_type=MESH)
    pl.semaphore_signal(barrier, inc=1, device_id={"col": side}, device_id_type=MESH)

    @pl.when(z > 0)
    def _():
        pl.semaphore_signal(barrier, inc=1, device_id={"col": me - 2}, device_id_type=MESH)

    @pl.when(z < ends)
    def _():
        pl.semaphore_signal(barrier, inc=1, device_id={"col": me + 2}, device_id_type=MESH)

    for k in range(PANEL_T):
        @pl.when(me == owner(k))
        def _():
            pltpu.make_async_copy(held, panel.at[k], own_sem).start()

    pl.semaphore_wait(barrier, R + jnp.minimum(z, 1) + jnp.minimum(ends - z, 1))

    for k in range(PANEL_T):
        @pl.when(me == owner(k))
        def _():
            pltpu.make_async_copy(held, panel.at[k], own_sem).wait()

    def hop(k, h, i, sem, to):
        ref = panel.at[k, h, pl.ds(i, c)]
        return remote(ref, ref, sem.at[k, i], recv.at[k, h, i], {"col": to})

    def sends(k, i, act):
        zk = owner(k) // 2

        @pl.when(me == owner(k))
        def _():
            act(hop(k, 1 - x, i, other, side))

        @pl.when((z >= zk) & (z < ends))
        def _():
            act(hop(k, x, i, up, me + 2))

        @pl.when((z <= zk) & (z > 0))
        def _():
            act(hop(k, x, i, down, me - 2))

    def swaps(k, i, act):
        @pl.when(((z != owner(k) // 2) | (x == owner(k) % 2)) & ~((me == owner(k)) & lone(k)))
        def _():
            act(hop(k, x, i, across, side))

    def main(k, i):
        @pl.when(me != owner(k))
        def _():
            hop(k, x, i, up, side).wait_recv()

        sends(k, i, lambda copy: copy.start())
        swaps(k, i, lambda copy: copy.start())

    def cross(k, i, o):
        to = partner if o == 0 else (my_row // 2 + o) % (R // 2) * 2 + (my_row + k) % 2
        return remote(panel.at[k, parity, pl.ds(i, c)], cols.at[k, pl.ds(i, c)], cross_send.at[k, i, o], cross_recv.at[k, i], {"row": to})

    def late(k, i):
        @pl.when(me != owner(k))
        def _():
            hop(k, 1 - x, i, up, side).wait_recv()

        @pl.when(behind(k))
        def _():
            hop(k, 1 - x, i, other, beside(k)).start()

        @pl.when(is_root)
        def _():
            for o in range(1, R // 2):
                cross(k, i, o).start()
            cross(k, i, 0).start()

    def relay(k, i):
        return remote(cols.at[k, pl.ds(i, c)], cols.at[k, pl.ds(i, c)], relay_send.at[k, i], cross_recv.at[k, i], {"row": partner})

    def direct(k):
        return ~near & ((my_row + root + k) % 2 == 0)

    def pass_on(k, i):
        @pl.when(direct(k))
        def _():
            relay(k, i).wait_recv()
            relay(k, i).start()

    per, tile = held.shape[0], held.shape[-1]

    def settle(k, i):
        @pl.when(~direct(k) & ~is_root)
        def _():
            relay(k, i).wait_recv()

        at = pl.ds(pl.multiple_of(k * tile, tile), tile)
        for j in range(c):
            top, rest = split(jnp.where(is_root, panel[k, parity, i + j], cols[k, i + j]))
            factors[2 * per * Bn + i + j, :, at] = top
            factors[(2 * per + 1) * Bn + i + j, :, at] = rest

    def scale(start):
        lax.fori_loop(start, start + c, scale_one, 0)

    def scale_one(i, _):
        rows = [jnp.concatenate([panel[k, q, i] for k in range(PANEL_T)], axis=1) for q in range(held.shape[0])]
        scaled = dot3(split(jnp.concatenate(rows, axis=0)), (inv_top[...], inv_low[...]), ((1,), (0,)))
        top, rest = split(scaled)
        factors[pl.ds(per * i, per)] = top.reshape(per, tile, -1)
        factors[pl.ds(per * (Bn + i), per)] = rest.reshape(per, tile, -1)
        return 0

    size = (Bn - b0) // c
    levels = 0
    for k in range(PANEL_T):
        levels = jnp.maximum(levels, jnp.maximum(hops(k, x), hops(k, 1 - x)))

    def body(t, _):
        g, k = t // PANEL_T, t % PANEL_T

        def turn(at, act, also=True):
            i = g - at

            @pl.when((i >= 0) & (i < size) & also)
            def _():
                act(b0 + i * c)

        here = hops(k, x)
        turn(here * STRIDE, lambda i: main(k, i))
        there = jnp.maximum(here, hops(k, 1 - x)) * STRIDE + LAG + (STRIDE + LAG) * (lone(k) & (me == beside(k))).astype(i32)
        turn(there, lambda i: late(k, i))
        turn(there + LAG, lambda i: pass_on(k, i))
        turn(there + 2 * LAG, lambda i: settle(k, i))
        turn(levels * STRIDE + 2 * LAG, scale, k == PANEL_T - 1)
        return 0

    lax.fori_loop(0, (levels * STRIDE + size + 4 * LAG) * PANEL_T, body, 0)

    def drain(t, _):
        i, k = b0 + t // PANEL_T * c, t % PANEL_T
        sends(k, i, lambda copy: copy.wait_send())
        swaps(k, i, lambda copy: copy.wait_send())

        @pl.when(behind(k))
        def _():
            hop(k, 1 - x, i, other, beside(k)).wait_send()

        @pl.when(is_root)
        def _():
            for o in range(R // 2):
                cross(k, i, o).wait_send()

        @pl.when(direct(k))
        def _():
            relay(k, i).wait_send()

        return 0

    lax.fori_loop(0, size * PANEL_T, drain, 0)


def gather_panel(first, b0, ident, held, *inverse):
    R = lax.axis_size("row")
    per, Bn, tile, _ = held.shape
    each = (PANEL_T, Bn)
    wide = PANEL_T * tile
    return pl.pallas_call(
        lambda *refs: panel_kernel(first, b0, *refs),
        in_specs=[VMEM] * 3,
        out_specs=VMEM,
        out_shape=jax.ShapeDtypeStruct(((2 * per + 2) * Bn, tile, wide), bf16),
        scratch_shapes=[pltpu.VMEM((PANEL_T,) + held.shape, f32), pltpu.VMEM(each + (tile, tile), f32)]
        + [DMA((PANEL_T, per, Bn))] + [DMA(each)] * 4 + [DMA, DMA(each + (R // 2,)), DMA(each), DMA(each)],
        compiler_params=pltpu.CompilerParams(collective_id=ident, has_side_effects=True, vmem_limit_bytes=ROOM),
        name=f"panel_{first}_{b0}",
    )(held, *inverse)


def final_kernel(bmap, start, parent, payload, row_top, row_low, columns, out):
    step = pl.program_id(0)
    per, bcols = parent.shape[0], parent.shape[2]
    tile = parent.shape[4]
    S = payload.shape[0]
    group = bcols // S
    spot = Layout(bmap, S)
    R, C = spot.R, spot.C
    first_active = start[0] + PANEL_T

    u = lax.div(step, 2)
    first = spot.first_row(u)
    places = [step * per + p - first for p in range(per)]
    hits = [(d >= 0) & (d < per) for d in places]
    big_rows = [spot.row + (step * per + p) * R for p in range(per)]
    big_cols = [spot.col + b * C for b in range(bcols)]

    for b in range(bcols):
        s = b // group
        reached = (spot.first_col(s) == b) & (s <= u)
        for p in range(per):
            out[p, 0, b, 0] = parent[p, 0, b, 0]

            @pl.when(hits[p] & reached)
            def _():
                out[p, 0, b, 0] = parent[p, 0, b, 0] + payload[s, u * per + places[p]]

    for g in range(S):
        @pl.when((big_rows[-1] >= big_cols[g * group]) & (big_cols[g * group + group - 1] >= first_active))
        def _():
            flat = lambda v: v.reshape(-1, v.shape[-1])
            mine = (flat(row_top[...]), flat(row_low[...]))
            theirs = [flat(columns[half * bcols + g * group : half * bcols + (g + 1) * group]) for half in range(2)]
            trailing = dot3(mine, theirs, ((1,), (1,)))
            for j in range(group):
                b = g * group + j
                for p in range(per):
                    active = (big_rows[p] >= big_cols[b]) & (big_cols[b] >= first_active)
                    part = trailing[p * tile : (p + 1) * tile, j * tile : (j + 1) * tile]
                    out[p, 0, b, 0] = out[p, 0, b, 0] - jnp.where(active, part, 0.0)


def finish(bmap, start, parent, payload, factors, per):
    rows, _, bcols, _, tile, _ = parent.shape
    whole = lambda a: pl.BlockSpec(a.shape, lambda i, m, t: (0,) * a.ndim, pipeline_mode=pl.Buffered(1))
    big = pl.BlockSpec((per, 1, bcols, 1, tile, tile), lambda i, m, t: (i, 0, 0, 0, 0, 0))
    pairs = rows // per
    wide = factors.shape[-1]
    picked = lambda half: pl.BlockSpec((per, tile, wide), lambda i, m, t: (half * pairs + i, 0, 0))
    columns = pl.BlockSpec((2 * bcols, tile, wide), lambda i, m, t: (per * pairs // bcols, 0, 0), pipeline_mode=pl.Buffered(1))
    flops = 6 * rows * tile * PANEL_T * tile * bcols * tile
    return pl.pallas_call(
        final_kernel,
        grid_spec=pltpu.PrefetchScalarGridSpec(
            num_scalar_prefetch=2,
            grid=(rows // per,),
            in_specs=[big, whole(payload), picked(0), picked(1), columns],
            out_specs=big,
        ),
        out_shape=jax.ShapeDtypeStruct(parent.shape, f32),
        compiler_params=pltpu.CompilerParams(vmem_limit_bytes=ROOM),
        cost_estimate=pl.CostEstimate(flops=flops, bytes_accessed=10 * parent.size, transcendentals=0),
        name="finish",
    )(bmap, start, parent, payload, factors, factors, factors)


def per_device(contribution, parent, row_basis, pivot_basis, ranks, block_map, panel_start, inverse):
    R, C = lax.axis_size("row"), lax.axis_size("col")
    S = contribution.shape[2]
    per = C // R
    shift = [block_map[u * C] - 2 * C * u for u in range(S)]

    ident = 2
    moved, all_piv, all_bas = [], [], []
    for s in range(S):
        branches = []
        for h in range(C):
            if s < GATHERS:
                branches.append(lambda *a, h=h, s=s, ident=ident: shift_columns(h, s, per, ident, *a))
                ident += 1
            else:
                pairs = [(d, (d + h) % C) for d in range(C)]
                branches.append(lambda v, p=pairs, h=h: lax.ppermute(v, "col", p) if h else v)
        if s < GATHERS:
            came, piv, bas = lax.switch(shift[s], branches, contribution, pivot_basis, row_basis)
            all_piv.append(piv)
            all_bas.append(bas)
        else:
            came = lax.switch(shift[s], branches, contribution[per * s :, 0, s, 0])
        moved.append(came)

    partial = products(block_map, all_piv, C, per)
    weights, landed, *halves = sum_and_rows(block_map, partial, inverse, moved, per)
    parent = pltpu.with_memory_space_constraint(parent, pltpu.HBM)
    payload, held = updates(block_map, panel_start, ranks, weights, all_bas, landed, parent, C, per)

    branches = []
    pairs = parent.shape[0] // (2 * per)
    for first in range(C):
        for b0 in range(0, pairs, 2):
            b0 += (first + PANEL_T) // C
            branches.append(lambda *v, first=first, b0=b0, ident=ident: gather_panel(first, b0, ident, *v))
            ident += 1
    start = panel_start[0]
    which = lax.rem(start, C) * (pairs // 2) + jnp.minimum(lax.div(start, 2 * C), pairs // 2 - 1)
    factors = lax.switch(which, branches, held, *halves)
    return finish(block_map, panel_start, parent, payload, factors, per)


def solution(mesh):
    placed = (
        P(None, "row", None, "col", None, None),
        P(None, "row", None, "col", None, None),
        P(None, "row", None, None),
        P(None, "row", None, "col"),
        P(),
        P(),
        P(),
        P(),
    )
    return jax.shard_map(
        per_device,
        mesh=mesh,
        in_specs=placed,
        out_specs=P(None, "row", None, "col", None, None),
        check_vma=False,
    )
```

```python
import jax
import jax.numpy as jnp
from jax import lax
from jax.experimental import pallas as pl
from jax.experimental.pallas import tpu as pltpu
from jax.sharding import PartitionSpec as P

PANEL_T = 4
f32 = jnp.float32
bf16 = jnp.bfloat16
i32 = jnp.int32
MESH = pl.DeviceIdType.MESH
DMA = pltpu.SemaphoreType.DMA
SMEM = pl.BlockSpec(memory_space=pltpu.SMEM)
VMEM = pl.BlockSpec(memory_space=pltpu.VMEM)
ANY = pl.BlockSpec(memory_space=pl.ANY)
HBM = pl.BlockSpec(memory_space=pltpu.HBM)
ROOM = 32 << 20
GATHERS = 1
LAG = 2
CHUNK = 1
STRIDE = 2


def split(x):
    top = x.astype(bf16)
    return top, (x - top.astype(f32)).astype(bf16)


def dot3(a, b, dims):
    (ah, al), (bh, bl) = a, b
    one = lambda p, q: lax.dot_general(p, q, (dims, ((), ())), preferred_element_type=f32)
    return one(ah, bh) + (one(ah, bl) + one(al, bh))


def ring_place(p, n):
    return jnp.where(p < n // 2, 2 * p, 2 * (n - 1 - p) + 1)


def ring_spot(me, n):
    return jnp.where(me % 2 == 0, me // 2, n - 1 - me // 2)


def greet(targets):
    barrier = pltpu.get_barrier_semaphore()
    for target in targets:
        pl.semaphore_signal(barrier, inc=1, device_id=target, device_id_type=MESH)
    pl.semaphore_wait(barrier, len(targets))


def remote(src, dst, send, recv, to):
    return pltpu.make_async_remote_copy(src, dst, send, recv, device_id=to, device_id_type=MESH)


class Layout:
    def __init__(self, bmap, blocks):
        self.map = bmap
        self.S = blocks
        self.R, self.C = lax.axis_size("row"), lax.axis_size("col")
        self.row, self.col = lax.axis_index("row"), lax.axis_index("col")

    def shift(self, u):
        return self.map[u * self.C] - 2 * self.C * u

    def src_row(self, u, row=None):
        row = self.row if row is None else row
        return lax.rem(row + self.C * self.R - self.shift(u), self.R)

    def src_col(self, s, col=None):
        col = self.col if col is None else col
        return lax.rem(col + self.C - self.shift(s), self.C)

    def first_row(self, u, row=None):
        return lax.div(2 * self.C * u + self.shift(u) + self.src_row(u, row), self.R)

    def first_col(self, s):
        return lax.div(2 * self.C * s + self.shift(s) + self.src_col(s), self.C)


def own_column(start, col, C, bcols):
    k = lax.rem(col - start + C * bcols, C)
    return jnp.minimum(lax.div(start + k, C), bcols - 1)


def shift_kernel(h, s, per, *refs):
    R, n = lax.axis_size("row"), lax.axis_size("col")
    me, my_col = lax.axis_index("row"), lax.axis_index("col")
    gather = s < GATHERS
    if gather:
        child, piv, bas, moved, all_piv, all_bas, send, recv, own_sem, d_send, d_recv, r_send, r_recv = refs
    else:
        child, moved, send, recv = refs
    blocks = moved.shape[0] // per
    pairs = R // 2
    other = me + 1 - 2 * (me % 2)

    signals = []
    if h:
        signals.append({"col": (my_col + n - h) % n})
    if gather:
        signals += [{"row": (me + k) % R} for k in range(1, R)]
    if signals:
        greet(signals)

    def part(i):
        src = child.at[pl.ds(per * (s + i), per), 0, s, 0]
        dst = moved.at[pl.ds(per * i, per)]
        if h:
            return remote(src, dst, send.at[i], recv.at[i], {"col": (my_col + h) % n})
        return pltpu.make_async_copy(src, dst, recv.at[i])

    if gather:
        half = piv.shape[0] // GATHERS
        cuts = [(src, dst, half * s + j * half // m, j * half // m, half // m)
                for src, dst, m in ((piv, all_piv, 4), (bas, all_bas, 2)) for j in range(m)]

        def direct(o, j):
            src, dst, a, b, size = cuts[j]
            to = other if o == 0 else (me // 2 + o) % pairs * 2 + me % 2
            return remote(src.at[pl.ds(a, size), 0], dst.at[me, pl.ds(b, size)], d_send.at[o, j], d_recv.at[o, j],
                          {"row": to})

        def relay(o, j):
            _, dst, _, b, size = cuts[j]
            d = (me // 2 - o + pairs) % pairs * 2 + me % 2
            return remote(dst.at[d, pl.ds(b, size)], dst.at[d, pl.ds(b, size)], r_send.at[o, j], r_recv.at[o, j],
                          {"row": other})

        away = [(o, j) for j in range(len(cuts)) for o in range(1, pairs)]
        near = [(0, j) for j in range(len(cuts))]
        for o, j in away:
            direct(o, j).start()
    for i in range(blocks):
        part(i).start()
    if gather:
        own = [pltpu.make_async_copy(src.at[pl.ds(half * s, half), 0], dst.at[me], own_sem.at[j])
               for j, (src, dst) in enumerate(((piv, all_piv), (bas, all_bas)))]
        for copy in own:
            copy.start()
        for o, j in near:
            direct(o, j).start()
        for o, j in away:
            direct(o, j).wait_recv()
            relay(o, j).start()
        for o, j in near:
            direct(o, j).wait_recv()
        for o, j in away:
            relay(o, j).wait_recv()
            relay(o, j).wait_send()
        for o, j in away + near:
            direct(o, j).wait_send()
        for copy in own:
            copy.wait()
    for i in range(blocks):
        if h:
            part(i).wait_recv()
            part(i).wait_send()
        else:
            part(i).wait()


def shift_columns(h, s, per, ident, child, *factors):
    R = lax.axis_size("row")
    T, tile = child.shape[0], child.shape[-1]
    blocks = T // per - s
    moved = jax.ShapeDtypeStruct((per * blocks, tile, tile), f32)
    remote_ids = bool(h) or bool(factors)
    params = (
        pltpu.CompilerParams(collective_id=ident, has_side_effects=True, vmem_limit_bytes=ROOM)
        if remote_ids
        else pltpu.CompilerParams(vmem_limit_bytes=ROOM)
    )
    shapes, scratch = [moved], [DMA((blocks,)), DMA((blocks,))]
    if factors:
        shapes += [jax.ShapeDtypeStruct((R,) + (f.shape[0] // GATHERS,) + f.shape[2:], f32) for f in factors]
        scratch += [DMA((2,))] + [DMA((R // 2, 6))] * 4
    out = pl.pallas_call(
        lambda *refs: shift_kernel(h, s, per, *refs),
        in_specs=[ANY] * (1 + len(factors)),
        out_specs=[VMEM] * len(shapes),
        out_shape=shapes,
        scratch_shapes=scratch,
        compiler_params=params,
        name=f"shift_{s}_{h}",
    )(child, *factors)
    return tuple(out)


def product_kernel(per, S, bmap, *refs):
    everyone, (out, mine_top, mine_low, their_top, their_low) = refs[:GATHERS], refs[GATHERS:]
    part = everyone[0].shape[1]
    rank = everyone[0].shape[2]
    T = part * GATHERS
    R, C = lax.axis_size("row"), out.shape[0]
    spot = Layout(bmap, S)
    for t in range(T):
        top, low = split(everyone[t // part][spot.src_row(t // per), t % part])
        mine_top[t * rank : (t + 1) * rank, :] = top
        mine_low[t * rank : (t + 1) * rank, :] = low
    at = 0
    for s in range(S):
        for c in range(C):
            src = spot.src_col(s, c)
            top, low = split(everyone[s * per // part][lax.rem(src, R), s * per % part + lax.div(src, R)])
            their_top[c * rank : (c + 1) * rank, :] = top
            their_low[c * rank : (c + 1) * rank, :] = low
        first = s * per * rank
        size = T * rank - first
        mine = (mine_top[first:, :], mine_low[first:, :])
        got = dot3((their_top[...], their_low[...]), mine, ((1,), (1,)))
        out[:, :, at : at + size] = got.reshape(C, rank, size)
        at += size


def products(bmap, everyone, C, per):
    R, part, rank, width = everyone[0].shape
    T = part * GATHERS
    S = T // per
    total = sum((S - s) * per * rank for s in range(S))
    return pl.pallas_call(
        lambda *refs: product_kernel(per, S, *refs),
        in_specs=[SMEM] + [VMEM] * GATHERS,
        out_specs=VMEM,
        out_shape=jax.ShapeDtypeStruct((C, rank, total), f32),
        scratch_shapes=[pltpu.VMEM((T * rank, width), bf16)] * 2 + [pltpu.VMEM((C * rank, width), bf16)] * 2,
        compiler_params=pltpu.CompilerParams(vmem_limit_bytes=ROOM),
        name="products",
    )(bmap, *everyone)


PARTS = 4


def sum_kernel(per, bmap, partial, inverse, *refs):
    S = len(refs) - 11
    moved = refs[:S]
    out, landed, inv_top, inv_low, slots, outbox, send, recv, row_send, row_recv, own_sem = refs[S:]
    R, n = lax.axis_size("row"), lax.axis_size("col")
    my_row, me = lax.axis_index("row"), lax.axis_index("col")
    chunk = partial.shape[1] // (2 * PARTS)
    pos = ring_spot(me, n)
    right = ring_place((pos + 1) % n, n)
    left = ring_place((pos + n - 1) % n, n)
    greet([{"col": left}, {"col": right}] + [{"row": (my_row + k) % R} for k in range(1, R)])
    rows = lambda side, h: pl.ds((PARTS * side + h) * chunk, chunk)

    def part(side, k, h):
        q = (pos - 1 - k + n) % n if side == 0 else (pos + 1 + k) % n
        return partial.at[ring_place(q, n), rows(side, h)]

    def hop(side, k, h):
        src = part(side, 0, h) if k == 0 else slots.at[side, k - 1, h]
        return remote(src, slots.at[side, k, h], send.at[side, k, h], recv.at[side, k, h],
                      {"col": right if side == 0 else left})

    def cross(k):
        return remote(outbox.at[k - 1], landed.at[k], row_send.at[k - 1], row_recv.at[k - 1], {"row": (my_row + k) % R})

    for h in range(PARTS):
        for side in range(2):
            hop(side, 0, h).start()

    spot = Layout(bmap, S)
    for k in [R // 2] + [k for k in range(R) if k != R // 2]:
        block = sum(u * (lax.rem(spot.shift(u), R) == k).astype(i32) for u in range(S))
        for s in range(S):
            place = jnp.clip(block - s, 0, S - 1 - s)
            for p in range(per):
                tile = moved[s][place * per + p]
                if k == 0:
                    landed[0, s, p] = tile
                else:
                    outbox[k - 1, s, p] = tile
        if k:
            cross(k).start()

    top, rest = split(inverse[...])
    inv_top[...] = top
    inv_low[...] = rest

    every = [(k, h, side) for k in range(n - 1) for h in range(PARTS) for side in range(2)]
    for k, h, side in every:
        if k > 0:
            hop(side, k - 1, h).wait_recv()
            slots[side, k - 1, h] = slots[side, k - 1, h] + part(side, k, h)[...]
            hop(side, k, h).start()
    for h in range(PARTS):
        for side in range(2):
            hop(side, n - 2, h).wait_recv()
            out[rows(side, h), :] = slots[side, n - 2, h] + partial[me, rows(side, h), :]
    for k in range(1, R):
        cross(k).wait_recv()
        cross(k).wait_send()
    for k, h, side in every:
        hop(side, k, h).wait_send()


def sum_and_rows(bmap, partial, inverse, moved, per):
    R = lax.axis_size("row")
    n, rank, total = partial.shape
    S, tile = len(moved), moved[0].shape[-1]
    box = (S, per, tile, tile)
    return pl.pallas_call(
        lambda *refs: sum_kernel(per, *refs),
        in_specs=[SMEM] + [VMEM] * (2 + S),
        out_specs=[VMEM] * 4,
        out_shape=[jax.ShapeDtypeStruct((rank, total), f32), jax.ShapeDtypeStruct((R,) + box, f32)]
        + [jax.ShapeDtypeStruct(inverse.shape, bf16)] * 2,
        scratch_shapes=[
            pltpu.VMEM((2, n - 1, PARTS, rank // (2 * PARTS), total), f32),
            pltpu.VMEM((R - 1,) + box, f32),
            DMA((2, n - 1, PARTS)), DMA((2, n - 1, PARTS)), DMA((R - 1,)), DMA((R - 1,)), DMA,
        ],
        compiler_params=pltpu.CompilerParams(collective_id=1, has_side_effects=True, vmem_limit_bytes=ROOM),
        name="sum_and_rows",
    )(bmap, partial, inverse, *moved)


def update_kernel(per, C, bmap, start, ranks, weights, *refs):
    bases, (landed, parent, out, held, sems) = refs[:GATHERS], refs[GATHERS:]
    S, T, tile = out.shape[:3]
    R, part, rank, _ = bases[0].shape
    bcols = parent.shape[2]
    spot = Layout(bmap, S)
    b = own_column(start[0], spot.col, C, bcols)
    copies = []
    for i in range(held.shape[1]):
        for q in range(per):
            copies.append(pltpu.make_async_copy(parent.at[per * i + q, 0, b, 0], held.at[q, i], sems.at[q, i]))
            copies[-1].start()

    depth = lax.broadcasted_iota(i32, (rank, tile), 0)

    def basis(row, block, p):
        t = block * per + p
        return split(jnp.where(depth < ranks[t * R + row], bases[block * per // part][row, block * per % part + p], 0.0))

    at = 0
    for s in range(S):
        size = (S - s) * per * rank
        src = spot.src_col(s)
        j = s * C + src
        col_basis = basis(lax.rem(src, R), s, lax.div(src, R))
        half = dot3(split(weights[:, at : at + size]), col_basis, ((0,), (0,)))
        at += size
        for t in range(s * per, T):
            u, p = t // per, t % per
            i = t - s * per
            row = spot.src_row(u)
            update = dot3(basis(row, u, p), split(half[i * rank : (i + 1) * rank]), ((0,), (0,)))
            moved = landed[lax.rem(spot.shift(u), R), s, p]
            out[s, t] = jnp.where(t * R + row >= j, moved - update, 0.0)

    s_own = lax.div(b, bcols // S)
    reached = spot.first_col(s_own) == b
    for copy in copies:
        copy.wait()

    @pl.when(reached)
    def _():
        for u in range(S):
            @pl.when(s_own <= u)
            def _():
                for p in range(per):
                    a = spot.first_row(u) + p
                    q, i = lax.rem(a, per), lax.div(a, per)
                    held[q, i] = held[q, i] + out[s_own, u * per + p]


def updates(bmap, start, ranks, weights, bases, landed, parent, C, per):
    R, part, rank, tile = bases[0].shape
    T, rows = part * GATHERS, parent.shape[0]
    S = T // per
    return pl.pallas_call(
        lambda *refs: update_kernel(per, C, *refs),
        in_specs=[SMEM] * 3 + [VMEM] * (2 + GATHERS) + [HBM],
        out_specs=[VMEM, VMEM],
        out_shape=[
            jax.ShapeDtypeStruct((S, T, tile, tile), f32),
            jax.ShapeDtypeStruct((per, rows // per, tile, tile), f32),
        ],
        scratch_shapes=[DMA((per, rows // per))],
        compiler_params=pltpu.CompilerParams(vmem_limit_bytes=ROOM),
        name="updates",
    )(bmap, start, ranks, weights, *bases, landed, parent)


def panel_kernel(first, b0, held, inv_top, inv_low, result, factors, row_sem, col_sem, panel, cols, recv, up, down, across,
                 other, own_sem, cross_send, cross_recv, relay_send):
    R, n = lax.axis_size("row"), lax.axis_size("col")
    my_row, me = lax.axis_index("row"), lax.axis_index("col")
    Bn = held.shape[1]
    z, x, ends = me // 2, me % 2, n // 2 - 1
    side = me + 1 - 2 * x
    root, parity = me % R, me // R
    is_root = my_row == root
    partner = my_row + 1 - 2 * (my_row % 2)
    near = my_row // 2 == root // 2
    owner = lambda k: (first + k) % n
    c = CHUNK if (Bn - b0) % CHUNK == 0 else 1

    def lone(k):
        return ((k == 0) | (k == PANEL_T - 1)) & (first % 2 == 1)

    def beside(k):
        return owner(k) + 1 - 2 * (owner(k) % 2)

    def behind(k):
        return lone(k) & (me == jnp.where(beside(k) < 2, beside(k) + 2, beside(k) - 2))

    def hops(k, lane):
        zk, xk = owner(k) // 2, owner(k) % 2
        return jnp.maximum(z - zk, zk - z) + (lane + xk) % 2

    barrier = pltpu.get_barrier_semaphore()
    for k in range(1, R):
        pl.semaphore_signal(barrier, inc=1, device_id={"row": (my_row + k) % R}, device_id_type=MESH)
    pl.semaphore_signal(barrier, inc=1, device_id={"col": side}, device_id_type=MESH)

    @pl.when(z > 0)
    def _():
        pl.semaphore_signal(barrier, inc=1, device_id={"col": me - 2}, device_id_type=MESH)

    @pl.when(z < ends)
    def _():
        pl.semaphore_signal(barrier, inc=1, device_id={"col": me + 2}, device_id_type=MESH)

    for k in range(PANEL_T):
        @pl.when(me == owner(k))
        def _():
            pltpu.make_async_copy(held, panel.at[k], own_sem).start()

    pl.semaphore_wait(barrier, R + jnp.minimum(z, 1) + jnp.minimum(ends - z, 1))

    for k in range(PANEL_T):
        @pl.when(me == owner(k))
        def _():
            pltpu.make_async_copy(held, panel.at[k], own_sem).wait()

    def hop(k, h, i, sem, to):
        ref = panel.at[k, h, pl.ds(i, c)]
        return remote(ref, ref, sem.at[k, i], recv.at[k, h, i], {"col": to})

    def sends(k, i, act):
        zk = owner(k) // 2

        @pl.when(me == owner(k))
        def _():
            act(hop(k, 1 - x, i, other, side))

        @pl.when((z >= zk) & (z < ends))
        def _():
            act(hop(k, x, i, up, me + 2))

        @pl.when((z <= zk) & (z > 0))
        def _():
            act(hop(k, x, i, down, me - 2))

    def swaps(k, i, act):
        @pl.when(((z != owner(k) // 2) | (x == owner(k) % 2)) & ~((me == owner(k)) & lone(k)))
        def _():
            act(hop(k, x, i, across, side))

    def main(k, i):
        @pl.when(me != owner(k))
        def _():
            hop(k, x, i, up, side).wait_recv()

        sends(k, i, lambda copy: copy.start())
        swaps(k, i, lambda copy: copy.start())

    def cross(k, i, o):
        to = partner if o == 0 else (my_row // 2 + o) % (R // 2) * 2 + (my_row + k) % 2
        return remote(panel.at[k, parity, pl.ds(i, c)], cols.at[k, pl.ds(i, c)], cross_send.at[k, i, o], cross_recv.at[k, i], {"row": to})

    def late(k, i):
        @pl.when(me != owner(k))
        def _():
            hop(k, 1 - x, i, up, side).wait_recv()

        @pl.when(behind(k))
        def _():
            hop(k, 1 - x, i, other, beside(k)).start()

        @pl.when(is_root)
        def _():
            for o in range(1, R // 2):
                cross(k, i, o).start()
            cross(k, i, 0).start()

    def relay(k, i):
        return remote(cols.at[k, pl.ds(i, c)], cols.at[k, pl.ds(i, c)], relay_send.at[k, i], cross_recv.at[k, i], {"row": partner})

    def direct(k):
        return ~near & ((my_row + root + k) % 2 == 0)

    def pass_on(k, i):
        @pl.when(direct(k))
        def _():
            relay(k, i).wait_recv()
            relay(k, i).start()

    per, tile = held.shape[0], held.shape[-1]

    def settle(k, i):
        @pl.when(~direct(k) & ~is_root)
        def _():
            relay(k, i).wait_recv()

        at = pl.ds(pl.multiple_of(k * tile, tile), tile)
        for j in range(c):
            top, rest = split(jnp.where(is_root, panel[k, parity, i + j], cols[k, i + j]))
            factors[2 * per * Bn + i + j, :, at] = top
            factors[(2 * per + 1) * Bn + i + j, :, at] = rest

    def scale(start):
        lax.fori_loop(start, start + c, scale_one, 0)

    def scale_one(i, _):
        rows = [jnp.concatenate([panel[k, q, i] for k in range(PANEL_T)], axis=1) for q in range(held.shape[0])]
        scaled = dot3(split(jnp.concatenate(rows, axis=0)), (inv_top[...], inv_low[...]), ((1,), (0,)))
        top, rest = split(scaled)
        factors[pl.ds(per * i, per)] = top.reshape(per, tile, -1)
        factors[pl.ds(per * (Bn + i), per)] = rest.reshape(per, tile, -1)
        for half in range(2):
            keep(i, half).start()
        return 0

    def keep(i, half):
        at = pl.ds(per * (half * Bn + i), per)
        return pltpu.make_async_copy(factors.at[at], result.at[at], row_sem.at[half, i])

    def keep_columns(half):
        at = pl.ds((2 * per + half) * Bn + b0, Bn - b0)
        return pltpu.make_async_copy(factors.at[at], result.at[at], col_sem.at[half])

    size = (Bn - b0) // c
    levels = 0
    for k in range(PANEL_T):
        levels = jnp.maximum(levels, jnp.maximum(hops(k, x), hops(k, 1 - x)))

    def body(t, _):
        g, k = t // PANEL_T, t % PANEL_T

        def turn(at, act, also=True):
            i = g - at

            @pl.when((i >= 0) & (i < size) & also)
            def _():
                act(b0 + i * c)

        here = hops(k, x)
        turn(here * STRIDE, lambda i: main(k, i))
        there = jnp.maximum(here, hops(k, 1 - x)) * STRIDE + LAG + (STRIDE + LAG) * (lone(k) & (me == beside(k))).astype(i32)
        turn(there, lambda i: late(k, i))
        turn(there + LAG, lambda i: pass_on(k, i))
        turn(there + 2 * LAG, lambda i: settle(k, i))
        turn(levels * STRIDE + 2 * LAG, scale, k == PANEL_T - 1)
        return 0

    lax.fori_loop(0, (levels * STRIDE + size + 4 * LAG) * PANEL_T, body, 0)

    for half in range(2):
        keep_columns(half).start()

    def drain(t, _):
        i, k = b0 + t // PANEL_T * c, t % PANEL_T
        sends(k, i, lambda copy: copy.wait_send())
        swaps(k, i, lambda copy: copy.wait_send())

        @pl.when(behind(k))
        def _():
            hop(k, 1 - x, i, other, beside(k)).wait_send()

        @pl.when(is_root)
        def _():
            for o in range(R // 2):
                cross(k, i, o).wait_send()

        @pl.when(direct(k))
        def _():
            relay(k, i).wait_send()

        return 0

    lax.fori_loop(0, size * PANEL_T, drain, 0)
    for half in range(2):
        for i in range(b0, Bn):
            keep(i, half).wait()
        keep_columns(half).wait()


def gather_panel(first, b0, ident, held, *inverse):
    R = lax.axis_size("row")
    per, Bn, tile, _ = held.shape
    each = (PANEL_T, Bn)
    wide = PANEL_T * tile
    return pl.pallas_call(
        lambda *refs: panel_kernel(first, b0, *refs),
        in_specs=[VMEM] * 3,
        out_specs=HBM,
        out_shape=jax.ShapeDtypeStruct(((2 * per + 2) * Bn, tile, wide), bf16),
        scratch_shapes=[pltpu.VMEM(((2 * per + 2) * Bn, tile, wide), bf16), DMA((2, Bn)), DMA((2,))]
        + [pltpu.VMEM((PANEL_T,) + held.shape, f32), pltpu.VMEM(each + (tile, tile), f32)]
        + [DMA((PANEL_T, per, Bn))] + [DMA(each)] * 4 + [DMA, DMA(each + (R // 2,)), DMA(each), DMA(each)],
        compiler_params=pltpu.CompilerParams(collective_id=ident, has_side_effects=True, vmem_limit_bytes=ROOM),
        name=f"panel_{first}_{b0}",
    )(held, *inverse)


def final_kernel(bmap, start, parent, payload, row_top, row_low, columns, out):
    step = pl.program_id(0)
    per, bcols = parent.shape[0], parent.shape[2]
    tile = parent.shape[4]
    S = payload.shape[0]
    group = bcols // S
    spot = Layout(bmap, S)
    R, C = spot.R, spot.C
    first_active = start[0] + PANEL_T

    u = lax.div(step, 2)
    first = spot.first_row(u)
    places = [step * per + p - first for p in range(per)]
    hits = [(d >= 0) & (d < per) for d in places]
    big_rows = [spot.row + (step * per + p) * R for p in range(per)]
    big_cols = [spot.col + b * C for b in range(bcols)]

    for b in range(bcols):
        s = b // group
        reached = (spot.first_col(s) == b) & (s <= u)
        for p in range(per):
            out[p, 0, b, 0] = parent[p, 0, b, 0]

            @pl.when(hits[p] & reached)
            def _():
                out[p, 0, b, 0] = parent[p, 0, b, 0] + payload[s, u * per + places[p]]

    for g in range(S):
        @pl.when((big_rows[-1] >= big_cols[g * group]) & (big_cols[g * group + group - 1] >= first_active))
        def _():
            flat = lambda v: v.reshape(-1, v.shape[-1])
            mine = (flat(row_top[...]), flat(row_low[...]))
            theirs = [flat(columns[half * bcols + g * group : half * bcols + (g + 1) * group]) for half in range(2)]
            trailing = dot3(mine, theirs, ((1,), (1,)))
            for j in range(group):
                b = g * group + j
                for p in range(per):
                    active = (big_rows[p] >= big_cols[b]) & (big_cols[b] >= first_active)
                    part = trailing[p * tile : (p + 1) * tile, j * tile : (j + 1) * tile]
                    out[p, 0, b, 0] = out[p, 0, b, 0] - jnp.where(active, part, 0.0)


def finish(bmap, start, parent, payload, factors, per):
    rows, _, bcols, _, tile, _ = parent.shape
    whole = lambda a: pl.BlockSpec(a.shape, lambda i, m, t: (0,) * a.ndim, pipeline_mode=pl.Buffered(1))
    big = pl.BlockSpec((per, 1, bcols, 1, tile, tile), lambda i, m, t: (i, 0, 0, 0, 0, 0))
    pairs = rows // per
    wide = factors.shape[-1]
    picked = lambda half: pl.BlockSpec((per, tile, wide), lambda i, m, t: (half * pairs + i, 0, 0))
    columns = pl.BlockSpec((2 * bcols, tile, wide), lambda i, m, t: (per * pairs // bcols, 0, 0), pipeline_mode=pl.Buffered(1))
    flops = 6 * rows * tile * PANEL_T * tile * bcols * tile
    return pl.pallas_call(
        final_kernel,
        grid_spec=pltpu.PrefetchScalarGridSpec(
            num_scalar_prefetch=2,
            grid=(rows // per,),
            in_specs=[big, whole(payload), picked(0), picked(1), columns],
            out_specs=big,
        ),
        out_shape=jax.ShapeDtypeStruct(parent.shape, f32),
        compiler_params=pltpu.CompilerParams(vmem_limit_bytes=ROOM),
        cost_estimate=pl.CostEstimate(flops=flops, bytes_accessed=10 * parent.size, transcendentals=0),
        name="finish",
    )(bmap, start, parent, payload, factors, factors, factors)


def per_device(contribution, parent, row_basis, pivot_basis, ranks, block_map, panel_start, inverse):
    R, C = lax.axis_size("row"), lax.axis_size("col")
    S = contribution.shape[2]
    per = C // R
    shift = [block_map[u * C] - 2 * C * u for u in range(S)]

    ident = 2
    moved, all_piv, all_bas = [], [], []
    for s in range(S):
        branches = []
        for h in range(C):
            if s < GATHERS:
                branches.append(lambda *a, h=h, s=s, ident=ident: shift_columns(h, s, per, ident, *a))
                ident += 1
            else:
                pairs = [(d, (d + h) % C) for d in range(C)]
                branches.append(lambda v, p=pairs, h=h: lax.ppermute(v, "col", p) if h else v)
        if s < GATHERS:
            came, piv, bas = lax.switch(shift[s], branches, contribution, pivot_basis, row_basis)
            all_piv.append(piv)
            all_bas.append(bas)
        else:
            came = lax.switch(shift[s], branches, contribution[per * s :, 0, s, 0])
        moved.append(came)

    partial = products(block_map, all_piv, C, per)
    weights, landed, *halves = sum_and_rows(block_map, partial, inverse, moved, per)
    parent = pltpu.with_memory_space_constraint(parent, pltpu.HBM)
    payload, held = updates(block_map, panel_start, ranks, weights, all_bas, landed, parent, C, per)

    branches = []
    pairs = parent.shape[0] // (2 * per)
    for first in range(C):
        for b0 in range(0, pairs, 2):
            b0 += (first + PANEL_T) // C
            branches.append(lambda *v, first=first, b0=b0, ident=ident: gather_panel(first, b0, ident, *v))
            ident += 1
    start = panel_start[0]
    which = lax.rem(start, C) * (pairs // 2) + jnp.minimum(lax.div(start, 2 * C), pairs // 2 - 1)
    factors = lax.switch(which, branches, held, *halves)
    return finish(block_map, panel_start, parent, payload, factors, per)


def solution(mesh):
    placed = (
        P(None, "row", None, "col", None, None),
        P(None, "row", None, "col", None, None),
        P(None, "row", None, None),
        P(None, "row", None, "col"),
        P(),
        P(),
        P(),
        P(),
    )
    return jax.shard_map(
        per_device,
        mesh=mesh,
        in_specs=placed,
        out_specs=P(None, "row", None, "col", None, None),
        check_vma=False,
    )
```

```python
import jax
import jax.numpy as jnp
from jax import lax
from jax.experimental import pallas as pl
from jax.experimental.pallas import tpu as pltpu
from jax.sharding import PartitionSpec as P

PANEL_T = 4
f32 = jnp.float32
bf16 = jnp.bfloat16
i32 = jnp.int32
MESH = pl.DeviceIdType.MESH
DMA = pltpu.SemaphoreType.DMA
SMEM = pl.BlockSpec(memory_space=pltpu.SMEM)
VMEM = pl.BlockSpec(memory_space=pltpu.VMEM)
ANY = pl.BlockSpec(memory_space=pl.ANY)
HBM = pl.BlockSpec(memory_space=pltpu.HBM)
ROOM = 32 << 20
GATHERS = 1
LAG = 2
CHUNK = 1
STRIDE = 2


def split(x):
    top = x.astype(bf16)
    return top, (x - top.astype(f32)).astype(bf16)


def dot3(a, b, dims):
    (ah, al), (bh, bl) = a, b
    one = lambda p, q: lax.dot_general(p, q, (dims, ((), ())), preferred_element_type=f32)
    return one(ah, bh) + (one(ah, bl) + one(al, bh))


def ring_place(p, n):
    return jnp.where(p < n // 2, 2 * p, 2 * (n - 1 - p) + 1)


def ring_spot(me, n):
    return jnp.where(me % 2 == 0, me // 2, n - 1 - me // 2)


def greet(targets):
    barrier = pltpu.get_barrier_semaphore()
    for target in targets:
        pl.semaphore_signal(barrier, inc=1, device_id=target, device_id_type=MESH)
    pl.semaphore_wait(barrier, len(targets))


def remote(src, dst, send, recv, to):
    return pltpu.make_async_remote_copy(src, dst, send, recv, device_id=to, device_id_type=MESH)


class Layout:
    def __init__(self, bmap, blocks):
        self.map = bmap
        self.S = blocks
        self.R, self.C = lax.axis_size("row"), lax.axis_size("col")
        self.row, self.col = lax.axis_index("row"), lax.axis_index("col")

    def shift(self, u):
        return self.map[u * self.C] - 2 * self.C * u

    def src_row(self, u, row=None):
        row = self.row if row is None else row
        return lax.rem(row + self.C * self.R - self.shift(u), self.R)

    def src_col(self, s, col=None):
        col = self.col if col is None else col
        return lax.rem(col + self.C - self.shift(s), self.C)

    def first_row(self, u, row=None):
        return lax.div(2 * self.C * u + self.shift(u) + self.src_row(u, row), self.R)

    def first_col(self, s):
        return lax.div(2 * self.C * s + self.shift(s) + self.src_col(s), self.C)


def own_column(start, col, C, bcols):
    k = lax.rem(col - start + C * bcols, C)
    return jnp.minimum(lax.div(start + k, C), bcols - 1)


def shift_kernel(h, s, per, *refs):
    R, n = lax.axis_size("row"), lax.axis_size("col")
    me, my_col = lax.axis_index("row"), lax.axis_index("col")
    gather = s < GATHERS
    if gather:
        child, piv, bas, moved, all_piv, all_bas, send, recv, own_sem, d_send, d_recv, r_send, r_recv = refs
    else:
        child, moved, send, recv = refs
    blocks = moved.shape[0] // per
    pairs = R // 2
    other = me + 1 - 2 * (me % 2)

    signals = []
    if h:
        signals.append({"col": (my_col + n - h) % n})
    if gather:
        signals += [{"row": (me + k) % R} for k in range(1, R)]
    if signals:
        greet(signals)

    def part(i):
        src = child.at[pl.ds(per * (s + i), per), 0, s, 0]
        dst = moved.at[pl.ds(per * i, per)]
        if h:
            return remote(src, dst, send.at[i], recv.at[i], {"col": (my_col + h) % n})
        return pltpu.make_async_copy(src, dst, recv.at[i])

    if gather:
        half = piv.shape[0] // GATHERS
        cuts = [(src, dst, half * s + j * half // m, j * half // m, half // m)
                for src, dst, m in ((piv, all_piv, 4), (bas, all_bas, 2)) for j in range(m)]

        def direct(o, j):
            src, dst, a, b, size = cuts[j]
            to = other if o == 0 else (me // 2 + o) % pairs * 2 + me % 2
            return remote(src.at[pl.ds(a, size), 0], dst.at[me, pl.ds(b, size)], d_send.at[o, j], d_recv.at[o, j],
                          {"row": to})

        def relay(o, j):
            _, dst, _, b, size = cuts[j]
            d = (me // 2 - o + pairs) % pairs * 2 + me % 2
            return remote(dst.at[d, pl.ds(b, size)], dst.at[d, pl.ds(b, size)], r_send.at[o, j], r_recv.at[o, j],
                          {"row": other})

        away = [(o, j) for j in range(len(cuts)) for o in range(1, pairs)]
        near = [(0, j) for j in range(len(cuts))]
        for o, j in away:
            direct(o, j).start()
    for i in range(blocks):
        part(i).start()
    if gather:
        own = [pltpu.make_async_copy(src.at[pl.ds(half * s, half), 0], dst.at[me], own_sem.at[j])
               for j, (src, dst) in enumerate(((piv, all_piv), (bas, all_bas)))]
        for copy in own:
            copy.start()
        for o, j in near:
            direct(o, j).start()
        for o, j in away:
            direct(o, j).wait_recv()
            relay(o, j).start()
        for o, j in near:
            direct(o, j).wait_recv()
        for o, j in away:
            relay(o, j).wait_recv()
            relay(o, j).wait_send()
        for o, j in away + near:
            direct(o, j).wait_send()
        for copy in own:
            copy.wait()
    for i in range(blocks):
        if h:
            part(i).wait_recv()
            part(i).wait_send()
        else:
            part(i).wait()


def shift_columns(h, s, per, ident, child, *factors):
    R = lax.axis_size("row")
    T, tile = child.shape[0], child.shape[-1]
    blocks = T // per - s
    moved = jax.ShapeDtypeStruct((per * blocks, tile, tile), f32)
    remote_ids = bool(h) or bool(factors)
    params = (
        pltpu.CompilerParams(collective_id=ident, has_side_effects=True, vmem_limit_bytes=ROOM)
        if remote_ids
        else pltpu.CompilerParams(vmem_limit_bytes=ROOM)
    )
    shapes, scratch = [moved], [DMA((blocks,)), DMA((blocks,))]
    if factors:
        shapes += [jax.ShapeDtypeStruct((R,) + (f.shape[0] // GATHERS,) + f.shape[2:], f32) for f in factors]
        scratch += [DMA((2,))] + [DMA((R // 2, 6))] * 4
    out = pl.pallas_call(
        lambda *refs: shift_kernel(h, s, per, *refs),
        in_specs=[ANY] * (1 + len(factors)),
        out_specs=[VMEM] * len(shapes),
        out_shape=shapes,
        scratch_shapes=scratch,
        compiler_params=params,
        name=f"shift_{s}_{h}",
    )(child, *factors)
    return tuple(out)


def product_kernel(per, S, bmap, *refs):
    everyone, (out, mine_top, mine_low, their_top, their_low) = refs[:GATHERS], refs[GATHERS:]
    part = everyone[0].shape[1]
    rank = everyone[0].shape[2]
    T = part * GATHERS
    R, C = lax.axis_size("row"), out.shape[0]
    spot = Layout(bmap, S)
    for t in range(T):
        top, low = split(everyone[t // part][spot.src_row(t // per), t % part])
        mine_top[t * rank : (t + 1) * rank, :] = top
        mine_low[t * rank : (t + 1) * rank, :] = low
    at = 0
    for s in range(S):
        for c in range(C):
            src = spot.src_col(s, c)
            top, low = split(everyone[s * per // part][lax.rem(src, R), s * per % part + lax.div(src, R)])
            their_top[c * rank : (c + 1) * rank, :] = top
            their_low[c * rank : (c + 1) * rank, :] = low
        first = s * per * rank
        size = T * rank - first
        mine = (mine_top[first:, :], mine_low[first:, :])
        got = dot3((their_top[...], their_low[...]), mine, ((1,), (1,)))
        out[:, :, at : at + size] = got.reshape(C, rank, size)
        at += size


def products(bmap, everyone, C, per):
    R, part, rank, width = everyone[0].shape
    T = part * GATHERS
    S = T // per
    total = sum((S - s) * per * rank for s in range(S))
    return pl.pallas_call(
        lambda *refs: product_kernel(per, S, *refs),
        in_specs=[SMEM] + [VMEM] * GATHERS,
        out_specs=VMEM,
        out_shape=jax.ShapeDtypeStruct((C, rank, total), f32),
        scratch_shapes=[pltpu.VMEM((T * rank, width), bf16)] * 2 + [pltpu.VMEM((C * rank, width), bf16)] * 2,
        compiler_params=pltpu.CompilerParams(vmem_limit_bytes=ROOM),
        name="products",
    )(bmap, *everyone)


PARTS = 4


def sum_kernel(per, bmap, partial, inverse, *refs):
    S = len(refs) - 11
    moved = refs[:S]
    out, landed, inv_top, inv_low, slots, outbox, send, recv, row_send, row_recv, own_sem = refs[S:]
    R, n = lax.axis_size("row"), lax.axis_size("col")
    my_row, me = lax.axis_index("row"), lax.axis_index("col")
    chunk = partial.shape[1] // (2 * PARTS)
    pos = ring_spot(me, n)
    right = ring_place((pos + 1) % n, n)
    left = ring_place((pos + n - 1) % n, n)
    greet([{"col": left}, {"col": right}] + [{"row": (my_row + k) % R} for k in range(1, R)])
    rows = lambda side, h: pl.ds((PARTS * side + h) * chunk, chunk)

    def part(side, k, h):
        q = (pos - 1 - k + n) % n if side == 0 else (pos + 1 + k) % n
        return partial.at[ring_place(q, n), rows(side, h)]

    def hop(side, k, h):
        src = part(side, 0, h) if k == 0 else slots.at[side, k - 1, h]
        return remote(src, slots.at[side, k, h], send.at[side, k, h], recv.at[side, k, h],
                      {"col": right if side == 0 else left})

    def cross(k):
        return remote(outbox.at[k - 1], landed.at[k], row_send.at[k - 1], row_recv.at[k - 1], {"row": (my_row + k) % R})

    for h in range(PARTS):
        for side in range(2):
            hop(side, 0, h).start()

    spot = Layout(bmap, S)
    for k in [R // 2] + [k for k in range(R) if k != R // 2]:
        block = sum(u * (lax.rem(spot.shift(u), R) == k).astype(i32) for u in range(S))
        for s in range(S):
            place = jnp.clip(block - s, 0, S - 1 - s)
            for p in range(per):
                tile = moved[s][place * per + p]
                if k == 0:
                    landed[0, s, p] = tile
                else:
                    outbox[k - 1, s, p] = tile
        if k:
            cross(k).start()

    top, rest = split(inverse[...])
    inv_top[...] = top
    inv_low[...] = rest

    every = [(k, h, side) for k in range(n - 1) for h in range(PARTS) for side in range(2)]
    for k, h, side in every:
        if k > 0:
            hop(side, k - 1, h).wait_recv()
            slots[side, k - 1, h] = slots[side, k - 1, h] + part(side, k, h)[...]
            hop(side, k, h).start()
    for h in range(PARTS):
        for side in range(2):
            hop(side, n - 2, h).wait_recv()
            out[rows(side, h), :] = slots[side, n - 2, h] + partial[me, rows(side, h), :]
    for k in range(1, R):
        cross(k).wait_recv()
        cross(k).wait_send()
    for k, h, side in every:
        hop(side, k, h).wait_send()


def sum_and_rows(bmap, partial, inverse, moved, per):
    R = lax.axis_size("row")
    n, rank, total = partial.shape
    S, tile = len(moved), moved[0].shape[-1]
    box = (S, per, tile, tile)
    return pl.pallas_call(
        lambda *refs: sum_kernel(per, *refs),
        in_specs=[SMEM] + [VMEM] * (2 + S),
        out_specs=[VMEM] * 4,
        out_shape=[jax.ShapeDtypeStruct((rank, total), f32), jax.ShapeDtypeStruct((R,) + box, f32)]
        + [jax.ShapeDtypeStruct(inverse.shape, bf16)] * 2,
        scratch_shapes=[
            pltpu.VMEM((2, n - 1, PARTS, rank // (2 * PARTS), total), f32),
            pltpu.VMEM((R - 1,) + box, f32),
            DMA((2, n - 1, PARTS)), DMA((2, n - 1, PARTS)), DMA((R - 1,)), DMA((R - 1,)), DMA,
        ],
        compiler_params=pltpu.CompilerParams(collective_id=1, has_side_effects=True, vmem_limit_bytes=ROOM),
        name="sum_and_rows",
    )(bmap, partial, inverse, *moved)


def update_kernel(per, C, bmap, start, ranks, weights, *refs):
    bases, (landed, parent, out, held, sems) = refs[:GATHERS], refs[GATHERS:]
    S, T, tile = out.shape[:3]
    R, part, rank, _ = bases[0].shape
    bcols = parent.shape[2]
    spot = Layout(bmap, S)
    b = own_column(start[0], spot.col, C, bcols)
    copies = []
    for i in range(held.shape[1]):
        for q in range(per):
            copies.append(pltpu.make_async_copy(parent.at[per * i + q, 0, b, 0], held.at[q, i], sems.at[q, i]))
            copies[-1].start()

    depth = lax.broadcasted_iota(i32, (rank, tile), 0)

    def basis(row, block, p):
        t = block * per + p
        return split(jnp.where(depth < ranks[t * R + row], bases[block * per // part][row, block * per % part + p], 0.0))

    at = 0
    for s in range(S):
        size = (S - s) * per * rank
        src = spot.src_col(s)
        j = s * C + src
        col_basis = basis(lax.rem(src, R), s, lax.div(src, R))
        half = dot3(split(weights[:, at : at + size]), col_basis, ((0,), (0,)))
        at += size
        for t in range(s * per, T):
            u, p = t // per, t % per
            i = t - s * per
            row = spot.src_row(u)
            update = dot3(basis(row, u, p), split(half[i * rank : (i + 1) * rank]), ((0,), (0,)))
            moved = landed[lax.rem(spot.shift(u), R), s, p]
            out[s, t] = jnp.where(t * R + row >= j, moved - update, 0.0)

    s_own = lax.div(b, bcols // S)
    reached = spot.first_col(s_own) == b
    for copy in copies:
        copy.wait()

    @pl.when(reached)
    def _():
        for u in range(S):
            @pl.when(s_own <= u)
            def _():
                for p in range(per):
                    a = spot.first_row(u) + p
                    q, i = lax.rem(a, per), lax.div(a, per)
                    held[q, i] = held[q, i] + out[s_own, u * per + p]


def updates(bmap, start, ranks, weights, bases, landed, parent, C, per):
    R, part, rank, tile = bases[0].shape
    T, rows = part * GATHERS, parent.shape[0]
    S = T // per
    return pl.pallas_call(
        lambda *refs: update_kernel(per, C, *refs),
        in_specs=[SMEM] * 3 + [VMEM] * (2 + GATHERS) + [HBM],
        out_specs=[VMEM, VMEM],
        out_shape=[
            jax.ShapeDtypeStruct((S, T, tile, tile), f32),
            jax.ShapeDtypeStruct((per, rows // per, tile, tile), f32),
        ],
        scratch_shapes=[DMA((per, rows // per))],
        compiler_params=pltpu.CompilerParams(vmem_limit_bytes=ROOM),
        name="updates",
    )(bmap, start, ranks, weights, *bases, landed, parent)


def panel_kernel(first, b0, held, inv_top, inv_low, factors, panel, cols, recv, up, down, across,
                 other, own_sem, cross_send, cross_recv, relay_send):
    R, n = lax.axis_size("row"), lax.axis_size("col")
    my_row, me = lax.axis_index("row"), lax.axis_index("col")
    Bn = held.shape[1]
    z, x, ends = me // 2, me % 2, n // 2 - 1
    side = me + 1 - 2 * x
    root, parity = me % R, me // R
    is_root = my_row == root
    partner = my_row + 1 - 2 * (my_row % 2)
    near = my_row // 2 == root // 2
    owner = lambda k: (first + k) % n
    c = CHUNK if (Bn - b0) % CHUNK == 0 else 1

    def lone(k):
        return ((k == 0) | (k == PANEL_T - 1)) & (first % 2 == 1)

    def beside(k):
        return owner(k) + 1 - 2 * (owner(k) % 2)

    def behind(k):
        return lone(k) & (me == jnp.where(beside(k) < 2, beside(k) + 2, beside(k) - 2))

    def hops(k, lane):
        zk, xk = owner(k) // 2, owner(k) % 2
        return jnp.maximum(z - zk, zk - z) + (lane + xk) % 2

    barrier = pltpu.get_barrier_semaphore()
    for k in range(1, R):
        pl.semaphore_signal(barrier, inc=1, device_id={"row": (my_row + k) % R}, device_id_type=MESH)
    pl.semaphore_signal(barrier, inc=1, device_id={"col": side}, device_id_type=MESH)

    @pl.when(z > 0)
    def _():
        pl.semaphore_signal(barrier, inc=1, device_id={"col": me - 2}, device_id_type=MESH)

    @pl.when(z < ends)
    def _():
        pl.semaphore_signal(barrier, inc=1, device_id={"col": me + 2}, device_id_type=MESH)

    for k in range(PANEL_T):
        @pl.when(me == owner(k))
        def _():
            pltpu.make_async_copy(held, panel.at[k], own_sem).start()

    pl.semaphore_wait(barrier, R + jnp.minimum(z, 1) + jnp.minimum(ends - z, 1))

    for k in range(PANEL_T):
        @pl.when(me == owner(k))
        def _():
            pltpu.make_async_copy(held, panel.at[k], own_sem).wait()

    def hop(k, h, i, sem, to):
        ref = panel.at[k, h, pl.ds(i, c)]
        return remote(ref, ref, sem.at[k, i], recv.at[k, h, i], {"col": to})

    def sends(k, i, act):
        zk = owner(k) // 2

        @pl.when(me == owner(k))
        def _():
            act(hop(k, 1 - x, i, other, side))

        @pl.when((z >= zk) & (z < ends))
        def _():
            act(hop(k, x, i, up, me + 2))

        @pl.when((z <= zk) & (z > 0))
        def _():
            act(hop(k, x, i, down, me - 2))

    def swaps(k, i, act):
        @pl.when(((z != owner(k) // 2) | (x == owner(k) % 2)) & ~((me == owner(k)) & lone(k)))
        def _():
            act(hop(k, x, i, across, side))

    def main(k, i):
        @pl.when(me != owner(k))
        def _():
            hop(k, x, i, up, side).wait_recv()

        sends(k, i, lambda copy: copy.start())
        swaps(k, i, lambda copy: copy.start())

    def cross(k, i, o):
        to = partner if o == 0 else (my_row // 2 + o) % (R // 2) * 2 + (my_row + k) % 2
        return remote(panel.at[k, parity, pl.ds(i, c)], cols.at[k, pl.ds(i, c)], cross_send.at[k, i, o], cross_recv.at[k, i], {"row": to})

    def late(k, i):
        @pl.when(me != owner(k))
        def _():
            hop(k, 1 - x, i, up, side).wait_recv()

        @pl.when(behind(k))
        def _():
            hop(k, 1 - x, i, other, beside(k)).start()

        @pl.when(is_root)
        def _():
            for o in range(1, R // 2):
                cross(k, i, o).start()
            cross(k, i, 0).start()

    def relay(k, i):
        return remote(cols.at[k, pl.ds(i, c)], cols.at[k, pl.ds(i, c)], relay_send.at[k, i], cross_recv.at[k, i], {"row": partner})

    def direct(k):
        return ~near & ((my_row + root + k) % 2 == 0)

    def pass_on(k, i):
        @pl.when(direct(k))
        def _():
            relay(k, i).wait_recv()
            relay(k, i).start()

    per, tile = held.shape[0], held.shape[-1]

    def settle(k, i):
        @pl.when(~direct(k) & ~is_root)
        def _():
            relay(k, i).wait_recv()

        at = pl.ds(pl.multiple_of(k * tile, tile), tile)
        for j in range(c):
            top, rest = split(jnp.where(is_root, panel[k, parity, i + j], cols[k, i + j]))
            factors[2 * per * Bn + i + j, :, at] = top
            factors[(2 * per + 1) * Bn + i + j, :, at] = rest

    def scale(start):
        lax.fori_loop(start, start + c, scale_one, 0)

    def scale_one(i, _):
        rows = [jnp.concatenate([panel[k, q, i] for k in range(PANEL_T)], axis=1) for q in range(held.shape[0])]
        scaled = dot3(split(jnp.concatenate(rows, axis=0)), (inv_top[...], inv_low[...]), ((1,), (0,)))
        top, rest = split(scaled)
        factors[pl.ds(per * i, per)] = top.reshape(per, tile, -1)
        factors[pl.ds(per * (Bn + i), per)] = rest.reshape(per, tile, -1)
        return 0

    size = (Bn - b0) // c
    levels = 0
    for k in range(PANEL_T):
        levels = jnp.maximum(levels, jnp.maximum(hops(k, x), hops(k, 1 - x)))

    def body(t, _):
        g, k = t // PANEL_T, t % PANEL_T

        def turn(at, act, also=True):
            i = g - at

            @pl.when((i >= 0) & (i < size) & also)
            def _():
                act(b0 + i * c)

        here = hops(k, x)
        turn(here * STRIDE, lambda i: main(k, i))
        there = jnp.maximum(here, hops(k, 1 - x)) * STRIDE + LAG + (STRIDE + LAG) * (lone(k) & (me == beside(k))).astype(i32)
        turn(there, lambda i: late(k, i))
        turn(there + LAG, lambda i: pass_on(k, i))
        turn(there + 2 * LAG, lambda i: settle(k, i))
        turn(levels * STRIDE + 2 * LAG, scale, k == PANEL_T - 1)
        return 0

    lax.fori_loop(0, (levels * STRIDE + size + 4 * LAG) * PANEL_T, body, 0)

    def drain(t, _):
        i, k = b0 + t // PANEL_T * c, t % PANEL_T
        sends(k, i, lambda copy: copy.wait_send())
        swaps(k, i, lambda copy: copy.wait_send())

        @pl.when(behind(k))
        def _():
            hop(k, 1 - x, i, other, beside(k)).wait_send()

        @pl.when(is_root)
        def _():
            for o in range(R // 2):
                cross(k, i, o).wait_send()

        @pl.when(direct(k))
        def _():
            relay(k, i).wait_send()

        return 0

    lax.fori_loop(0, size * PANEL_T, drain, 0)


def gather_panel(first, b0, ident, held, *inverse):
    R = lax.axis_size("row")
    per, Bn, tile, _ = held.shape
    each = (PANEL_T, Bn)
    wide = PANEL_T * tile
    return pl.pallas_call(
        lambda *refs: panel_kernel(first, b0, *refs),
        in_specs=[VMEM] * 3,
        out_specs=VMEM,
        out_shape=jax.ShapeDtypeStruct(((2 * per + 2) * Bn, tile, wide), bf16),
        scratch_shapes=[pltpu.VMEM((PANEL_T,) + held.shape, f32), pltpu.VMEM(each + (tile, tile), f32)]
        + [DMA((PANEL_T, per, Bn))] + [DMA(each)] * 4 + [DMA, DMA(each + (R // 2,)), DMA(each), DMA(each)],
        compiler_params=pltpu.CompilerParams(collective_id=ident, has_side_effects=True, vmem_limit_bytes=ROOM),
        name=f"panel_{first}_{b0}",
    )(held, *inverse)


def final_kernel(bmap, start, parent, payload, row_top, row_low, columns, out):
    step = pl.program_id(0)
    per, bcols = parent.shape[0], parent.shape[2]
    tile = parent.shape[4]
    S = payload.shape[0]
    group = bcols // S
    spot = Layout(bmap, S)
    R, C = spot.R, spot.C
    first_active = start[0] + PANEL_T

    u = lax.div(step, 2)
    first = spot.first_row(u)
    places = [step * per + p - first for p in range(per)]
    hits = [(d >= 0) & (d < per) for d in places]
    big_rows = [spot.row + (step * per + p) * R for p in range(per)]
    big_cols = [spot.col + b * C for b in range(bcols)]

    for b in range(bcols):
        s = b // group
        reached = (spot.first_col(s) == b) & (s <= u)
        for p in range(per):
            out[p, 0, b, 0] = parent[p, 0, b, 0]

            @pl.when(hits[p] & reached)
            def _():
                out[p, 0, b, 0] = parent[p, 0, b, 0] + payload[s, u * per + places[p]]

    for g in range(S):
        @pl.when((big_rows[-1] >= big_cols[g * group]) & (big_cols[g * group + group - 1] >= first_active))
        def _():
            flat = lambda v: v.reshape(-1, v.shape[-1])
            mine = (flat(row_top[...]), flat(row_low[...]))
            theirs = [flat(columns[half * bcols + g * group : half * bcols + (g + 1) * group]) for half in range(2)]
            trailing = dot3(mine, theirs, ((1,), (1,)))
            for j in range(group):
                b = g * group + j
                for p in range(per):
                    active = (big_rows[p] >= big_cols[b]) & (big_cols[b] >= first_active)
                    part = trailing[p * tile : (p + 1) * tile, j * tile : (j + 1) * tile]
                    out[p, 0, b, 0] = out[p, 0, b, 0] - jnp.where(active, part, 0.0)


def finish(bmap, start, parent, payload, factors, per):
    rows, _, bcols, _, tile, _ = parent.shape
    whole = lambda a: pl.BlockSpec(a.shape, lambda i, m, t: (0,) * a.ndim, pipeline_mode=pl.Buffered(1))
    big = pl.BlockSpec((per, 1, bcols, 1, tile, tile), lambda i, m, t: (i, 0, 0, 0, 0, 0))
    pairs = rows // per
    wide = factors.shape[-1]
    picked = lambda half: pl.BlockSpec((per, tile, wide), lambda i, m, t: (half * pairs + i, 0, 0))
    columns = pl.BlockSpec((2 * bcols, tile, wide), lambda i, m, t: (per * pairs // bcols, 0, 0), pipeline_mode=pl.Buffered(1))
    flops = 6 * rows * tile * PANEL_T * tile * bcols * tile
    return pl.pallas_call(
        final_kernel,
        grid_spec=pltpu.PrefetchScalarGridSpec(
            num_scalar_prefetch=2,
            grid=(rows // per,),
            in_specs=[big, whole(payload), picked(0), picked(1), columns],
            out_specs=big,
        ),
        out_shape=jax.ShapeDtypeStruct(parent.shape, f32),
        compiler_params=pltpu.CompilerParams(vmem_limit_bytes=ROOM),
        cost_estimate=pl.CostEstimate(flops=flops, bytes_accessed=10 * parent.size, transcendentals=0),
        name="finish",
    )(bmap, start, parent, payload, factors, factors, factors)


def per_device(contribution, parent, row_basis, pivot_basis, ranks, block_map, panel_start, inverse):
    R, C = lax.axis_size("row"), lax.axis_size("col")
    S = contribution.shape[2]
    per = C // R
    shift = [block_map[u * C] - 2 * C * u for u in range(S)]

    ident = 2
    moved, all_piv, all_bas = [], [], []
    for s in range(S):
        branches = []
        for h in range(C):
            if s < GATHERS:
                branches.append(lambda *a, h=h, s=s, ident=ident: shift_columns(h, s, per, ident, *a))
                ident += 1
            else:
                pairs = [(d, (d + h) % C) for d in range(C)]
                branches.append(lambda v, p=pairs, h=h: lax.ppermute(v, "col", p) if h else v)
        if s < GATHERS:
            came, piv, bas = lax.switch(shift[s], branches, contribution, pivot_basis, row_basis)
            all_piv.append(piv)
            all_bas.append(bas)
            contribution, came = lax.optimization_barrier((contribution, came))
        else:
            came = lax.switch(shift[s], branches, contribution[per * s :, 0, s, 0])
        moved.append(came)

    partial = products(block_map, all_piv, C, per)
    weights, landed, *halves = sum_and_rows(block_map, partial, inverse, moved, per)
    parent = pltpu.with_memory_space_constraint(parent, pltpu.HBM)
    payload, held = updates(block_map, panel_start, ranks, weights, all_bas, landed, parent, C, per)

    branches = []
    pairs = parent.shape[0] // (2 * per)
    for first in range(C):
        for b0 in range(0, pairs, 2):
            b0 += (first + PANEL_T) // C
            branches.append(lambda *v, first=first, b0=b0, ident=ident: gather_panel(first, b0, ident, *v))
            ident += 1
    start = panel_start[0]
    which = lax.rem(start, C) * (pairs // 2) + jnp.minimum(lax.div(start, 2 * C), pairs // 2 - 1)
    factors = lax.switch(which, branches, held, *halves)
    return finish(block_map, panel_start, parent, payload, factors, per)


def solution(mesh):
    placed = (
        P(None, "row", None, "col", None, None),
        P(None, "row", None, "col", None, None),
        P(None, "row", None, None),
        P(None, "row", None, "col"),
        P(),
        P(),
        P(),
        P(),
    )
    return jax.shard_map(
        per_device,
        mesh=mesh,
        in_specs=placed,
        out_specs=P(None, "row", None, "col", None, None),
        check_vma=False,
    )
```
